32 devices in a mesh: grp: 4 (over y, core), shard: 8 (over z, x).
Axes of the slice: x: 2, y: 2, z: 4, core: 2. Of those that a mesh axis runs over, the one named last changes fastest.
Arguments:
- tokens: bfloat16 [16384, 768], P(('grp', 'shard')), may hold values from -6 to 6
- cotangent: bfloat16 [16384, 768], P(('grp', 'shard')), may hold values from -6 to 6
- seq_lengths: int32 [4, 8], replicated, may hold values from 1 to 1024, 3840 in all within a row
- seq_order: int32 [4, 8], replicated, may hold values from 0 to 7, each once within a row
- w_project: bfloat16 [2, 768, 2304], P(None, 'shard'), may hold values from -0.21875 to 0.21875
- w_mixer: bfloat16 [2, 768, 768], P(None, 'shard'), may hold values from -4 to 4
- w_expand: bfloat16 [2, 768, 3072], P(None, 'shard'), may hold values from -0.21875 to 0.21875
- w_reduce: bfloat16 [2, 3072, 768], P(None, 'shard'), may hold values from -0.109375 to 0.109375
- biases: bfloat16 [2, 7680], P(None, 'shard'), may hold values from -1.1953125 to 1.1953125
- norm_gains: bfloat16 [2, 1536], P(None, 'shard'), may hold values from 0.5 to 1.5
Outputs:
- activations: bfloat16 [16384, 768], P(('grp', 'shard'))
- input_grad: float32 [16384, 768], P(('grp', 'shard'))
- project_grad: float32 [2, 768, 2304], P(None, 'shard')
- mixer_grad: float32 [2, 768, 768], P(None, 'shard')
- expand_grad: float32 [2, 768, 3072], P(None, 'shard')
- reduce_grad: float32 [2, 3072, 768], P(None, 'shard')
- bias_grad: float32 [2, 7680], P(None, 'shard')
- gain_grad: float32 [2, 1536], P(None, 'shard')
The draws below stay inside these ranges and needn't reach their ends.
Inputs may be any that keep to these rules, and one draw needn't show every extreme that they name: `seq_lengths`: each row holds the lengths of one group's 8 sequences; they sum to 3840, and the largest of each row is exactly 1024. `seq_order`: each row is a permutation.
All inputs are finite; a program needn't handle non-finite values.
Results may differ from the reference program's by a relative error of at most 0.019.
Values may be sent and summed in bfloat16 or wider, within the bound.
No kernel may reach another device: no remote copies, remote signals or barrier semaphores. Data moves between devices by JAX's collectives and lax.ppermute only.
A program may use at most 320 MiB of HBM per device.

```python
import math
import jax
import jax.numpy as jnp
import numpy as np
from jax import lax

D = 768
HEADS = 12
HEAD_DIM = 64
FF = 3072
LAYERS = 2
TOK_DEV = 512
GROUP_TOK = 4096
TOKENS = 16384
MOST = 1024
SEQS = 8
BIAS_LEN = 7680
N_GRP = 4


def level_of(stream_key, extent, split, low, largest):
    level, own = 1.0, jax.random.fold_in(stream_key, 6)
    for dim, blocks in split:
        heights = jnp.exp(jax.random.uniform(jax.random.fold_in(own, dim), (blocks,), jnp.float32, low / len(split), largest / len(split)))
        level = level * jnp.repeat(heights, extent[dim] // blocks).reshape([-1 if axis == dim else 1 for axis in range(len(extent))])
    return level


def split_up(amount, total, reach, skew):
    portions = [(1 << 20) // math.isqrt(standing ** skew) + 1 for standing in range(2, amount + 1)]
    rest, holding = total - reach - (amount - 1), [1] * (amount - 1)
    while rest > 0:
        free = [i for i in range(amount - 1) if holding[i] < reach]
        whole, remaining = sum([portions[i] for i in free]), rest
        for i in free:
            extra = min(reach - holding[i], max(1, remaining * portions[i] // whole), rest)
            holding[i] = holding[i] + extra
            rest = rest - extra
    return np.array([reach] + holding)


def uneven(own_key, number_of, total, limit, lean):
    if number_of == 2:
        one = jax.random.randint(own_key, (), max(1, total - limit), min(limit, total - 1) + 1)
        return jnp.stack([one, total - one])
    lengths = jnp.asarray(split_up(number_of, total, limit, lean), jnp.int32)
    couples = (number_of - 1) // 2
    donor, taker = lengths[1:1 + 2 * couples:2], lengths[2:2 + 2 * couples:2]
    slack = jnp.minimum(donor - 1, limit - taker)
    shifted = jax.random.randint(jax.random.fold_in(own_key, 1), (couples,), 0, 1 << 20) % (slack + 1)
    lengths = lengths.at[1:1 + 2 * couples:2].set(donor - shifted).at[2:2 + 2 * couples:2].set(taker + shifted)
    return lengths[jax.random.permutation(jax.random.fold_in(own_key, 2), number_of)]


def gaussian(stream_key, dims, scale, reach, cuts=(), kind=jnp.bfloat16):
    drawn = scale * jax.random.normal(stream_key, dims, jnp.float32)
    if cuts:
        drawn = drawn * level_of(stream_key, dims, cuts, -0.22, 0.18)
    return jnp.clip(drawn, -reach, reach).astype(kind)


def setup_inputs(seed: int = 0) -> dict:
    seeds = jax.random.split(jax.random.key(seed), 11)
    tokens = gaussian(seeds[0], (TOKENS, D), 1.0, 6.0, ((0, 32),))
    cotangent = gaussian(seeds[1], (TOKENS, D), 1.0, 6.0, ((0, 32),))
    seq_lengths = jax.vmap(lambda own: uneven(own, SEQS, GROUP_TOK - TOK_DEV // 2, MOST, 1))(jax.random.split(seeds[2], N_GRP)).reshape((N_GRP, SEQS)).astype(jnp.int32)
    seq_order = jax.vmap(lambda own: jax.random.permutation(own, SEQS))(jax.random.split(seeds[3], N_GRP)).reshape((N_GRP, SEQS)).astype(jnp.int32)
    w_project = gaussian(seeds[4], (LAYERS, D, 3 * D), D ** -0.5, 0.21875, ((1, 8),))
    w_mixer = gaussian(seeds[5], (LAYERS, D, D), 2 ** -0.5, 4.0, ((1, 8),))
    w_expand = gaussian(seeds[6], (LAYERS, D, FF), D ** -0.5, 0.21875, ((1, 8),))
    w_reduce = gaussian(seeds[7], (LAYERS, FF, D), FF ** -0.5, 0.109375, ((1, 8),))
    biases = gaussian(seeds[8], (LAYERS, BIAS_LEN), 0.3, 1.1953125, ((1, 8),))
    norm_gains = jnp.clip(1.0 + 0.1 * jax.random.normal(seeds[9], (LAYERS, 2 * D), jnp.float32), 0.5, 1.5).astype(jnp.bfloat16)
    return dict(tokens=tokens, cotangent=cotangent, seq_lengths=seq_lengths, seq_order=seq_order, w_project=w_project, w_mixer=w_mixer, w_expand=w_expand, w_reduce=w_reduce, biases=biases, norm_gains=norm_gains)


@jax.custom_vjp
def low(v):
    return lax.optimization_barrier(v.astype(jnp.bfloat16)).astype(jnp.float32)

@jax.custom_vjp
def low_back(v):
    return v

def low_keep(v):
    return (low(v), None)

def low_pass(kept, grad):
    return (grad,)

def back_keep(v):
    return (v, None)

def back_low(kept, grad):
    return (low(grad),)
low.defvjp(low_keep, low_pass)
low_back.defvjp(back_keep, back_low)
EPSILON = 1e-12
NEGATIVE = -1e+30
HIGHEST = lax.Precision.HIGHEST

def layer_norm(values, gain, shift):
    middle = lax.optimization_barrier(jnp.mean(values, axis=-1, keepdims=True))
    centered = values - middle
    spread = lax.optimization_barrier(jnp.mean(centered * centered, axis=-1, keepdims=True))
    return centered * lax.rsqrt(spread + EPSILON) * gain + shift

def segment_ids(lengths_row, order_row):
    places = jnp.arange(SEQS, dtype=jnp.int32)
    picked = order_row[:, None] == places[None, :]
    placed = lax.optimization_barrier(jnp.sum(jnp.where(picked, lengths_row[None, :], 0), axis=1, dtype=jnp.int32))
    seq_ends = jnp.cumsum(placed, dtype=jnp.int32)
    slot_index = jnp.arange(GROUP_TOK, dtype=jnp.int32)
    return lax.optimization_barrier(jnp.sum((seq_ends[None, :] <= slot_index[:, None]).astype(jnp.int32), axis=1, dtype=jnp.int32))

def attend_group(queries, key_rows, value_rows, segment):
    block_rows = math.gcd(GROUP_TOK, 512)
    score_scale = HEAD_DIM ** (-0.5)

    def one_block(block_index):
        begin_at = (block_index * block_rows).astype(jnp.int32)
        query_block = lax.dynamic_slice_in_dim(queries, begin_at, block_rows, 0)
        query_seg = lax.dynamic_slice_in_dim(segment, begin_at, block_rows, 0)
        raw_scores = jnp.einsum('qhd,khd->hqk', query_block, key_rows, precision=HIGHEST)
        scores = low_back(score_scale * raw_scores)
        allowed = (query_seg[:, None] == segment[None, :])[None]
        probs = jax.nn.softmax(jnp.where(allowed, scores, NEGATIVE), axis=-1)
        return jnp.einsum('hqk,khd->qhd', low(probs), value_rows, precision=HIGHEST)
    mixed = lax.map(jax.checkpoint(one_block), jnp.arange(GROUP_TOK // block_rows, dtype=jnp.int32))
    return mixed.reshape(GROUP_TOK, HEADS, HEAD_DIM)

def one_layer(hidden_state, project, mixing, expand, shrink, bias_vec, gain_vec, segments):
    bias_q = bias_vec[0:D]
    bias_v = bias_vec[D:2 * D]
    bias_mix = bias_vec[2 * D:3 * D]
    shift_one = bias_vec[3 * D:4 * D]
    bias_in = bias_vec[4 * D:4 * D + FF]
    bias_out = bias_vec[4 * D + FF:5 * D + FF]
    shift_two = bias_vec[5 * D + FF:6 * D + FF]
    state_low = low(hidden_state)
    project_bias = jnp.concatenate([bias_q, jnp.zeros_like(bias_q), bias_v])
    projected = low(low_back(jnp.dot(state_low, project, precision=HIGHEST) + project_bias))
    shaped = projected.reshape(N_GRP, GROUP_TOK, 3, HEADS, HEAD_DIM)

    def per_group(group_parts):
        return attend_group(group_parts[0], group_parts[1], group_parts[2], group_parts[3])
    mixed = lax.map(per_group, (shaped[:, :, 0], shaped[:, :, 1], shaped[:, :, 2], segments))
    mixed = low(low_back(mixed.reshape(TOKENS, D)))
    branch = low_back(jnp.dot(mixed, mixing, precision=HIGHEST) + bias_mix)
    normed_one = layer_norm(hidden_state + branch, gain_vec[:D], shift_one)
    normed_low = low(normed_one)
    before = low_back(jnp.dot(normed_low, expand, precision=HIGHEST) + bias_in)
    active = low(jax.nn.gelu(before, approximate=False))
    feed_out = low_back(jnp.dot(active, shrink, precision=HIGHEST) + bias_out)
    return layer_norm(normed_one + feed_out, gain_vec[D:], shift_two)

def reference(tokens, cotangent, seq_lengths, seq_order, w_project, w_mixer, w_expand, w_reduce, biases, norm_gains):
    segments = jax.vmap(segment_ids)(seq_lengths, seq_order)
    valid_rows = (segments < SEQS).reshape(TOKENS, 1).astype(jnp.float32)

    def forward(inputs, project, mixing, expand, shrink, bias_all, gain_all):
        hidden_state = inputs
        for layer_index in range(LAYERS):
            hidden_state = one_layer(hidden_state, project[layer_index], mixing[layer_index], expand[layer_index], shrink[layer_index], bias_all[layer_index], gain_all[layer_index], segments)
        return hidden_state
    outputs, pullback = jax.vjp(forward, tokens.astype(jnp.float32), w_project.astype(jnp.float32), w_mixer.astype(jnp.float32), w_expand.astype(jnp.float32), w_reduce.astype(jnp.float32), biases.astype(jnp.float32), norm_gains.astype(jnp.float32))
    grads = pullback(cotangent.astype(jnp.float32) * valid_rows)
    return ((outputs * valid_rows).astype(jnp.bfloat16), grads[0], grads[1], grads[2], grads[3], grads[4], grads[5], grads[6])
```

```python
import jax
import jax.numpy as jnp
from jax import lax
from jax.experimental import pallas as pl
from jax.experimental.pallas import tpu as pltpu
from jax.sharding import PartitionSpec as P

HEADS = 12
LAYERS = 2
SEQ_MAX = 2048


EPSILON = 1e-12
NEGATIVE = -1e30


def passed_along(shard, axis, by):
    size = lax.axis_size(axis)
    pairs = [(i, i + by) for i in range(size) if 0 <= i + by < size]
    return lax.ppermute(shard, axis, pairs)


def layer_norm(values, gain, shift):
    middle = jnp.mean(values, axis=-1, keepdims=True)
    centered = values - middle
    spread = jnp.mean(centered * centered, axis=-1, keepdims=True)
    return centered * lax.rsqrt(spread + EPSILON) * gain + shift


def gelu_exact(values):
    return jax.nn.gelu(values, approximate=False)


def keep_same(carried):
    return carried


def group_ends(seq_lengths, seq_order, group_index):
    lengths_row = lax.dynamic_index_in_dim(seq_lengths, group_index, 0, keepdims=False)
    order_row = lax.dynamic_index_in_dim(seq_order, group_index, 0, keepdims=False)
    places = jnp.arange(lengths_row.shape[0], dtype=jnp.int32)
    picked = order_row[:, None] == places[None, :]
    placed = jnp.sum(jnp.where(picked, lengths_row[None, :], 0), axis=1, dtype=jnp.int32)
    return jnp.cumsum(placed, dtype=jnp.int32)


def slot_segments(slot_index, seq_ends):
    flattened = slot_index.reshape(-1)
    counted = jnp.sum(
        (seq_ends[None, :] <= flattened[:, None]).astype(jnp.int32), axis=1, dtype=jnp.int32
    )
    return counted.reshape(slot_index.shape)


def unpack_weights(weights, width, hidden_units):
    bias_vec = weights[4].astype(jnp.float32)
    gain_vec = weights[5].astype(jnp.float32)
    piece_lens = [width, width, width, width, hidden_units, width, width]
    bias_list = []
    begin_at = 0
    for piece_len in piece_lens:
        bias_list.append(bias_vec[begin_at : begin_at + piece_len])
        begin_at = begin_at + piece_len
    return (
        weights[0],
        weights[1],
        weights[2],
        weights[3],
        bias_list,
        gain_vec[:width],
        gain_vec[width:],
    )


def block_probs(queries, keys_block, seg_block, own_segment, log_total, score_scale):
    raw_scores = jnp.einsum("qhd,khd->hqk", queries, keys_block, preferred_element_type=jnp.float32)
    allowed = (own_segment[:, None] == seg_block[None, :])[None]
    return jnp.where(allowed, jnp.exp(raw_scores * score_scale - log_total[:, :, None]), 0.0)


def gather_window(key_rows, value_rows, reach_blocks):
    key_list = []
    value_list = []
    for step_offset in range(-reach_blocks, reach_blocks + 1):
        if step_offset == 0:
            moved = (key_rows, value_rows)
        else:
            moved = passed_along((key_rows, value_rows), "shard", -step_offset)
        key_list.append(moved[0])
        value_list.append(moved[1])
    return (jnp.stack(key_list), jnp.stack(value_list))


def return_parts(key_parts, value_parts, reach_blocks):
    key_total = key_parts[reach_blocks]
    value_total = value_parts[reach_blocks]
    for step_offset in range(-reach_blocks, reach_blocks + 1):
        if step_offset != 0:
            arrived = (
                passed_along(
                    key_parts[step_offset + reach_blocks].astype(jnp.bfloat16), "shard", step_offset
                ).astype(jnp.float32),
                passed_along(
                    value_parts[step_offset + reach_blocks].astype(jnp.bfloat16),
                    "shard",
                    step_offset,
                ).astype(jnp.float32),
            )
            key_total = key_total + arrived[0]
            value_total = value_total + arrived[1]
    return (key_total, value_total)


def attend_forward(
    queries, window_keys, window_values, window_segment, live_block, own_segment, score_scale
):
    row_count, head_count, head_dim = queries.shape

    def stats_step(carry, items):
        keys_block, seg_block, alive = items

        def stats_compute(state_pair):
            running_top, running_sum = state_pair
            allowed = (own_segment[:, None] == seg_block[None, :])[None]
            raw_scores = jnp.einsum(
                "qhd,khd->hqk", queries, keys_block, preferred_element_type=jnp.float32
            )
            scores = jnp.where(allowed, raw_scores * score_scale, NEGATIVE)
            new_top = jnp.maximum(running_top, jnp.max(scores, axis=-1))
            weighted = jnp.where(allowed, jnp.exp(scores - new_top[:, :, None]), 0.0)
            return (
                new_top,
                running_sum * jnp.exp(running_top - new_top) + jnp.sum(weighted, axis=-1),
            )

        return (lax.cond(alive, stats_compute, keep_same, carry), None)

    begin_stats = (
        jnp.full((head_count, row_count), NEGATIVE, jnp.float32),
        jnp.zeros((head_count, row_count), jnp.float32),
    )
    (running_top, running_sum), unused = lax.scan(
        stats_step, begin_stats, (window_keys, window_segment, live_block)
    )
    log_total = running_top + jnp.log(running_sum)

    def mix_step(carry, items):
        keys_block, values_block, seg_block, alive = items

        def mix_compute(state_pair):
            mixed, extra = state_pair
            probs = block_probs(queries, keys_block, seg_block, own_segment, log_total, score_scale)
            probs_low = probs.astype(jnp.bfloat16)
            rest_low = (probs - lax.optimization_barrier(probs_low).astype(jnp.float32)).astype(
                jnp.bfloat16
            )
            mixed = mixed + jnp.einsum(
                "hqk,khd->qhd", probs_low, values_block, preferred_element_type=jnp.float32
            )
            extra = extra + jnp.einsum(
                "hqk,khd->qhd", rest_low, values_block, preferred_element_type=jnp.float32
            )
            return (mixed, extra)

        return (lax.cond(alive, mix_compute, keep_same, carry), None)

    zeros_mix = jnp.zeros((row_count, head_count, head_dim), jnp.float32)
    (mixed, extra), unused = lax.scan(
        mix_step, (zeros_mix, zeros_mix), (window_keys, window_values, window_segment, live_block)
    )
    return (log_total, mixed, mixed + extra)


def attend_backward(
    queries,
    window_keys,
    window_values,
    window_segment,
    live_block,
    own_segment,
    log_total,
    delta,
    grad_low,
    score_scale,
):

    def grad_step(query_grad, items):
        keys_block, values_block, seg_block, alive = items

        def grad_compute(carried):
            probs = block_probs(queries, keys_block, seg_block, own_segment, log_total, score_scale)
            prob_grad = jnp.einsum(
                "qhd,khd->hqk", grad_low, values_block, preferred_element_type=jnp.float32
            )
            score_low = (probs * (prob_grad - delta[:, :, None])).astype(jnp.bfloat16)
            carried = carried + jnp.einsum(
                "hqk,khd->qhd", score_low, keys_block, preferred_element_type=jnp.float32
            )
            probs_low = probs.astype(jnp.bfloat16)
            value_part = jnp.einsum(
                "hqk,qhd->khd", probs_low, grad_low, preferred_element_type=jnp.float32
            )
            key_part = jnp.einsum(
                "hqk,qhd->khd", score_low, queries, preferred_element_type=jnp.float32
            )
            return (carried, (key_part, value_part))

        def skipped(carried):
            nothing = jnp.zeros(keys_block.shape, jnp.float32)
            return (carried, (nothing, nothing))

        return lax.cond(alive, grad_compute, skipped, query_grad)

    zero_grad = jnp.zeros(queries.shape, jnp.float32)
    query_grad, key_value = lax.scan(
        grad_step, zero_grad, (window_keys, window_values, window_segment, live_block)
    )
    return (query_grad, key_value)


def on_device(
    tokens,
    cotangent,
    seq_lengths,
    seq_order,
    w_project,
    w_mixer,
    w_expand,
    w_reduce,
    biases,
    norm_gains,
):
    row_count, width = tokens.shape
    shard_count = lax.axis_size("shard")
    shard_index = lax.axis_index("shard")
    group_index = lax.axis_index("grp")
    head_dim = width // HEADS
    hidden_units = w_expand.shape[2]
    score_scale = head_dim ** (-0.5)
    longest = min(SEQ_MAX, row_count * shard_count // 4)
    reach_blocks = longest // row_count
    seq_count = seq_lengths.shape[1]
    seq_ends = group_ends(seq_lengths, seq_order, group_index)
    neighbour = shard_index + jnp.arange(-reach_blocks, reach_blocks + 1, dtype=jnp.int32)
    slot_index = neighbour[:, None] * row_count + jnp.arange(row_count, dtype=jnp.int32)[None, :]
    window_segment = slot_segments(slot_index, seq_ends)
    own_segment = window_segment[reach_blocks]
    inside = (neighbour >= 0) & (neighbour < shard_count)
    live_block = (
        inside
        & (window_segment[:, 0] <= own_segment[row_count - 1])
        & (window_segment[:, row_count - 1] >= own_segment[0])
    )
    valid_rows = (own_segment < seq_count).astype(jnp.float32)[:, None]
    hidden_state = tokens.astype(jnp.float32)
    state_low = tokens
    kept_list = []
    for layer_index in range(LAYERS):
        weights = (
            lax.all_gather(w_project[layer_index], "shard", axis=0, tiled=True),
            lax.all_gather(w_mixer[layer_index], "shard", axis=0, tiled=True),
            lax.all_gather(w_expand[layer_index], "shard", axis=0, tiled=True),
            lax.all_gather(w_reduce[layer_index], "shard", axis=0, tiled=True),
            lax.all_gather(biases[layer_index], "shard", axis=0, tiled=True),
            lax.all_gather(norm_gains[layer_index], "shard", axis=0, tiled=True),
        )
        project, mixing, expand, shrink, bias_list, gain_one, gain_two = unpack_weights(
            weights, width, hidden_units
        )
        bias_q, bias_v, bias_mix, shift_one, bias_in, bias_out, shift_two = bias_list
        projected = jnp.dot(state_low, project, preferred_element_type=jnp.float32)
        projected = projected + jnp.concatenate([bias_q, jnp.zeros_like(bias_q), bias_v])
        projected_low = projected.astype(jnp.bfloat16)
        queries = projected_low[:, :width].reshape(row_count, HEADS, head_dim)
        key_rows = projected_low[:, width : 2 * width].reshape(row_count, HEADS, head_dim)
        value_rows = projected_low[:, 2 * width :].reshape(row_count, HEADS, head_dim)
        window_keys, window_values = gather_window(key_rows, value_rows, reach_blocks)
        log_total, mixed, full_mix = attend_forward(
            queries,
            window_keys,
            window_values,
            window_segment,
            live_block,
            own_segment,
            score_scale,
        )
        mixed_low = mixed.reshape(row_count, width).astype(jnp.bfloat16)
        branch = jnp.dot(mixed_low, mixing, preferred_element_type=jnp.float32) + bias_mix
        summed_one = hidden_state + branch
        normed_one = layer_norm(summed_one, gain_one, shift_one)
        normed_low = normed_one.astype(jnp.bfloat16)
        before = jnp.dot(normed_low, expand, preferred_element_type=jnp.float32) + bias_in
        active_low = gelu_exact(before).astype(jnp.bfloat16)
        feed_out = jnp.dot(active_low, shrink, preferred_element_type=jnp.float32) + bias_out
        summed_two = normed_one + feed_out
        hidden_state = layer_norm(summed_two, gain_two, shift_two)
        kept_list.append(
            (
                state_low,
                queries,
                key_rows,
                value_rows,
                window_keys,
                window_values,
                log_total,
                full_mix,
                mixed_low,
                summed_one,
                normed_low,
                before,
                active_low,
                summed_two,
                weights,
            )
        )
        state_low = hidden_state.astype(jnp.bfloat16)
    activations = (hidden_state * valid_rows).astype(jnp.bfloat16)
    state_grad = cotangent.astype(jnp.float32) * valid_rows
    results = [None] * LAYERS
    for layer_index in reversed(range(LAYERS)):
        (
            layer_low,
            queries,
            key_rows,
            value_rows,
            window_keys,
            window_values,
            log_total,
            full_mix,
            mixed_low,
            summed_one,
            normed_low,
            before,
            active_low,
            summed_two,
            kept_weights,
        ) = kept_list[layer_index]
        weights = (
            lax.all_gather(w_project[layer_index], "shard", axis=0, tiled=True),
            lax.all_gather(w_mixer[layer_index], "shard", axis=0, tiled=True),
            lax.all_gather(w_expand[layer_index], "shard", axis=0, tiled=True),
            lax.all_gather(w_reduce[layer_index], "shard", axis=0, tiled=True),
            lax.all_gather(biases[layer_index], "shard", axis=0, tiled=True),
            lax.all_gather(norm_gains[layer_index], "shard", axis=0, tiled=True),
        )
        project, mixing, expand, shrink, bias_list, gain_one, gain_two = unpack_weights(
            weights, width, hidden_units
        )
        bias_q, bias_v, bias_mix, shift_one, bias_in, bias_out, shift_two = bias_list
        unused_two, norm_pull = jax.vjp(layer_norm, summed_two, gain_two, shift_two)
        sum_two_grad, gain_two_grad, shift_two_grad = norm_pull(state_grad)
        feed_low = sum_two_grad.astype(jnp.bfloat16)
        shrink_grad = jnp.einsum(
            "tf,td->fd", active_low, feed_low, preferred_element_type=jnp.float32
        )
        bias_out_grad = jnp.sum(feed_low, axis=0, dtype=jnp.float32)
        active_grad = jnp.einsum("td,fd->tf", feed_low, shrink, preferred_element_type=jnp.float32)
        unused_gelu, gelu_pull = jax.vjp(gelu_exact, before)
        before_low = gelu_pull(active_grad)[0].astype(jnp.bfloat16)
        expand_grad = jnp.einsum(
            "td,tf->df", normed_low, before_low, preferred_element_type=jnp.float32
        )
        bias_in_grad = jnp.sum(before_low, axis=0, dtype=jnp.float32)
        normed_grad = sum_two_grad + jnp.einsum(
            "tf,df->td", before_low, expand, preferred_element_type=jnp.float32
        )
        unused_one, first_pull = jax.vjp(layer_norm, summed_one, gain_one, shift_one)
        sum_one_grad, gain_one_grad, shift_one_grad = first_pull(normed_grad)
        branch_low = sum_one_grad.astype(jnp.bfloat16)
        mixing_grad = jnp.einsum(
            "td,te->de", mixed_low, branch_low, preferred_element_type=jnp.float32
        )
        bias_mix_grad = jnp.sum(branch_low, axis=0, dtype=jnp.float32)
        mixed_grad = jnp.einsum("te,de->td", branch_low, mixing, preferred_element_type=jnp.float32)
        mixed_grad_low = mixed_grad.astype(jnp.bfloat16).reshape(row_count, HEADS, head_dim)
        delta = jnp.sum(mixed_grad_low.astype(jnp.float32) * full_mix, axis=-1).T
        query_grad, key_value = attend_backward(
            queries,
            window_keys,
            window_values,
            window_segment,
            live_block,
            own_segment,
            log_total,
            delta,
            mixed_grad_low,
            score_scale,
        )
        key_total, value_total = return_parts(key_value[0], key_value[1], reach_blocks)
        projected_grad = jnp.concatenate(
            [
                (query_grad * score_scale).reshape(row_count, width),
                (key_total * score_scale).reshape(row_count, width),
                value_total.reshape(row_count, width),
            ],
            axis=1,
        )
        projected_low = projected_grad.astype(jnp.bfloat16)
        project_grad = jnp.einsum(
            "td,te->de", layer_low, projected_low, preferred_element_type=jnp.float32
        )
        bias_q_grad = jnp.sum(projected_low[:, :width], axis=0, dtype=jnp.float32)
        bias_v_grad = jnp.sum(projected_low[:, 2 * width :], axis=0, dtype=jnp.float32)
        state_grad = sum_one_grad + jnp.einsum(
            "te,de->td", projected_low, project, preferred_element_type=jnp.float32
        )
        bias_all = jnp.concatenate(
            [
                bias_q_grad,
                bias_v_grad,
                bias_mix_grad,
                shift_one_grad,
                bias_in_grad,
                bias_out_grad,
                shift_two_grad,
            ]
        )
        gain_all = jnp.concatenate([gain_one_grad, gain_two_grad])
        shares = (
            lax.psum_scatter(
                project_grad.astype(jnp.bfloat16), "shard", scatter_dimension=0, tiled=True
            ).astype(jnp.float32),
            lax.psum_scatter(
                mixing_grad.astype(jnp.bfloat16), "shard", scatter_dimension=0, tiled=True
            ).astype(jnp.float32),
            lax.psum_scatter(
                expand_grad.astype(jnp.bfloat16), "shard", scatter_dimension=0, tiled=True
            ).astype(jnp.float32),
            lax.psum_scatter(
                shrink_grad.astype(jnp.bfloat16), "shard", scatter_dimension=0, tiled=True
            ).astype(jnp.float32),
            lax.psum_scatter(
                bias_all.astype(jnp.bfloat16), "shard", scatter_dimension=0, tiled=True
            ).astype(jnp.float32),
            lax.psum_scatter(
                gain_all.astype(jnp.bfloat16), "shard", scatter_dimension=0, tiled=True
            ).astype(jnp.float32),
        )
        shares = (
            lax.psum(shares[0].astype(jnp.bfloat16), "grp").astype(jnp.float32),
            lax.psum(shares[1].astype(jnp.bfloat16), "grp").astype(jnp.float32),
            lax.psum(shares[2].astype(jnp.bfloat16), "grp").astype(jnp.float32),
            lax.psum(shares[3].astype(jnp.bfloat16), "grp").astype(jnp.float32),
            lax.psum(shares[4].astype(jnp.bfloat16), "grp").astype(jnp.float32),
            lax.psum(shares[5].astype(jnp.bfloat16), "grp").astype(jnp.float32),
        )
        results[layer_index] = shares
    stacked = [jnp.stack([layer_share[member] for layer_share in results]) for member in range(6)]
    return (
        activations,
        state_grad,
        stacked[0],
        stacked[1],
        stacked[2],
        stacked[3],
        stacked[4],
        stacked[5],
    )


Q_TILE = 256
K_TILE = 256


def fold_lanes(values, combine):
    total = values[:, :128]
    for begin_at in range(128, values.shape[1], 128):
        total = combine(total, values[:, begin_at : begin_at + 128])
    return total


def halves_of(block):
    lane = lax.broadcasted_iota(jnp.int32, block.shape, 1)
    nothing = jnp.zeros_like(block)
    return (jnp.where(lane < 64, block, nothing), jnp.where(lane < 64, nothing, block))


def flash_forward_kernel(
    bounds, q_ref, k_ref, v_ref, low_ref, high_ref, mix_ref, lse_ref, score_scr
):
    rows = q_ref.shape[0]
    for tile in range(rows // Q_TILE):
        span = pl.ds(tile * Q_TILE, Q_TILE)
        heads = halves_of(q_ref[span, :] * jnp.bfloat16(0.125))
        low = low_ref[span, 0:1]
        high = high_ref[span, 0:1]
        first = bounds[2 * tile]
        last = bounds[2 * tile + 1]

        def score_step(key_tile, tops):
            begin_at = pl.multiple_of(key_tile * K_TILE, K_TILE)
            keys = k_ref[pl.ds(begin_at, K_TILE), :]
            place = lax.broadcasted_iota(jnp.int32, (Q_TILE, K_TILE), 1) + begin_at
            allowed = (place >= low) & (place < high)
            out = []
            for head in range(2):
                scores = lax.dot_general(
                    heads[head], keys, (((1,), (1,)), ((), ())), preferred_element_type=jnp.float32
                )
                scores = jnp.where(allowed, scores, NEGATIVE)
                score_scr[head, key_tile] = scores
                out.append(jnp.maximum(tops[head], fold_lanes(scores, jnp.maximum)))
            return tuple(out)

        floor = jnp.full((Q_TILE, 128), NEGATIVE, jnp.float32)
        tops = lax.fori_loop(first, last, score_step, (floor, floor))
        tops = [jnp.max(top, axis=1, keepdims=True) for top in tops]

        def mix_step(key_tile, carry):
            begin_at = pl.multiple_of(key_tile * K_TILE, K_TILE)
            values = v_ref[pl.ds(begin_at, K_TILE), :]
            out = []
            for head in range(2):
                total, mixed = carry[head]
                weight = jnp.exp(score_scr[head, key_tile] - tops[head])
                total = total + fold_lanes(weight, jnp.add)
                mixed = mixed + jnp.dot(
                    weight.astype(jnp.bfloat16), values, preferred_element_type=jnp.float32
                )
                out.append((total, mixed))
            return tuple(out)

        zero = jnp.zeros((Q_TILE, 128), jnp.float32)
        carry = lax.fori_loop(first, last, mix_step, ((zero, zero), (zero, zero)))
        totals = [jnp.sum(total, axis=1, keepdims=True) for total, mixed in carry]
        lane = lax.broadcasted_iota(jnp.int32, (Q_TILE, 128), 1)
        mix_ref[span, :] = jnp.where(
            lane < 64, carry[0][1] / totals[0], carry[1][1] / totals[1]
        ).astype(jnp.bfloat16)
        lse_ref[span, :] = jnp.where(
            lane < 64, tops[0] + jnp.log(totals[0]), tops[1] + jnp.log(totals[1])
        )


def flash_backward_kernel(
    bounds,
    q_ref,
    k_ref,
    v_ref,
    grad_ref,
    lse_ref,
    low_ref,
    high_ref,
    q_grad_ref,
    k_grad_ref,
    v_grad_ref,
    prob_scr,
    slope_scr,
    k_acc,
    v_acc,
):
    rows = q_ref.shape[0]
    k_acc[...] = jnp.zeros_like(k_acc)
    v_acc[...] = jnp.zeros_like(v_acc)
    for tile in range(rows // Q_TILE):
        span = pl.ds(tile * Q_TILE, Q_TILE)
        heads = halves_of(q_ref[span, :] * jnp.bfloat16(0.125))
        grads = halves_of(grad_ref[span, :])
        lse_turned = lse_ref[span, :].T
        lse = (lse_turned[0:1, :], lse_turned[64:65, :])
        low = low_ref[0:1, span]
        high = high_ref[0:1, span]
        first = bounds[2 * tile]
        last = bounds[2 * tile + 1]

        def prob_step(key_tile, deltas):
            begin_at = pl.multiple_of(key_tile * K_TILE, K_TILE)
            keys = k_ref[pl.ds(begin_at, K_TILE), :]
            values = v_ref[pl.ds(begin_at, K_TILE), :]
            place = lax.broadcasted_iota(jnp.int32, (K_TILE, Q_TILE), 0) + begin_at
            allowed = (place >= low) & (place < high)
            out = []
            for head in range(2):
                scores = lax.dot_general(
                    keys, heads[head], (((1,), (1,)), ((), ())), preferred_element_type=jnp.float32
                )
                probs = jnp.where(allowed, jnp.exp(scores - lse[head]), 0.0)
                slope = lax.dot_general(
                    values, grads[head], (((1,), (1,)), ((), ())), preferred_element_type=jnp.float32
                )
                prob_scr[head, key_tile] = probs
                slope_scr[head, key_tile] = slope
                out.append(
                    deltas[head]
                    + jnp.sum((probs * slope).reshape(K_TILE // 8, 8, Q_TILE), axis=0)
                )
            return tuple(out)

        zero = jnp.zeros((8, Q_TILE), jnp.float32)
        deltas = lax.fori_loop(first, last, prob_step, (zero, zero))
        deltas = [jnp.sum(delta, axis=0, keepdims=True) for delta in deltas]

        def grad_step(key_tile, carry):
            begin_at = pl.multiple_of(key_tile * K_TILE, K_TILE)
            key_span = pl.ds(begin_at, K_TILE)
            keys = k_ref[key_span, :]
            out = []
            k_part = None
            for head in range(2):
                probs = prob_scr[head, key_tile]
                low_slope = (probs * (slope_scr[head, key_tile] - deltas[head])).astype(jnp.bfloat16)
                v_term = jnp.dot(
                    probs.astype(jnp.bfloat16), grads[head], preferred_element_type=jnp.float32
                )
                k_term = jnp.dot(low_slope, heads[head], preferred_element_type=jnp.float32)
                out.append(
                    carry[head]
                    + lax.dot_general(
                        low_slope, keys, (((0,), (0,)), ((), ())), preferred_element_type=jnp.float32
                    )
                )
                v_part = v_term if head == 0 else v_part + v_term
                k_part = k_term if head == 0 else k_part + k_term
            k_acc[key_span, :] += k_part
            v_acc[key_span, :] += v_part
            return tuple(out)

        zero = jnp.zeros((Q_TILE, 128), jnp.float32)
        q_parts = lax.fori_loop(first, last, grad_step, (zero, zero))
        lane = lax.broadcasted_iota(jnp.int32, (Q_TILE, 128), 1)
        q_grad_ref[span, :] = (jnp.where(lane < 64, q_parts[0], q_parts[1]) * 0.125).astype(
            jnp.bfloat16
        )
    k_grad_ref[...] = k_acc[...].astype(jnp.bfloat16)
    v_grad_ref[...] = v_acc[...].astype(jnp.bfloat16)


def flash_forward(bounds, queries, key_value, low, high):
    rows, width = queries.shape
    window = key_value.shape[0]
    pairs = width // 128
    tiles = window // K_TILE
    return pl.pallas_call(
        flash_forward_kernel,
        out_shape=(
            jax.ShapeDtypeStruct((rows, width), jnp.bfloat16),
            jax.ShapeDtypeStruct((rows, width), jnp.float32),
        ),
        grid_spec=pltpu.PrefetchScalarGridSpec(
            num_scalar_prefetch=1,
            grid=(pairs,),
            in_specs=[
                pl.BlockSpec((rows, 128), lambda i, b: (0, i)),
                pl.BlockSpec((window, 128), lambda i, b: (0, i)),
                pl.BlockSpec((window, 128), lambda i, b: (0, i + pairs)),
                pl.BlockSpec((rows, 128), lambda i, b: (0, 0)),
                pl.BlockSpec((rows, 128), lambda i, b: (0, 0)),
            ],
            out_specs=[
                pl.BlockSpec((rows, 128), lambda i, b: (0, i)),
                pl.BlockSpec((rows, 128), lambda i, b: (0, i)),
            ],
            scratch_shapes=[pltpu.VMEM((2, tiles, Q_TILE, K_TILE), jnp.float32)],
        ),
        compiler_params=pltpu.CompilerParams(vmem_limit_bytes=40 * 2**20),
        cost_estimate=pl.CostEstimate(
            flops=4 * rows * width * 1536, bytes_accessed=8 * 2**20, transcendentals=rows * 12 * 1536
        ),
        name="flash_forward",
    )(bounds, queries, key_value, key_value, low, high)


def flash_backward(bounds, queries, key_value, grad_low, lse, low, high):
    rows, width = queries.shape
    window = key_value.shape[0]
    pairs = width // 128
    tiles = window // K_TILE
    own = pl.BlockSpec((rows, 128), lambda i, b: (0, i))
    wide = pl.BlockSpec((window, 128), lambda i, b: (0, i))
    line = pl.BlockSpec((8, rows), lambda i, b: (0, 0))
    return pl.pallas_call(
        flash_backward_kernel,
        out_shape=(
            jax.ShapeDtypeStruct((rows, width), jnp.bfloat16),
            jax.ShapeDtypeStruct((window, width), jnp.bfloat16),
            jax.ShapeDtypeStruct((window, width), jnp.bfloat16),
        ),
        grid_spec=pltpu.PrefetchScalarGridSpec(
            num_scalar_prefetch=1,
            grid=(pairs,),
            in_specs=[
                own,
                wide,
                pl.BlockSpec((window, 128), lambda i, b: (0, i + pairs)),
                own,
                own,
                line,
                line,
            ],
            out_specs=[own, wide, wide],
            scratch_shapes=[
                pltpu.VMEM((2, tiles, K_TILE, Q_TILE), jnp.float32),
                pltpu.VMEM((2, tiles, K_TILE, Q_TILE), jnp.float32),
                pltpu.VMEM((window, 128), jnp.float32),
                pltpu.VMEM((window, 128), jnp.float32),
            ],
        ),
        compiler_params=pltpu.CompilerParams(vmem_limit_bytes=48 * 2**20),
        cost_estimate=pl.CostEstimate(
            flops=10 * rows * width * 1536,
            bytes_accessed=16 * 2**20,
            transcendentals=rows * 12 * 1536,
        ),
        name="flash_backward",
    )(bounds, queries, key_value, key_value, grad_low, lse, low, high)


GRP_Y, GRP_CORE, SHARD_Z, SHARD_X = 2, 2, 4, 2
BOTH = ("grp", "shard")


def device_pairs(place):
    pairs = []
    for y in range(GRP_Y):
        for core in range(GRP_CORE):
            for z in range(SHARD_Z):
                for x in range(SHARD_X):
                    target = place(y, core, z, x)
                    if target is not None:
                        ty, tcore, tz, tx = target
                        pairs.append(
                            (
                                (y * GRP_CORE + core) * SHARD_Z * SHARD_X + z * SHARD_X + x,
                                (ty * GRP_CORE + tcore) * SHARD_Z * SHARD_X + tz * SHARD_X + tx,
                            )
                        )
    return pairs


def send(values, place):
    return lax.ppermute(values, BOTH, device_pairs(place))


def turn_rows(values):
    return send(values, lambda y, core, z, x: (y, x, z, core))


def swap_core(values):
    return send(values, lambda y, core, z, x: (y, 1 - core, z, x))


def send_up(values):
    return send(values, lambda y, core, z, x: (y, core, z + 1, x) if z + 1 < SHARD_Z else None)


def send_down(values):
    return send(values, lambda y, core, z, x: (y, core, z - 1, x) if z > 0 else None)


def window_of(rows, core):
    from_below = send_up(rows)
    from_above = send_down(rows)
    other = swap_core(jnp.concatenate([rows, jnp.where(core == 1, from_below, from_above)]))
    count = rows.shape[0]
    other_own, other_far = other[:count], other[count:]
    return jnp.concatenate(
        [
            from_below,
            jnp.where(core == 0, other_far, other_own),
            rows,
            jnp.where(core == 0, other_own, other_far),
            from_above,
        ]
    )


def window_back(parts, core, count):
    low = parts.astype(jnp.bfloat16)
    block = [low[i * count : (i + 1) * count] for i in range(5)]
    near = jnp.where(core == 0, block[3], block[1])
    far = jnp.where(core == 0, block[1], block[3])
    other = swap_core(jnp.concatenate([near, far])).astype(jnp.float32)
    other_near, other_far = other[:count], other[count:]
    below = block[0].astype(jnp.float32)
    above = block[4].astype(jnp.float32)
    below = jnp.where(core == 1, below + other_far, below).astype(jnp.bfloat16)
    above = jnp.where(core == 0, above + other_far, above).astype(jnp.bfloat16)
    from_above = send_down(below).astype(jnp.float32)
    from_below = send_up(above).astype(jnp.float32)
    return parts[2 * count : 3 * count] + other_near + from_above + from_below


def quarter_rows(shard, quarter):
    count = shard.shape[0] // 4
    return lax.dynamic_slice_in_dim(shard, quarter * count, count, 0)


def split_columns(rows, width):
    return jnp.concatenate(
        [rows[:, i : i + width] for i in range(0, rows.shape[1], width)], axis=0
    )


def gather_layer(project, mixer, expand, reduce, small, quarter, width):
    local = jnp.concatenate(
        [
            split_columns(quarter_rows(project, quarter), width),
            quarter_rows(mixer, quarter),
            split_columns(quarter_rows(expand, quarter), width),
            quarter_rows(reduce, quarter),
            small,
        ]
    )
    return lax.all_gather(local, BOTH, axis=0, tiled=False)


def joined(pieces, begin_at, count, columns):
    width = pieces.shape[2]
    part = pieces[:, begin_at : begin_at + count * columns]
    part = part.reshape(4, 8, columns, count, width).transpose(1, 0, 3, 2, 4)
    return part.reshape(32 * count, columns * width)


def parted(grad, columns):
    rows = grad.shape[0] // 32
    width = grad.shape[1] // columns
    part = grad.reshape(8, 4, rows, columns, width).transpose(1, 0, 3, 2, 4)
    return part.reshape(32, columns * rows, width)


def on_device_turned(
    tokens,
    cotangent,
    seq_lengths,
    seq_order,
    w_project,
    w_mixer,
    w_expand,
    w_reduce,
    biases,
    norm_gains,
):
    row_count, width = tokens.shape
    shard_index = lax.axis_index("shard")
    quarter = lax.axis_index("grp")
    z, x = shard_index // SHARD_X, shard_index % SHARD_X
    y, core = quarter // GRP_CORE, quarter % GRP_CORE
    hidden_units = w_expand.shape[2]
    group_slots = row_count * 8
    seq_count = seq_lengths.shape[1]
    seq_ends = group_ends(seq_lengths, seq_order, y * GRP_CORE + x)
    block_index = z * GRP_CORE + core
    slot_index = block_index * row_count + jnp.arange(row_count, dtype=jnp.int32)
    before_slot = seq_ends[None, :] <= slot_index[:, None]
    own_segment = jnp.sum(before_slot.astype(jnp.int32), axis=1, dtype=jnp.int32)
    starts = jnp.max(jnp.where(before_slot, seq_ends[None, :], 0), axis=1)
    stops = jnp.min(jnp.where(before_slot, group_slots, seq_ends[None, :]), axis=1)
    window_begin = (block_index - 2) * row_count
    low = starts - window_begin
    high = stops - window_begin
    low_wide = jnp.broadcast_to(low[:, None], (row_count, 128))
    high_wide = jnp.broadcast_to(high[:, None], (row_count, 128))
    low_line = jnp.broadcast_to(low[None, :], (8, row_count))
    high_line = jnp.broadcast_to(high[None, :], (8, row_count))
    bounds = jnp.stack(
        [low[0::Q_TILE] // K_TILE, (high[Q_TILE - 1 :: Q_TILE] + K_TILE - 1) // K_TILE], axis=1
    ).reshape(-1)
    valid_rows = (own_segment < seq_count).astype(jnp.float32)[:, None]

    small = jnp.concatenate(
        [jnp.concatenate([biases[i], norm_gains[i]]) for i in range(LAYERS)]
    ).reshape(-1, width)
    small = jnp.concatenate([small, jnp.zeros((8 - small.shape[0], width), small.dtype)])
    gathered = [
        gather_layer(
            w_project[i], w_mixer[i], w_expand[i], w_reduce[i], small, quarter, width
        )
        for i in range(LAYERS)
    ]
    state_low = turn_rows(tokens)
    state_grad = turn_rows(cotangent)
    share = w_project.shape[1] // 4
    deep = w_reduce.shape[1] // 4
    counts = [share * 3, share, share * (hidden_units // width), deep]
    small_at = sum(counts)
    small_all = gathered[0][:8, small_at : small_at + 3].reshape(8, LAYERS, -1)
    bias_count = biases.shape[1]
    weights = []
    for layer_index in range(LAYERS):
        pieces = gathered[layer_index]
        begin_at = 0
        whole = []
        for count, columns in zip(counts, (3, 1, hidden_units // width, 1)):
            whole.append(joined(pieces, begin_at, count // columns, columns))
            begin_at += count
        bias_vec = small_all[:, layer_index, :bias_count].reshape(-1)
        gain_vec = small_all[:, layer_index, bias_count:].reshape(-1)
        weights.append(unpack_weights(whole + [bias_vec, gain_vec], width, hidden_units))

    hidden_state = state_low.astype(jnp.float32)
    kept_list = []
    for layer_index in range(LAYERS):
        project, mixing, expand, shrink, bias_list, gain_one, gain_two = weights[layer_index]
        bias_q, bias_v, bias_mix, shift_one, bias_in, bias_out, shift_two = bias_list
        state_window = window_of(state_low, core)
        queries = (
            jnp.dot(state_low, project[:, :width], preferred_element_type=jnp.float32) + bias_q
        ).astype(jnp.bfloat16)
        key_value = (
            jnp.dot(state_window, project[:, width:], preferred_element_type=jnp.float32)
            + jnp.concatenate([jnp.zeros_like(bias_v), bias_v])
        ).astype(jnp.bfloat16)
        mixed_low, lse = flash_forward(bounds, queries, key_value, low_wide, high_wide)
        branch = jnp.dot(mixed_low, mixing, preferred_element_type=jnp.float32) + bias_mix
        summed_one = hidden_state + branch
        normed_one = layer_norm(summed_one, gain_one, shift_one)
        normed_low = normed_one.astype(jnp.bfloat16)
        before = jnp.dot(normed_low, expand, preferred_element_type=jnp.float32) + bias_in
        active_low = gelu_exact(before).astype(jnp.bfloat16)
        feed_out = jnp.dot(active_low, shrink, preferred_element_type=jnp.float32) + bias_out
        summed_two = normed_one + feed_out
        hidden_state = layer_norm(summed_two, gain_two, shift_two)
        kept_list.append(
            (
                state_low,
                state_window,
                queries,
                key_value,
                lse,
                mixed_low,
                summed_one,
                normed_low,
                before,
                active_low,
                summed_two,
            )
        )
        state_low = hidden_state.astype(jnp.bfloat16)
    activations = turn_rows((hidden_state * valid_rows).astype(jnp.bfloat16))
    state_grad = state_grad.astype(jnp.float32) * valid_rows
    results = [None] * LAYERS
    for layer_index in reversed(range(LAYERS)):
        (
            layer_low,
            state_window,
            queries,
            key_value,
            lse,
            mixed_low,
            summed_one,
            normed_low,
            before,
            active_low,
            summed_two,
        ) = kept_list[layer_index]
        project, mixing, expand, shrink, bias_list, gain_one, gain_two = weights[layer_index]
        bias_q, bias_v, bias_mix, shift_one, bias_in, bias_out, shift_two = bias_list
        unused_two, norm_pull = jax.vjp(layer_norm, summed_two, gain_two, shift_two)
        sum_two_grad, gain_two_grad, shift_two_grad = norm_pull(state_grad)
        feed_low = sum_two_grad.astype(jnp.bfloat16)
        shrink_grad = jnp.einsum(
            "tf,td->fd", active_low, feed_low, preferred_element_type=jnp.float32
        )
        bias_out_grad = jnp.sum(feed_low, axis=0, dtype=jnp.float32)
        active_grad = jnp.einsum("td,fd->tf", feed_low, shrink, preferred_element_type=jnp.float32)
        unused_gelu, gelu_pull = jax.vjp(gelu_exact, before)
        before_low = gelu_pull(active_grad)[0].astype(jnp.bfloat16)
        expand_grad = jnp.einsum(
            "td,tf->df", normed_low, before_low, preferred_element_type=jnp.float32
        )
        bias_in_grad = jnp.sum(before_low, axis=0, dtype=jnp.float32)
        normed_grad = sum_two_grad + jnp.einsum(
            "tf,df->td", before_low, expand, preferred_element_type=jnp.float32
        )
        unused_one, first_pull = jax.vjp(layer_norm, summed_one, gain_one, shift_one)
        sum_one_grad, gain_one_grad, shift_one_grad = first_pull(normed_grad)
        branch_low = sum_one_grad.astype(jnp.bfloat16)
        mixing_grad = jnp.einsum(
            "td,te->de", mixed_low, branch_low, preferred_element_type=jnp.float32
        )
        bias_mix_grad = jnp.sum(branch_low, axis=0, dtype=jnp.float32)
        mixed_grad_low = jnp.einsum(
            "te,de->td", branch_low, mixing, preferred_element_type=jnp.float32
        ).astype(jnp.bfloat16)
        query_grad, key_grad, value_grad = flash_backward(
            bounds, queries, key_value, mixed_grad_low, lse, low_line, high_line
        )
        query_term = jnp.einsum(
            "td,te->de", layer_low, query_grad, preferred_element_type=jnp.float32
        )
        key_term = jnp.einsum(
            "td,te->de", state_window, key_grad, preferred_element_type=jnp.float32
        )
        value_term = jnp.einsum(
            "td,te->de", state_window, value_grad, preferred_element_type=jnp.float32
        )
        bias_q_grad = jnp.sum(query_grad, axis=0, dtype=jnp.float32)
        bias_v_grad = jnp.sum(value_grad, axis=0, dtype=jnp.float32)
        window_grad = jnp.einsum(
            "te,de->td", key_grad, project[:, width : 2 * width], preferred_element_type=jnp.float32
        ) + jnp.einsum(
            "te,de->td", value_grad, project[:, 2 * width :], preferred_element_type=jnp.float32
        )
        state_grad = (
            sum_one_grad
            + jnp.einsum(
                "te,de->td", query_grad, project[:, :width], preferred_element_type=jnp.float32
            )
            + window_back(window_grad, core, row_count)
        )
        vectors = jnp.concatenate(
            [
                bias_q_grad,
                bias_v_grad,
                bias_mix_grad,
                shift_one_grad,
                bias_in_grad,
                bias_out_grad,
                shift_two_grad,
            ]
        ).reshape(8, -1)
        gains = jnp.concatenate([gain_one_grad, gain_two_grad]).reshape(8, -1)
        vectors = jnp.concatenate([vectors, gains], axis=1).astype(jnp.bfloat16)
        vectors = vectors.reshape(8, 4, -1).transpose(1, 0, 2).reshape(32, 1, -1)
        vectors = jnp.pad(vectors, ((0, 0), (0, 7), (0, width - vectors.shape[2])))
        pieces = jnp.concatenate(
            [
                parted(query_term.astype(jnp.bfloat16), 1),
                parted(key_term.astype(jnp.bfloat16), 1),
                parted(value_term.astype(jnp.bfloat16), 1),
                parted(mixing_grad.astype(jnp.bfloat16), 1),
                parted(expand_grad.astype(jnp.bfloat16), hidden_units // width),
                parted(shrink_grad.astype(jnp.bfloat16), 1),
                vectors,
            ],
            axis=1,
        )
        results[layer_index] = lax.psum_scatter(pieces, BOTH, scatter_dimension=0, tiled=True)[0]
    both = jnp.concatenate(results)
    both = lax.all_gather(both, "grp", axis=0, tiled=False)
    both = both.reshape(4, LAYERS, -1, width).transpose(1, 0, 2, 3).astype(jnp.float32)
    outs = []
    begin_at = 0
    for count, columns in zip(counts, (3, 1, hidden_units // width, 1)):
        part = both[:, :, begin_at : begin_at + count]
        part = part.reshape(LAYERS, 4, columns, count // columns, width).transpose(0, 1, 3, 2, 4)
        outs.append(part.reshape(LAYERS, 4 * count // columns, columns * width))
        begin_at += count
    quarter_len = (bias_count + norm_gains.shape[1]) // 4
    vectors = both[:, :, begin_at, :quarter_len].reshape(LAYERS, -1)
    input_grad = turn_rows(state_grad.astype(jnp.bfloat16)).astype(jnp.float32)
    return (
        activations,
        input_grad,
        outs[0],
        outs[1],
        outs[2],
        outs[3],
        vectors[:, :bias_count],
        vectors[:, bias_count:],
    )


def solution(mesh):
    in_specs = (
        P(("grp", "shard"), None),
        P(("grp", "shard"), None),
        P(),
        P(),
        P(None, "shard", None),
        P(None, "shard", None),
        P(None, "shard", None),
        P(None, "shard", None),
        P(None, "shard"),
        P(None, "shard"),
    )
    out_specs = (
        P(("grp", "shard"), None),
        P(("grp", "shard"), None),
        P(None, "shard", None),
        P(None, "shard", None),
        P(None, "shard", None),
        P(None, "shard", None),
        P(None, "shard"),
        P(None, "shard"),
    )
    body = on_device_turned if mesh.shape["shard"] == 8 and mesh.shape["grp"] == 4 else on_device
    return jax.shard_map(
        body, mesh=mesh, in_specs=in_specs, out_specs=out_specs, check_vma=False
    )
```

```python
import functools

import jax
import jax.numpy as jnp
from jax import lax
from jax.experimental import pallas as pl
from jax.experimental.pallas import tpu as pltpu
from jax.sharding import PartitionSpec as P

HEADS = 12
LAYERS = 2
SEQ_MAX = 2048


EPSILON = 1e-12
NEGATIVE = -1e30


def passed_along(shard, axis, by):
    size = lax.axis_size(axis)
    pairs = [(i, i + by) for i in range(size) if 0 <= i + by < size]
    return lax.ppermute(shard, axis, pairs)


def layer_norm(values, gain, shift):
    middle = jnp.mean(values, axis=-1, keepdims=True)
    centered = values - middle
    spread = jnp.mean(centered * centered, axis=-1, keepdims=True)
    return centered * lax.rsqrt(spread + EPSILON) * gain + shift


def gelu_exact(values):
    return jax.nn.gelu(values, approximate=False)


def keep_same(carried):
    return carried


def group_ends(seq_lengths, seq_order, group_index):
    lengths_row = lax.dynamic_index_in_dim(seq_lengths, group_index, 0, keepdims=False)
    order_row = lax.dynamic_index_in_dim(seq_order, group_index, 0, keepdims=False)
    places = jnp.arange(lengths_row.shape[0], dtype=jnp.int32)
    picked = order_row[:, None] == places[None, :]
    placed = jnp.sum(jnp.where(picked, lengths_row[None, :], 0), axis=1, dtype=jnp.int32)
    return jnp.cumsum(placed, dtype=jnp.int32)


def slot_segments(slot_index, seq_ends):
    flattened = slot_index.reshape(-1)
    counted = jnp.sum(
        (seq_ends[None, :] <= flattened[:, None]).astype(jnp.int32), axis=1, dtype=jnp.int32
    )
    return counted.reshape(slot_index.shape)


def unpack_weights(weights, width, hidden_units):
    bias_vec = weights[4].astype(jnp.float32)
    gain_vec = weights[5].astype(jnp.float32)
    piece_lens = [width, width, width, width, hidden_units, width, width]
    bias_list = []
    begin_at = 0
    for piece_len in piece_lens:
        bias_list.append(bias_vec[begin_at : begin_at + piece_len])
        begin_at = begin_at + piece_len
    return (
        weights[0],
        weights[1],
        weights[2],
        weights[3],
        bias_list,
        gain_vec[:width],
        gain_vec[width:],
    )


def block_probs(queries, keys_block, seg_block, own_segment, log_total, score_scale):
    raw_scores = jnp.einsum("qhd,khd->hqk", queries, keys_block, preferred_element_type=jnp.float32)
    allowed = (own_segment[:, None] == seg_block[None, :])[None]
    return jnp.where(allowed, jnp.exp(raw_scores * score_scale - log_total[:, :, None]), 0.0)


def gather_window(key_rows, value_rows, reach_blocks):
    key_list = []
    value_list = []
    for step_offset in range(-reach_blocks, reach_blocks + 1):
        if step_offset == 0:
            moved = (key_rows, value_rows)
        else:
            moved = passed_along((key_rows, value_rows), "shard", -step_offset)
        key_list.append(moved[0])
        value_list.append(moved[1])
    return (jnp.stack(key_list), jnp.stack(value_list))


def return_parts(key_parts, value_parts, reach_blocks):
    key_total = key_parts[reach_blocks]
    value_total = value_parts[reach_blocks]
    for step_offset in range(-reach_blocks, reach_blocks + 1):
        if step_offset != 0:
            arrived = (
                passed_along(
                    key_parts[step_offset + reach_blocks].astype(jnp.bfloat16), "shard", step_offset
                ).astype(jnp.float32),
                passed_along(
                    value_parts[step_offset + reach_blocks].astype(jnp.bfloat16),
                    "shard",
                    step_offset,
                ).astype(jnp.float32),
            )
            key_total = key_total + arrived[0]
            value_total = value_total + arrived[1]
    return (key_total, value_total)


def attend_forward(
    queries, window_keys, window_values, window_segment, live_block, own_segment, score_scale
):
    row_count, head_count, head_dim = queries.shape

    def stats_step(carry, items):
        keys_block, seg_block, alive = items

        def stats_compute(state_pair):
            running_top, running_sum = state_pair
            allowed = (own_segment[:, None] == seg_block[None, :])[None]
            raw_scores = jnp.einsum(
                "qhd,khd->hqk", queries, keys_block, preferred_element_type=jnp.float32
            )
            scores = jnp.where(allowed, raw_scores * score_scale, NEGATIVE)
            new_top = jnp.maximum(running_top, jnp.max(scores, axis=-1))
            weighted = jnp.where(allowed, jnp.exp(scores - new_top[:, :, None]), 0.0)
            return (
                new_top,
                running_sum * jnp.exp(running_top - new_top) + jnp.sum(weighted, axis=-1),
            )

        return (lax.cond(alive, stats_compute, keep_same, carry), None)

    begin_stats = (
        jnp.full((head_count, row_count), NEGATIVE, jnp.float32),
        jnp.zeros((head_count, row_count), jnp.float32),
    )
    (running_top, running_sum), unused = lax.scan(
        stats_step, begin_stats, (window_keys, window_segment, live_block)
    )
    log_total = running_top + jnp.log(running_sum)

    def mix_step(carry, items):
        keys_block, values_block, seg_block, alive = items

        def mix_compute(state_pair):
            mixed, extra = state_pair
            probs = block_probs(queries, keys_block, seg_block, own_segment, log_total, score_scale)
            probs_low = probs.astype(jnp.bfloat16)
            rest_low = (probs - lax.optimization_barrier(probs_low).astype(jnp.float32)).astype(
                jnp.bfloat16
            )
            mixed = mixed + jnp.einsum(
                "hqk,khd->qhd", probs_low, values_block, preferred_element_type=jnp.float32
            )
            extra = extra + jnp.einsum(
                "hqk,khd->qhd", rest_low, values_block, preferred_element_type=jnp.float32
            )
            return (mixed, extra)

        return (lax.cond(alive, mix_compute, keep_same, carry), None)

    zeros_mix = jnp.zeros((row_count, head_count, head_dim), jnp.float32)
    (mixed, extra), unused = lax.scan(
        mix_step, (zeros_mix, zeros_mix), (window_keys, window_values, window_segment, live_block)
    )
    return (log_total, mixed, mixed + extra)


def attend_backward(
    queries,
    window_keys,
    window_values,
    window_segment,
    live_block,
    own_segment,
    log_total,
    delta,
    grad_low,
    score_scale,
):

    def grad_step(query_grad, items):
        keys_block, values_block, seg_block, alive = items

        def grad_compute(carried):
            probs = block_probs(queries, keys_block, seg_block, own_segment, log_total, score_scale)
            prob_grad = jnp.einsum(
                "qhd,khd->hqk", grad_low, values_block, preferred_element_type=jnp.float32
            )
            score_low = (probs * (prob_grad - delta[:, :, None])).astype(jnp.bfloat16)
            carried = carried + jnp.einsum(
                "hqk,khd->qhd", score_low, keys_block, preferred_element_type=jnp.float32
            )
            probs_low = probs.astype(jnp.bfloat16)
            value_part = jnp.einsum(
                "hqk,qhd->khd", probs_low, grad_low, preferred_element_type=jnp.float32
            )
            key_part = jnp.einsum(
                "hqk,qhd->khd", score_low, queries, preferred_element_type=jnp.float32
            )
            return (carried, (key_part, value_part))

        def skipped(carried):
            nothing = jnp.zeros(keys_block.shape, jnp.float32)
            return (carried, (nothing, nothing))

        return lax.cond(alive, grad_compute, skipped, query_grad)

    zero_grad = jnp.zeros(queries.shape, jnp.float32)
    query_grad, key_value = lax.scan(
        grad_step, zero_grad, (window_keys, window_values, window_segment, live_block)
    )
    return (query_grad, key_value)


def on_device(
    tokens,
    cotangent,
    seq_lengths,
    seq_order,
    w_project,
    w_mixer,
    w_expand,
    w_reduce,
    biases,
    norm_gains,
):
    row_count, width = tokens.shape
    shard_count = lax.axis_size("shard")
    shard_index = lax.axis_index("shard")
    group_index = lax.axis_index("grp")
    head_dim = width // HEADS
    hidden_units = w_expand.shape[2]
    score_scale = head_dim ** (-0.5)
    longest = min(SEQ_MAX, row_count * shard_count // 4)
    reach_blocks = longest // row_count
    seq_count = seq_lengths.shape[1]
    seq_ends = group_ends(seq_lengths, seq_order, group_index)
    neighbour = shard_index + jnp.arange(-reach_blocks, reach_blocks + 1, dtype=jnp.int32)
    slot_index = neighbour[:, None] * row_count + jnp.arange(row_count, dtype=jnp.int32)[None, :]
    window_segment = slot_segments(slot_index, seq_ends)
    own_segment = window_segment[reach_blocks]
    inside = (neighbour >= 0) & (neighbour < shard_count)
    live_block = (
        inside
        & (window_segment[:, 0] <= own_segment[row_count - 1])
        & (window_segment[:, row_count - 1] >= own_segment[0])
    )
    valid_rows = (own_segment < seq_count).astype(jnp.float32)[:, None]
    hidden_state = tokens.astype(jnp.float32)
    state_low = tokens
    kept_list = []
    for layer_index in range(LAYERS):
        weights = (
            lax.all_gather(w_project[layer_index], "shard", axis=0, tiled=True),
            lax.all_gather(w_mixer[layer_index], "shard", axis=0, tiled=True),
            lax.all_gather(w_expand[layer_index], "shard", axis=0, tiled=True),
            lax.all_gather(w_reduce[layer_index], "shard", axis=0, tiled=True),
            lax.all_gather(biases[layer_index], "shard", axis=0, tiled=True),
            lax.all_gather(norm_gains[layer_index], "shard", axis=0, tiled=True),
        )
        project, mixing, expand, shrink, bias_list, gain_one, gain_two = unpack_weights(
            weights, width, hidden_units
        )
        bias_q, bias_v, bias_mix, shift_one, bias_in, bias_out, shift_two = bias_list
        projected = jnp.dot(state_low, project, preferred_element_type=jnp.float32)
        projected = projected + jnp.concatenate([bias_q, jnp.zeros_like(bias_q), bias_v])
        projected_low = projected.astype(jnp.bfloat16)
        queries = projected_low[:, :width].reshape(row_count, HEADS, head_dim)
        key_rows = projected_low[:, width : 2 * width].reshape(row_count, HEADS, head_dim)
        value_rows = projected_low[:, 2 * width :].reshape(row_count, HEADS, head_dim)
        window_keys, window_values = gather_window(key_rows, value_rows, reach_blocks)
        log_total, mixed, full_mix = attend_forward(
            queries,
            window_keys,
            window_values,
            window_segment,
            live_block,
            own_segment,
            score_scale,
        )
        mixed_low = mixed.reshape(row_count, width).astype(jnp.bfloat16)
        branch = jnp.dot(mixed_low, mixing, preferred_element_type=jnp.float32) + bias_mix
        summed_one = hidden_state + branch
        normed_one = layer_norm(summed_one, gain_one, shift_one)
        normed_low = normed_one.astype(jnp.bfloat16)
        before = jnp.dot(normed_low, expand, preferred_element_type=jnp.float32) + bias_in
        active_low = gelu_exact(before).astype(jnp.bfloat16)
        feed_out = jnp.dot(active_low, shrink, preferred_element_type=jnp.float32) + bias_out
        summed_two = normed_one + feed_out
        hidden_state = layer_norm(summed_two, gain_two, shift_two)
        kept_list.append(
            (
                state_low,
                queries,
                key_rows,
                value_rows,
                window_keys,
                window_values,
                log_total,
                full_mix,
                mixed_low,
                summed_one,
                normed_low,
                before,
                active_low,
                summed_two,
                weights,
            )
        )
        state_low = hidden_state.astype(jnp.bfloat16)
    activations = (hidden_state * valid_rows).astype(jnp.bfloat16)
    state_grad = cotangent.astype(jnp.float32) * valid_rows
    results = [None] * LAYERS
    for layer_index in reversed(range(LAYERS)):
        (
            layer_low,
            queries,
            key_rows,
            value_rows,
            window_keys,
            window_values,
            log_total,
            full_mix,
            mixed_low,
            summed_one,
            normed_low,
            before,
            active_low,
            summed_two,
            kept_weights,
        ) = kept_list[layer_index]
        weights = (
            lax.all_gather(w_project[layer_index], "shard", axis=0, tiled=True),
            lax.all_gather(w_mixer[layer_index], "shard", axis=0, tiled=True),
            lax.all_gather(w_expand[layer_index], "shard", axis=0, tiled=True),
            lax.all_gather(w_reduce[layer_index], "shard", axis=0, tiled=True),
            lax.all_gather(biases[layer_index], "shard", axis=0, tiled=True),
            lax.all_gather(norm_gains[layer_index], "shard", axis=0, tiled=True),
        )
        project, mixing, expand, shrink, bias_list, gain_one, gain_two = unpack_weights(
            weights, width, hidden_units
        )
        bias_q, bias_v, bias_mix, shift_one, bias_in, bias_out, shift_two = bias_list
        unused_two, norm_pull = jax.vjp(layer_norm, summed_two, gain_two, shift_two)
        sum_two_grad, gain_two_grad, shift_two_grad = norm_pull(state_grad)
        feed_low = sum_two_grad.astype(jnp.bfloat16)
        shrink_grad = jnp.einsum(
            "tf,td->fd", active_low, feed_low, preferred_element_type=jnp.float32
        )
        bias_out_grad = jnp.sum(feed_low, axis=0, dtype=jnp.float32)
        active_grad = jnp.einsum("td,fd->tf", feed_low, shrink, preferred_element_type=jnp.float32)
        unused_gelu, gelu_pull = jax.vjp(gelu_exact, before)
        before_low = gelu_pull(active_grad)[0].astype(jnp.bfloat16)
        expand_grad = jnp.einsum(
            "td,tf->df", normed_low, before_low, preferred_element_type=jnp.float32
        )
        bias_in_grad = jnp.sum(before_low, axis=0, dtype=jnp.float32)
        normed_grad = sum_two_grad + jnp.einsum(
            "tf,df->td", before_low, expand, preferred_element_type=jnp.float32
        )
        unused_one, first_pull = jax.vjp(layer_norm, summed_one, gain_one, shift_one)
        sum_one_grad, gain_one_grad, shift_one_grad = first_pull(normed_grad)
        branch_low = sum_one_grad.astype(jnp.bfloat16)
        mixing_grad = jnp.einsum(
            "td,te->de", mixed_low, branch_low, preferred_element_type=jnp.float32
        )
        bias_mix_grad = jnp.sum(branch_low, axis=0, dtype=jnp.float32)
        mixed_grad = jnp.einsum("te,de->td", branch_low, mixing, preferred_element_type=jnp.float32)
        mixed_grad_low = mixed_grad.astype(jnp.bfloat16).reshape(row_count, HEADS, head_dim)
        delta = jnp.sum(mixed_grad_low.astype(jnp.float32) * full_mix, axis=-1).T
        query_grad, key_value = attend_backward(
            queries,
            window_keys,
            window_values,
            window_segment,
            live_block,
            own_segment,
            log_total,
            delta,
            mixed_grad_low,
            score_scale,
        )
        key_total, value_total = return_parts(key_value[0], key_value[1], reach_blocks)
        projected_grad = jnp.concatenate(
            [
                (query_grad * score_scale).reshape(row_count, width),
                (key_total * score_scale).reshape(row_count, width),
                value_total.reshape(row_count, width),
            ],
            axis=1,
        )
        projected_low = projected_grad.astype(jnp.bfloat16)
        project_grad = jnp.einsum(
            "td,te->de", layer_low, projected_low, preferred_element_type=jnp.float32
        )
        bias_q_grad = jnp.sum(projected_low[:, :width], axis=0, dtype=jnp.float32)
        bias_v_grad = jnp.sum(projected_low[:, 2 * width :], axis=0, dtype=jnp.float32)
        state_grad = sum_one_grad + jnp.einsum(
            "te,de->td", projected_low, project, preferred_element_type=jnp.float32
        )
        bias_all = jnp.concatenate(
            [
                bias_q_grad,
                bias_v_grad,
                bias_mix_grad,
                shift_one_grad,
                bias_in_grad,
                bias_out_grad,
                shift_two_grad,
            ]
        )
        gain_all = jnp.concatenate([gain_one_grad, gain_two_grad])
        shares = (
            lax.psum_scatter(
                project_grad.astype(jnp.bfloat16), "shard", scatter_dimension=0, tiled=True
            ).astype(jnp.float32),
            lax.psum_scatter(
                mixing_grad.astype(jnp.bfloat16), "shard", scatter_dimension=0, tiled=True
            ).astype(jnp.float32),
            lax.psum_scatter(
                expand_grad.astype(jnp.bfloat16), "shard", scatter_dimension=0, tiled=True
            ).astype(jnp.float32),
            lax.psum_scatter(
                shrink_grad.astype(jnp.bfloat16), "shard", scatter_dimension=0, tiled=True
            ).astype(jnp.float32),
            lax.psum_scatter(
                bias_all.astype(jnp.bfloat16), "shard", scatter_dimension=0, tiled=True
            ).astype(jnp.float32),
            lax.psum_scatter(
                gain_all.astype(jnp.bfloat16), "shard", scatter_dimension=0, tiled=True
            ).astype(jnp.float32),
        )
        shares = (
            lax.psum(shares[0].astype(jnp.bfloat16), "grp").astype(jnp.float32),
            lax.psum(shares[1].astype(jnp.bfloat16), "grp").astype(jnp.float32),
            lax.psum(shares[2].astype(jnp.bfloat16), "grp").astype(jnp.float32),
            lax.psum(shares[3].astype(jnp.bfloat16), "grp").astype(jnp.float32),
            lax.psum(shares[4].astype(jnp.bfloat16), "grp").astype(jnp.float32),
            lax.psum(shares[5].astype(jnp.bfloat16), "grp").astype(jnp.float32),
        )
        results[layer_index] = shares
    stacked = [jnp.stack([layer_share[member] for layer_share in results]) for member in range(6)]
    return (
        activations,
        state_grad,
        stacked[0],
        stacked[1],
        stacked[2],
        stacked[3],
        stacked[4],
        stacked[5],
    )


HEAD_SCALE = 0.125


def fold_rows(values, combine):
    total = values[:8]
    for begin_at in range(8, values.shape[0], 8):
        total = combine(total, values[begin_at : begin_at + 8])
    return total


def halves_of(block):
    lane = lax.broadcasted_iota(jnp.int32, block.shape, 1)
    nothing = jnp.zeros_like(block)
    return (jnp.where(lane < 64, block, nothing), jnp.where(lane < 64, nothing, block))


def turned_dot(keys, queries):
    return lax.dot_general(
        keys, queries, (((1,), (1,)), ((), ())), preferred_element_type=jnp.float32
    )


def across_dot(weight, values):
    return lax.dot_general(
        weight, values, (((0,), (0,)), ((), ())), preferred_element_type=jnp.float32
    )


def fill_mask(first, last, key_tile_rows, low_ref, high_ref, mask_scr):
    low = low_ref[0:1, :]
    high = high_ref[0:1, :]

    def mask_step(key_tile, carry):
        begin_at = pl.multiple_of(key_tile * key_tile_rows, key_tile_rows)
        shape = (key_tile_rows, low_ref.shape[1])
        place = lax.broadcasted_iota(jnp.int32, shape, 0) + begin_at
        allowed = (place >= low) & (place < high)
        mask_scr[pl.ds(begin_at, key_tile_rows), :] = jnp.where(allowed, 0.0, NEGATIVE)
        return carry

    lax.fori_loop(first, last, mask_step, 0)


def flash_forward_kernel(
    key_tile_rows, bounds, q_ref, kv_ref, low_ref, high_ref, mix_ref, lse_ref, mask_scr, score_scr
):
    rows, width = q_ref.shape
    pairs = width // 128
    first = bounds[0] // key_tile_rows
    last = (bounds[1] + key_tile_rows - 1) // key_tile_rows
    fill_mask(first, last, key_tile_rows, low_ref, high_ref, mask_scr)

    def pair_step(pair, unused):
        lanes = pl.ds(pl.multiple_of(pair * 128, 128), 128)
        value_lanes = pl.ds(pl.multiple_of(pair * 128 + width, 128), 128)
        heads = halves_of(q_ref[:, lanes] * jnp.bfloat16(HEAD_SCALE))

        def score_step(key_tile, tops):
            key_span = pl.ds(pl.multiple_of(key_tile * key_tile_rows, key_tile_rows), key_tile_rows)
            keys = kv_ref[key_span, lanes]
            mask = mask_scr[key_span, :]
            out = []
            for head in range(2):
                scores = turned_dot(keys, heads[head]) + mask
                score_scr[head, key_span, :] = scores
                out.append(jnp.maximum(tops[head], fold_rows(scores, jnp.maximum)))
            return tuple(out)

        floor = jnp.full((8, rows), NEGATIVE, jnp.float32)
        tops = lax.fori_loop(first, last, score_step, (floor, floor))
        tops = [jnp.max(top, axis=0, keepdims=True) for top in tops]

        def mix_step(key_tile, carry):
            key_span = pl.ds(pl.multiple_of(key_tile * key_tile_rows, key_tile_rows), key_tile_rows)
            values = halves_of(kv_ref[key_span, value_lanes])
            totals, mixed = [], carry[2]
            for head in range(2):
                weight = jnp.exp(score_scr[head, key_span, :] - tops[head])
                totals.append(carry[head] + fold_rows(weight, jnp.add))
                mixed = mixed + across_dot(weight.astype(jnp.bfloat16), values[head])
            return (totals[0], totals[1], mixed)

        zero = jnp.zeros((8, rows), jnp.float32)
        carry = lax.fori_loop(
            first, last, mix_step, (zero, zero, jnp.zeros((rows, 128), jnp.float32))
        )
        totals = [jnp.sum(total, axis=0, keepdims=True) for total in carry[:2]]
        scale = jnp.concatenate(
            [jnp.broadcast_to(1.0 / total, (64, rows)) for total in totals], axis=0
        ).T
        mix_ref[:, lanes] = (carry[2] * scale).astype(jnp.bfloat16)
        lse_rows = [tops[head] + jnp.log(totals[head]) for head in range(2)]
        lse_ref[pl.ds(pl.multiple_of(pair * 8, 8), 8), :] = jnp.concatenate(
            [jnp.broadcast_to(line, (4, rows)) for line in lse_rows]
        )
        return unused

    lax.fori_loop(0, pairs, pair_step, 0)


def flash_backward_kernel(
    key_tile_rows,
    bounds,
    q_ref,
    kv_ref,
    grad_ref,
    lse_ref,
    low_ref,
    high_ref,
    q_grad_ref,
    kv_grad_ref,
    mask_scr,
    prob_scr,
    slope_scr,
):
    rows, width = q_ref.shape
    pairs = width // 128
    first = bounds[0] // key_tile_rows
    last = (bounds[1] + key_tile_rows - 1) // key_tile_rows
    fill_mask(first, last, key_tile_rows, low_ref, high_ref, mask_scr)
    tiles = kv_ref.shape[0] // key_tile_rows

    def clear_step(key_tile, carry):
        key_span = pl.ds(pl.multiple_of(key_tile * key_tile_rows, key_tile_rows), key_tile_rows)
        kv_grad_ref[key_span, :] = jnp.zeros((key_tile_rows, 2 * width), jnp.bfloat16)
        return carry

    lax.fori_loop(0, first, clear_step, 0)
    lax.fori_loop(last, tiles, clear_step, 0)

    def pair_step(pair, unused):
        lanes = pl.ds(pl.multiple_of(pair * 128, 128), 128)
        value_lanes = pl.ds(pl.multiple_of(pair * 128 + width, 128), 128)
        heads = halves_of(q_ref[:, lanes] * jnp.bfloat16(HEAD_SCALE))
        grads = halves_of(grad_ref[:, lanes])
        lse_rows = lse_ref[pl.ds(pl.multiple_of(pair * 8, 8), 8), :]
        lse = (lse_rows[0:1], lse_rows[4:5])

        def prob_step(key_tile, deltas):
            key_span = pl.ds(pl.multiple_of(key_tile * key_tile_rows, key_tile_rows), key_tile_rows)
            keys = kv_ref[key_span, lanes]
            values = kv_ref[key_span, value_lanes]
            mask = mask_scr[key_span, :]
            out = []
            for head in range(2):
                scores = turned_dot(keys, heads[head])
                probs = jnp.exp((scores - lse[head]) + mask)
                slope = turned_dot(values, grads[head])
                prob_scr[head, key_span, :] = probs
                slope_scr[head, key_span, :] = slope
                out.append(deltas[head] + fold_rows(probs * slope, jnp.add))
            return tuple(out)

        zero = jnp.zeros((8, rows), jnp.float32)
        deltas = lax.fori_loop(first, last, prob_step, (zero, zero))
        deltas = [jnp.sum(delta, axis=0, keepdims=True) for delta in deltas]

        def grad_step(key_tile, q_sum):
            key_span = pl.ds(pl.multiple_of(key_tile * key_tile_rows, key_tile_rows), key_tile_rows)
            keys = halves_of(kv_ref[key_span, lanes])
            k_part = None
            v_part = None
            for head in range(2):
                probs = prob_scr[head, key_span, :]
                low_slope = (probs * (slope_scr[head, key_span, :] - deltas[head])).astype(
                    jnp.bfloat16
                )
                v_term = jnp.dot(
                    probs.astype(jnp.bfloat16), grads[head], preferred_element_type=jnp.float32
                )
                k_term = jnp.dot(low_slope, heads[head], preferred_element_type=jnp.float32)
                q_sum = q_sum + across_dot(low_slope, keys[head])
                v_part = v_term if head == 0 else v_part + v_term
                k_part = k_term if head == 0 else k_part + k_term
            kv_grad_ref[key_span, lanes] = k_part.astype(jnp.bfloat16)
            kv_grad_ref[key_span, value_lanes] = v_part.astype(jnp.bfloat16)
            return q_sum

        q_part = lax.fori_loop(first, last, grad_step, jnp.zeros((rows, 128), jnp.float32))
        q_grad_ref[:, lanes] = (q_part * HEAD_SCALE).astype(jnp.bfloat16)
        return unused

    lax.fori_loop(0, pairs, pair_step, 0)


def whole_block(shape):
    return pl.BlockSpec(shape, lambda i, b: (0,) * len(shape), pipeline_mode=pl.Buffered(1))


FORWARD_KEYS = 512
BACKWARD_KEYS = 512


def flash_forward(bounds, queries, key_value, low, high):
    rows, width = queries.shape
    window = key_value.shape[0]
    pairs = width // 128
    line = whole_block((8, rows))
    return pl.pallas_call(
        functools.partial(flash_forward_kernel, FORWARD_KEYS),
        out_shape=(
            jax.ShapeDtypeStruct((rows, width), jnp.bfloat16),
            jax.ShapeDtypeStruct((pairs * 8, rows), jnp.float32),
        ),
        grid_spec=pltpu.PrefetchScalarGridSpec(
            num_scalar_prefetch=1,
            grid=(1,),
            in_specs=[whole_block((rows, width)), whole_block((window, 2 * width)), line, line],
            out_specs=[whole_block((rows, width)), whole_block((pairs * 8, rows))],
            scratch_shapes=[
                pltpu.VMEM((window, rows), jnp.float32),
                pltpu.VMEM((2, window, rows), jnp.float32),
            ],
        ),
        compiler_params=pltpu.CompilerParams(vmem_limit_bytes=48 * 2**20),
        cost_estimate=pl.CostEstimate(
            flops=4 * rows * width * 2560, bytes_accessed=12 * 2**20, transcendentals=rows * 12 * 2560
        ),
        name="flash_forward",
    )(bounds, queries, key_value, low, high)


def flash_backward(bounds, queries, key_value, grad_low, lse, low, high):
    rows, width = queries.shape
    window = key_value.shape[0]
    pairs = width // 128
    own = whole_block((rows, width))
    wide = whole_block((window, 2 * width))
    line = whole_block((8, rows))
    return pl.pallas_call(
        functools.partial(flash_backward_kernel, BACKWARD_KEYS),
        out_shape=(
            jax.ShapeDtypeStruct((rows, width), jnp.bfloat16),
            jax.ShapeDtypeStruct((window, 2 * width), jnp.bfloat16),
        ),
        grid_spec=pltpu.PrefetchScalarGridSpec(
            num_scalar_prefetch=1,
            grid=(1,),
            in_specs=[own, wide, own, whole_block((pairs * 8, rows)), line, line],
            out_specs=[own, wide],
            scratch_shapes=[
                pltpu.VMEM((window, rows), jnp.float32),
                pltpu.VMEM((2, window, rows), jnp.float32),
                pltpu.VMEM((2, window, rows), jnp.float32),
            ],
        ),
        compiler_params=pltpu.CompilerParams(vmem_limit_bytes=56 * 2**20),
        cost_estimate=pl.CostEstimate(
            flops=10 * rows * width * 2560,
            bytes_accessed=20 * 2**20,
            transcendentals=rows * 12 * 2560,
        ),
        name="flash_backward",
    )(bounds, queries, key_value, grad_low, lse, low, high)


GRP_Y, GRP_CORE, SHARD_Z, SHARD_X = 2, 2, 4, 2
BOTH = ("grp", "shard")


def device_pairs(place):
    pairs = []
    for y in range(GRP_Y):
        for core in range(GRP_CORE):
            for z in range(SHARD_Z):
                for x in range(SHARD_X):
                    target = place(y, core, z, x)
                    if target is not None:
                        ty, tcore, tz, tx = target
                        pairs.append(
                            (
                                (y * GRP_CORE + core) * SHARD_Z * SHARD_X + z * SHARD_X + x,
                                (ty * GRP_CORE + tcore) * SHARD_Z * SHARD_X + tz * SHARD_X + tx,
                            )
                        )
    return pairs


def send(values, place):
    return lax.ppermute(values, BOTH, device_pairs(place))


def turn_rows(values):
    return send(values, lambda y, core, z, x: (y, x, z, core))


def swap_core(values):
    return send(values, lambda y, core, z, x: (y, 1 - core, z, x))


def send_up(values):
    return send(values, lambda y, core, z, x: (y, core, z + 1, x) if z + 1 < SHARD_Z else None)


def send_down(values):
    return send(values, lambda y, core, z, x: (y, core, z - 1, x) if z > 0 else None)


def window_of(rows, core):
    from_below = send_up(rows)
    from_above = send_down(rows)
    other = swap_core(jnp.concatenate([rows, jnp.where(core == 1, from_below, from_above)]))
    count = rows.shape[0]
    other_own, other_far = other[:count], other[count:]
    return jnp.concatenate(
        [
            from_below,
            jnp.where(core == 0, other_far, other_own),
            rows,
            jnp.where(core == 0, other_own, other_far),
            from_above,
        ]
    )


def window_back(parts, core, count):
    low = parts.astype(jnp.bfloat16)
    block = [low[i * count : (i + 1) * count] for i in range(5)]
    near = jnp.where(core == 0, block[3], block[1])
    far = jnp.where(core == 0, block[1], block[3])
    other = swap_core(jnp.concatenate([near, far])).astype(jnp.float32)
    other_near, other_far = other[:count], other[count:]
    below = block[0].astype(jnp.float32)
    above = block[4].astype(jnp.float32)
    below = jnp.where(core == 1, below + other_far, below).astype(jnp.bfloat16)
    above = jnp.where(core == 0, above + other_far, above).astype(jnp.bfloat16)
    from_above = send_down(below).astype(jnp.float32)
    from_below = send_up(above).astype(jnp.float32)
    return parts[2 * count : 3 * count] + other_near + from_above + from_below


def unpack_kernel(kinds, in_ref, *outs):
    width = in_ref.shape[-1]
    share = in_ref.shape[3]
    place = 0
    for kind, ref in zip(kinds, outs):
        if kind == "columns":
            for column in range(ref.shape[-1] // width):
                ref[:, 0, :, column * width : (column + 1) * width] = in_ref[0, :, place]
                place += 1
        else:
            for piece in range(ref.shape[2] // share):
                ref[:, 0, piece * share : (piece + 1) * share, :] = in_ref[0, :, place]
                place += 1


def unpack_weights_of(pieces, kinds, shapes):
    quarters, shards, places, share, width = pieces.shape
    outs = pl.pallas_call(
        functools.partial(unpack_kernel, kinds),
        out_shape=[
            jax.ShapeDtypeStruct((shards, quarters, rows, wide), pieces.dtype)
            for rows, wide in shapes
        ],
        grid=(quarters,),
        in_specs=[pl.BlockSpec((1, shards, places, share, width), lambda q: (q, 0, 0, 0, 0))],
        out_specs=[
            pl.BlockSpec((shards, 1, rows, wide), lambda q: (0, q, 0, 0)) for rows, wide in shapes
        ],
        compiler_params=pltpu.CompilerParams(vmem_limit_bytes=32 * 2**20),
        cost_estimate=pl.CostEstimate(flops=0, bytes_accessed=4 * pieces.size, transcendentals=0),
        name="unpack_weights",
    )(pieces)
    return [out.reshape(-1, out.shape[-1]) for out in outs]


def pick_kernel(me, project_ref, mixer_ref, expand_ref, reduce_ref, small_ref, *outs):
    def fill(a_ref, f_ref):
        share, width = a_ref.shape[-2:]
        for column in range(3):
            a_ref[column] = project_ref[0, :, column * width : (column + 1) * width]
        a_ref[3] = jnp.zeros((share, width), a_ref.dtype)
        a_ref[3, 0:8, :] = small_ref[...]
        f_ref[0] = mixer_ref[0]
        wide = expand_ref.shape[-1] // width
        for column in range(wide):
            f_ref[1 + column] = expand_ref[0, :, column * width : (column + 1) * width]
        for piece in range(reduce_ref.shape[1] // share):
            f_ref[1 + wide + piece] = reduce_ref[0, piece * share : (piece + 1) * share, :]

    for layer in range(LAYERS):
        pl.when(pl.program_id(0) == layer)(
            functools.partial(fill, outs[2 * layer], outs[2 * layer + 1])
        )


def pick_quarters(me, project, mixer, expand, reduce, small):
    share, width = mixer.shape[1] // 4, mixer.shape[2]
    far = 1 + expand.shape[2] // width + reduce.shape[1] // 4 // share

    def quarter_spec(array):
        return pl.BlockSpec(
            (1, array.shape[1] // 4, array.shape[2]),
            lambda i, me: (i, me[0] * GRP_CORE + me[1], 0),
        )

    shapes = [(4, share, width), (far, share, width)] * LAYERS
    return pl.pallas_call(
        pick_kernel,
        out_shape=[jax.ShapeDtypeStruct(shape, jnp.bfloat16) for shape in shapes],
        grid_spec=pltpu.PrefetchScalarGridSpec(
            num_scalar_prefetch=1,
            grid=(LAYERS,),
            in_specs=[quarter_spec(array) for array in (project, mixer, expand, reduce)]
            + [pl.BlockSpec(small.shape, lambda i, me: (0, 0))],
            out_specs=[pl.BlockSpec(shape, lambda i, me: (0, 0, 0)) for shape in shapes],
        ),
        name="pick_quarters",
    )(me, project, mixer, expand, reduce, small)


def pack_kernel(kinds, *refs):
    ins, out_ref = refs[:-1], refs[-1]
    width = out_ref.shape[-1]
    share = out_ref.shape[3]
    place = 0
    for kind, ref in zip(kinds, ins):
        if kind == "columns":
            for column in range(ref.shape[-1] // width):
                out_ref[0, :, place] = ref[:, 0, :, column * width : (column + 1) * width]
                place += 1
        else:
            for piece in range(ref.shape[2] // share):
                out_ref[0, :, place] = ref[:, 0, piece * share : (piece + 1) * share, :]
                place += 1


def pack_terms(terms, kinds, share, width):
    places = sum(t.size for t in terms) // (32 * share * width)
    views = [t.reshape(8, 4, -1, t.shape[1]) for t in terms]
    return pl.pallas_call(
        functools.partial(pack_kernel, kinds),
        out_shape=jax.ShapeDtypeStruct((4, 8, places, share, width), jnp.bfloat16),
        grid=(4,),
        in_specs=[pl.BlockSpec((8, 1) + view.shape[2:], lambda q: (0, q, 0, 0)) for view in views],
        out_specs=pl.BlockSpec((1, 8, places, share, width), lambda q: (q, 0, 0, 0, 0)),
        compiler_params=pltpu.CompilerParams(vmem_limit_bytes=32 * 2**20),
        cost_estimate=pl.CostEstimate(
            flops=0, bytes_accessed=4 * 32 * places * share * width, transcendentals=0
        ),
        name="pack_terms",
    )(*views)


def swap_y(values):
    return send(values, lambda y, core, z, x: (1 - y, core, z, x))


def swap_x(values):
    return send(values, lambda y, core, z, x: (y, core, z, 1 - x))


def swap_z(values, bit):
    return send(values, lambda y, core, z, x: (y, core, z ^ bit, x))


def halve_kernel(kinds, me, *refs):
    ins, keep_ref, away_ref = refs[: len(kinds)], refs[-2], refs[-1]
    width = keep_ref.shape[-1]
    share = keep_ref.shape[-2]

    def fill(out_ref):
        for x_bit in range(SHARD_X):
            for z_bits in range(SHARD_Z):
                shard = (z_bits ^ me[3]) * SHARD_X + (x_bit ^ me[2])
                place = 0
                for kind, ref in zip(kinds, ins):
                    if kind == "columns":
                        for column in range(ref.shape[-1] // width):
                            lanes = slice(column * width, (column + 1) * width)
                            out_ref[0, x_bit, z_bits, place] = ref[shard, 0, :, lanes]
                            place += 1
                    elif kind == "rows":
                        for piece in range(ref.shape[2] // share):
                            span = slice(piece * share, (piece + 1) * share)
                            out_ref[0, x_bit, z_bits, place] = ref[shard, 0, span, :]
                            place += 1
                    else:
                        out_ref[0, x_bit, z_bits, place] = jnp.zeros((share, width), jnp.bfloat16)
                        out_ref[0, x_bit, z_bits, place, 0:8, :] = ref[0, shard]
                        place += 1

    @pl.when(pl.program_id(0) == 0)
    def first():
        fill(keep_ref)

    @pl.when(pl.program_id(0) == 1)
    def second():
        fill(away_ref)


def halve_terms(me, terms, kinds, share, width):
    views, specs, places = [], [], 0

    def quarter_of(i, j, me):
        return (j ^ me[0]) * GRP_CORE + (i ^ me[1])

    for term, kind in zip(terms, kinds):
        if kind == "vector":
            views.append(term)
            specs.append(
                pl.BlockSpec((1,) + term.shape[1:], lambda i, j, me: (quarter_of(i, j, me), 0, 0, 0))
            )
            places += 1
        else:
            view = term.reshape(8, 4, -1, term.shape[1])
            views.append(view)
            specs.append(
                pl.BlockSpec(
                    (8, 1) + view.shape[2:], lambda i, j, me: (0, quarter_of(i, j, me), 0, 0)
                )
            )
            places += term.shape[0] * term.shape[1] // (32 * share * width)
    shape = (GRP_Y, SHARD_X, SHARD_Z, places, share, width)
    block = (1,) + shape[1:]
    return pl.pallas_call(
        functools.partial(halve_kernel, kinds),
        out_shape=[jax.ShapeDtypeStruct(shape, jnp.bfloat16)] * 2,
        grid_spec=pltpu.PrefetchScalarGridSpec(
            num_scalar_prefetch=1,
            grid=(2, 2),
            in_specs=specs,
            out_specs=[
                pl.BlockSpec(block, lambda i, j, me: (jnp.where(i == 0, j, 1), 0, 0, 0, 0, 0)),
                pl.BlockSpec(block, lambda i, j, me: (jnp.where(i == 0, 0, j), 0, 0, 0, 0, 0)),
            ],
        ),
        compiler_params=pltpu.CompilerParams(vmem_limit_bytes=40 * 2**20),
        cost_estimate=pl.CostEstimate(
            flops=0, bytes_accessed=128 * places * share * width, transcendentals=0
        ),
        name="halve_terms",
    )(me, *views)


def summed(one, other):
    return (one.astype(jnp.float32) + other.astype(jnp.float32)).astype(jnp.bfloat16)


def scatter_terms(me, terms, kinds, share, width, part):
    keep, away = halve_terms(me, terms, kinds, share, width)
    come = swap_core(away)
    a_keep, a_come = keep[:, :, :, :part], come[:, :, :, :part]
    b_keep, b_come = keep[:, :, :, part:], come[:, :, :, part:]
    a_next = swap_y(summed(a_keep[1], a_come[1]))
    b_next = swap_x(summed(b_keep[:, 1], b_come[:, 1]))
    a_keep = summed(a_keep[0], a_come[0])
    b_keep = summed(b_keep[:, 0], b_come[:, 0])
    a_last = swap_x(summed(a_keep[1], a_next[1]))
    b_last = swap_y(summed(b_keep[1], b_next[1]))
    a_keep = summed(a_keep[0], a_next[0])
    b_keep = summed(b_keep[0], b_next[0])
    whole = jnp.concatenate([a_keep, b_keep], axis=1)
    come = jnp.concatenate([a_last, b_last], axis=1)
    far = swap_z(summed(whole[2:], come[2:]), 2)
    whole = summed(whole[:2], come[:2])
    near = swap_z(summed(whole[1], far[1]), 1)
    return summed(summed(whole[0], far[0]), near)


def gather_quarters(piece):
    pair = jnp.stack([piece, swap_y(piece)])
    return jnp.stack([pair, swap_core(pair)])


def finish_kernel(me, *refs):
    layers = len(refs) - 5
    outs = refs[layers:]

    def fill(in_ref):
        width = in_ref.shape[-1]
        share = in_ref.shape[-2]
        place = 0
        for ref in outs[:3]:
            for column in range(ref.shape[-1] // width):
                ref[0, 0, :, column * width : (column + 1) * width] = in_ref[0, 0, place].astype(
                    jnp.float32
                )
                place += 1
        for piece in range(outs[3].shape[2] // share):
            outs[3][0, 0, piece * share : (piece + 1) * share, :] = in_ref[0, 0, place].astype(
                jnp.float32
            )
            place += 1
        outs[4][0, 0] = in_ref[0, 0, place, 0:8, :].astype(jnp.float32)

    for layer in range(layers):
        pl.when(pl.program_id(0) == layer)(functools.partial(fill, refs[layer]))


def finish_shares(me, shares, columns, deep):
    layers = len(shares)
    places, share, width = shares[0].shape[2:]
    shapes = [(share, n * width) for n in columns] + [(deep, width), (8, width)]
    block = (1, 1, places, share, width)

    def spec_of(layer):
        def place_of(i, j, me):
            k = jnp.where(i == layer, j, jnp.where(i < layer, 0, 3))
            return ((k % GRP_CORE) ^ me[1], (k // GRP_CORE) ^ me[0], 0, 0, 0)

        return pl.BlockSpec(block, place_of)

    outs = pl.pallas_call(
        finish_kernel,
        out_shape=[jax.ShapeDtypeStruct((layers, 4) + shape, jnp.float32) for shape in shapes],
        grid_spec=pltpu.PrefetchScalarGridSpec(
            num_scalar_prefetch=1,
            grid=(layers, 4),
            in_specs=[spec_of(layer) for layer in range(layers)],
            out_specs=[
                pl.BlockSpec((1, 1) + shape, lambda i, j, me: (i, j, 0, 0)) for shape in shapes
            ],
        ),
        name="finish_shares",
    )(me, *shares)
    return [out.reshape(layers, -1, out.shape[-1]) for out in outs[:4]] + [outs[4]]


def gather_all(local):
    places, share, width = local.shape
    gathered = lax.all_gather(local.reshape(-1, width), BOTH, axis=0, tiled=False)
    return gathered.reshape(4, 8, places, share, width)


def join_kernel(me, a_ref, a_far_ref, b_ref, b_far_ref, project_ref, small_ref):
    width = a_ref.shape[-1]
    for core_bit in range(2):
        one = a_far_ref if core_bit else a_ref
        two = b_far_ref if core_bit else b_ref
        for y_bit in range(GRP_Y):
            quarter = (y_bit ^ me[0]) * GRP_CORE + (core_bit ^ me[1])
            for x_bit in range(SHARD_X):
                for z_bits in range(SHARD_Z):
                    shard = (z_bits ^ me[3]) * SHARD_X + (x_bit ^ me[2])
                    for column in range(3):
                        lanes = slice(column * width, (column + 1) * width)
                        if column < 2:
                            piece = one[y_bit, x_bit, z_bits, column]
                        else:
                            piece = two[x_bit, y_bit, z_bits, 0]
                        project_ref[shard, quarter, :, lanes] = piece
                    if core_bit == 0 and y_bit == 0:
                        small_ref[shard] = two[x_bit, y_bit, z_bits, 1, 0:8, :]


def gather_first(me, local):
    share, width = local.shape[1:]
    pair = jnp.stack([local, swap_z(local, 1)])
    four = jnp.concatenate([pair, swap_z(pair, 2)])
    a_part, b_part = four[:, :2], four[:, 2:]
    a_two = jnp.stack([a_part, swap_x(a_part)])
    b_two = jnp.stack([b_part, swap_y(b_part)])
    a_four = jnp.stack([a_two, swap_y(a_two)])
    b_four = jnp.stack([b_two, swap_x(b_two)])
    project, small = pl.pallas_call(
        join_kernel,
        out_shape=[
            jax.ShapeDtypeStruct((8, 4, share, 3 * width), local.dtype),
            jax.ShapeDtypeStruct((8, 8, width), local.dtype),
        ],
        grid_spec=pltpu.PrefetchScalarGridSpec(
            num_scalar_prefetch=1,
            grid=(1,),
            in_specs=[whole_block(a_four.shape)] * 4,
            out_specs=[whole_block((8, 4, share, 3 * width)), whole_block((8, 8, width))],
        ),
        compiler_params=pltpu.CompilerParams(vmem_limit_bytes=24 * 2**20),
        name="join_projection",
    )(me, a_four, swap_core(a_four), b_four, swap_core(b_four))
    return project.reshape(-1, 3 * width), small


def on_device_turned(
    tokens,
    cotangent,
    seq_lengths,
    seq_order,
    w_project,
    w_mixer,
    w_expand,
    w_reduce,
    biases,
    norm_gains,
):
    row_count, width = tokens.shape
    shard_index = lax.axis_index("shard")
    quarter = lax.axis_index("grp")
    z, x = shard_index // SHARD_X, shard_index % SHARD_X
    y, core = quarter // GRP_CORE, quarter % GRP_CORE
    me = jnp.stack([y, core, x, z]).astype(jnp.int32)
    hidden_units = w_expand.shape[2]
    group_slots = row_count * 8
    seq_count = seq_lengths.shape[1]
    seq_ends = group_ends(seq_lengths, seq_order, y * GRP_CORE + x)
    block_index = z * GRP_CORE + core
    slot_index = block_index * row_count + jnp.arange(row_count, dtype=jnp.int32)
    before_slot = seq_ends[None, :] <= slot_index[:, None]
    own_segment = jnp.sum(before_slot.astype(jnp.int32), axis=1, dtype=jnp.int32)
    starts = jnp.max(jnp.where(before_slot, seq_ends[None, :], 0), axis=1)
    stops = jnp.min(jnp.where(before_slot, group_slots, seq_ends[None, :]), axis=1)
    window_begin = (block_index - 2) * row_count
    low = starts - window_begin
    high = stops - window_begin
    low_line = jnp.broadcast_to(low[None, :], (8, row_count))
    high_line = jnp.broadcast_to(high[None, :], (8, row_count))
    bounds = jnp.stack([low[0], high[row_count - 1]])
    valid_rows = (own_segment < seq_count).astype(jnp.float32)[:, None]

    small = jnp.concatenate(
        [jnp.concatenate([biases[i], norm_gains[i]]) for i in range(LAYERS)]
    ).reshape(-1, width)
    share = w_project.shape[1] // 4
    deep = w_reduce.shape[1] // 4
    bias_count = biases.shape[1]
    small_rows = small.shape[0]
    small = jnp.concatenate([small, jnp.zeros((8 - small_rows, width), small.dtype)])
    near_first, far_first, near_last, far_last = pick_quarters(
        me, w_project, w_mixer, w_expand, w_reduce, small
    )
    state_low = turn_rows(tokens)
    state_grad = turn_rows(cotangent)
    columns = (3, 1, hidden_units // width)
    project_first, small_all = gather_first(me, near_first)
    far_kinds = ("columns", "columns", "rows")
    far_shapes = [(share, width), (share, hidden_units), (deep, width)]
    far_pieces = gather_all(far_first)
    last_pieces = gather_all(jnp.concatenate([near_last[:3], far_last]))
    first_whole = [project_first] + unpack_weights_of(far_pieces, far_kinds, far_shapes)
    last_whole = unpack_weights_of(
        last_pieces, ("columns",) + far_kinds, [(share, 3 * width)] + far_shapes
    )
    small_all = small_all[:, :small_rows].reshape(8, LAYERS, -1)
    weights = []
    for layer_index, whole in enumerate([first_whole, last_whole]):
        bias_vec = small_all[:, layer_index, :bias_count].reshape(-1)
        gain_vec = small_all[:, layer_index, bias_count:].reshape(-1)
        weights.append(unpack_weights(whole + [bias_vec, gain_vec], width, hidden_units))

    hidden_state = state_low.astype(jnp.float32)
    kept_list = []
    for layer_index in range(LAYERS):
        project, mixing, expand, shrink, bias_list, gain_one, gain_two = weights[layer_index]
        bias_q, bias_v, bias_mix, shift_one, bias_in, bias_out, shift_two = bias_list
        state_window = window_of(state_low, core)
        queries = (
            jnp.dot(state_low, project[:, :width], preferred_element_type=jnp.float32) + bias_q
        ).astype(jnp.bfloat16)
        key_value = (
            jnp.dot(state_window, project[:, width:], preferred_element_type=jnp.float32)
            + jnp.concatenate([jnp.zeros_like(bias_v), bias_v])
        ).astype(jnp.bfloat16)
        mixed_low, lse = flash_forward(bounds, queries, key_value, low_line, high_line)
        branch = jnp.dot(mixed_low, mixing, preferred_element_type=jnp.float32) + bias_mix
        summed_one = hidden_state + branch
        normed_one = layer_norm(summed_one, gain_one, shift_one)
        normed_low = normed_one.astype(jnp.bfloat16)
        before = jnp.dot(normed_low, expand, preferred_element_type=jnp.float32) + bias_in
        active_low = gelu_exact(before).astype(jnp.bfloat16)
        feed_out = jnp.dot(active_low, shrink, preferred_element_type=jnp.float32) + bias_out
        summed_two = normed_one + feed_out
        hidden_state = layer_norm(summed_two, gain_two, shift_two)
        kept_list.append(
            (
                state_low,
                state_window,
                queries,
                key_value,
                lse,
                mixed_low,
                summed_one,
                normed_low,
                before,
                active_low,
                summed_two,
            )
        )
        state_low = hidden_state.astype(jnp.bfloat16)
    activations = turn_rows((hidden_state * valid_rows).astype(jnp.bfloat16))
    state_grad = state_grad.astype(jnp.float32) * valid_rows
    results = [None] * LAYERS
    for layer_index in reversed(range(LAYERS)):
        (
            layer_low,
            state_window,
            queries,
            key_value,
            lse,
            mixed_low,
            summed_one,
            normed_low,
            before,
            active_low,
            summed_two,
        ) = kept_list[layer_index]
        project, mixing, expand, shrink, bias_list, gain_one, gain_two = weights[layer_index]
        bias_q, bias_v, bias_mix, shift_one, bias_in, bias_out, shift_two = bias_list
        unused_two, norm_pull = jax.vjp(layer_norm, summed_two, gain_two, shift_two)
        sum_two_grad, gain_two_grad, shift_two_grad = norm_pull(state_grad)
        feed_low = sum_two_grad.astype(jnp.bfloat16)
        shrink_grad = jnp.einsum(
            "tf,td->fd", active_low, feed_low, preferred_element_type=jnp.float32
        )
        bias_out_grad = jnp.sum(feed_low, axis=0, dtype=jnp.float32)
        active_grad = jnp.einsum("td,fd->tf", feed_low, shrink, preferred_element_type=jnp.float32)
        unused_gelu, gelu_pull = jax.vjp(gelu_exact, before)
        before_low = gelu_pull(active_grad)[0].astype(jnp.bfloat16)
        expand_grad = jnp.einsum(
            "td,tf->df", normed_low, before_low, preferred_element_type=jnp.float32
        )
        bias_in_grad = jnp.sum(before_low, axis=0, dtype=jnp.float32)
        normed_grad = sum_two_grad + jnp.einsum(
            "tf,df->td", before_low, expand, preferred_element_type=jnp.float32
        )
        unused_one, first_pull = jax.vjp(layer_norm, summed_one, gain_one, shift_one)
        sum_one_grad, gain_one_grad, shift_one_grad = first_pull(normed_grad)
        branch_low = sum_one_grad.astype(jnp.bfloat16)
        mixing_grad = jnp.einsum(
            "td,te->de", mixed_low, branch_low, preferred_element_type=jnp.float32
        )
        bias_mix_grad = jnp.sum(branch_low, axis=0, dtype=jnp.float32)
        mixed_grad_low = jnp.einsum(
            "te,de->td", branch_low, mixing, preferred_element_type=jnp.float32
        ).astype(jnp.bfloat16)
        query_grad, key_value_grad = flash_backward(
            bounds, queries, key_value, mixed_grad_low, lse, low_line, high_line
        )
        query_term = jnp.einsum(
            "td,te->de", layer_low, query_grad, preferred_element_type=jnp.float32
        )
        key_value_term = jnp.einsum(
            "td,te->de", state_window, key_value_grad, preferred_element_type=jnp.float32
        )
        bias_q_grad = jnp.sum(query_grad, axis=0, dtype=jnp.float32)
        bias_v_grad = jnp.sum(key_value_grad[:, width:], axis=0, dtype=jnp.float32)
        window_grad = jnp.einsum(
            "te,de->td", key_value_grad, project[:, width:], preferred_element_type=jnp.float32
        )
        state_grad = (
            sum_one_grad
            + jnp.einsum(
                "te,de->td", query_grad, project[:, :width], preferred_element_type=jnp.float32
            )
            + window_back(window_grad, core, row_count)
        )
        vectors = jnp.concatenate(
            [
                bias_q_grad,
                bias_v_grad,
                bias_mix_grad,
                shift_one_grad,
                bias_in_grad,
                bias_out_grad,
                shift_two_grad,
            ]
        ).reshape(8, -1)
        gains = jnp.concatenate([gain_one_grad, gain_two_grad]).reshape(8, -1)
        vectors = jnp.concatenate([vectors, gains], axis=1).astype(jnp.bfloat16)
        vectors = vectors.reshape(8, 4, -1).transpose(1, 0, 2)
        vectors = jnp.pad(vectors, ((0, 0), (0, 0), (0, width - vectors.shape[2])))
        vectors = jnp.broadcast_to(vectors[:, :, None], (4, 8, 8, width))
        terms = [t.astype(jnp.bfloat16) for t in (mixing_grad, expand_grad, shrink_grad)]
        pieces = pack_terms(terms, far_kinds, share, width)
        fed = lax.psum_scatter(
            pieces.reshape(32, -1, width), BOTH, scatter_dimension=0, tiled=True
        ).reshape(-1, share, width)
        attended = scatter_terms(
            me,
            [query_term.astype(jnp.bfloat16), key_value_term.astype(jnp.bfloat16), vectors],
            ("columns", "columns", "vector"),
            share,
            width,
            2,
        )
        results[layer_index] = jnp.concatenate([attended[:3], fed, attended[3:]])
    outs = finish_shares(me, [gather_quarters(result) for result in results], columns, deep)
    quarter_len = (bias_count + norm_gains.shape[1]) // 4
    vectors = outs[4][:, :, 0, :quarter_len].reshape(LAYERS, -1)
    input_grad = turn_rows(state_grad.astype(jnp.bfloat16)).astype(jnp.float32)
    return (
        activations,
        input_grad,
        outs[0],
        outs[1],
        outs[2],
        outs[3],
        vectors[:, :bias_count],
        vectors[:, bias_count:],
    )


def solution(mesh):
    in_specs = (
        P(("grp", "shard"), None),
        P(("grp", "shard"), None),
        P(),
        P(),
        P(None, "shard", None),
        P(None, "shard", None),
        P(None, "shard", None),
        P(None, "shard", None),
        P(None, "shard"),
        P(None, "shard"),
    )
    out_specs = (
        P(("grp", "shard"), None),
        P(("grp", "shard"), None),
        P(None, "shard", None),
        P(None, "shard", None),
        P(None, "shard", None),
        P(None, "shard", None),
        P(None, "shard"),
        P(None, "shard"),
    )
    body = on_device_turned if mesh.shape["shard"] == 8 and mesh.shape["grp"] == 4 else on_device
    return jax.shard_map(
        body, mesh=mesh, in_specs=in_specs, out_specs=out_specs, check_vma=False
    )
```

```python
import functools

import jax
import jax.numpy as jnp
from jax import lax
from jax.experimental import pallas as pl
from jax.experimental.pallas import tpu as pltpu
from jax.sharding import PartitionSpec as P

HEADS = 12
LAYERS = 2
SEQ_MAX = 2048


EPSILON = 1e-12
NEGATIVE = -1e30


def passed_along(shard, axis, by):
    size = lax.axis_size(axis)
    pairs = [(i, i + by) for i in range(size) if 0 <= i + by < size]
    return lax.ppermute(shard, axis, pairs)


def layer_norm(values, gain, shift):
    middle = jnp.mean(values, axis=-1, keepdims=True)
    centered = values - middle
    spread = jnp.mean(centered * centered, axis=-1, keepdims=True)
    return centered * lax.rsqrt(spread + EPSILON) * gain + shift


def gelu_exact(values):
    return jax.nn.gelu(values, approximate=False)


def keep_same(carried):
    return carried


def group_ends(seq_lengths, seq_order, group_index):
    lengths_row = lax.dynamic_index_in_dim(seq_lengths, group_index, 0, keepdims=False)
    order_row = lax.dynamic_index_in_dim(seq_order, group_index, 0, keepdims=False)
    places = jnp.arange(lengths_row.shape[0], dtype=jnp.int32)
    picked = order_row[:, None] == places[None, :]
    placed = jnp.sum(jnp.where(picked, lengths_row[None, :], 0), axis=1, dtype=jnp.int32)
    return jnp.cumsum(placed, dtype=jnp.int32)


def slot_segments(slot_index, seq_ends):
    flattened = slot_index.reshape(-1)
    counted = jnp.sum(
        (seq_ends[None, :] <= flattened[:, None]).astype(jnp.int32), axis=1, dtype=jnp.int32
    )
    return counted.reshape(slot_index.shape)


def unpack_weights(weights, width, hidden_units):
    bias_vec = weights[4].astype(jnp.float32)
    gain_vec = weights[5].astype(jnp.float32)
    piece_lens = [width, width, width, width, hidden_units, width, width]
    bias_list = []
    begin_at = 0
    for piece_len in piece_lens:
        bias_list.append(bias_vec[begin_at : begin_at + piece_len])
        begin_at = begin_at + piece_len
    return (
        weights[0],
        weights[1],
        weights[2],
        weights[3],
        bias_list,
        gain_vec[:width],
        gain_vec[width:],
    )


def block_probs(queries, keys_block, seg_block, own_segment, log_total, score_scale):
    raw_scores = jnp.einsum("qhd,khd->hqk", queries, keys_block, preferred_element_type=jnp.float32)
    allowed = (own_segment[:, None] == seg_block[None, :])[None]
    return jnp.where(allowed, jnp.exp(raw_scores * score_scale - log_total[:, :, None]), 0.0)


def gather_window(key_rows, value_rows, reach_blocks):
    key_list = []
    value_list = []
    for step_offset in range(-reach_blocks, reach_blocks + 1):
        if step_offset == 0:
            moved = (key_rows, value_rows)
        else:
            moved = passed_along((key_rows, value_rows), "shard", -step_offset)
        key_list.append(moved[0])
        value_list.append(moved[1])
    return (jnp.stack(key_list), jnp.stack(value_list))


def return_parts(key_parts, value_parts, reach_blocks):
    key_total = key_parts[reach_blocks]
    value_total = value_parts[reach_blocks]
    for step_offset in range(-reach_blocks, reach_blocks + 1):
        if step_offset != 0:
            arrived = (
                passed_along(
                    key_parts[step_offset + reach_blocks].astype(jnp.bfloat16), "shard", step_offset
                ).astype(jnp.float32),
                passed_along(
                    value_parts[step_offset + reach_blocks].astype(jnp.bfloat16),
                    "shard",
                    step_offset,
                ).astype(jnp.float32),
            )
            key_total = key_total + arrived[0]
            value_total = value_total + arrived[1]
    return (key_total, value_total)


def attend_forward(
    queries, window_keys, window_values, window_segment, live_block, own_segment, score_scale
):
    row_count, head_count, head_dim = queries.shape

    def stats_step(carry, items):
        keys_block, seg_block, alive = items

        def stats_compute(state_pair):
            running_top, running_sum = state_pair
            allowed = (own_segment[:, None] == seg_block[None, :])[None]
            raw_scores = jnp.einsum(
                "qhd,khd->hqk", queries, keys_block, preferred_element_type=jnp.float32
            )
            scores = jnp.where(allowed, raw_scores * score_scale, NEGATIVE)
            new_top = jnp.maximum(running_top, jnp.max(scores, axis=-1))
            weighted = jnp.where(allowed, jnp.exp(scores - new_top[:, :, None]), 0.0)
            return (
                new_top,
                running_sum * jnp.exp(running_top - new_top) + jnp.sum(weighted, axis=-1),
            )

        return (lax.cond(alive, stats_compute, keep_same, carry), None)

    begin_stats = (
        jnp.full((head_count, row_count), NEGATIVE, jnp.float32),
        jnp.zeros((head_count, row_count), jnp.float32),
    )
    (running_top, running_sum), unused = lax.scan(
        stats_step, begin_stats, (window_keys, window_segment, live_block)
    )
    log_total = running_top + jnp.log(running_sum)

    def mix_step(carry, items):
        keys_block, values_block, seg_block, alive = items

        def mix_compute(state_pair):
            mixed, extra = state_pair
            probs = block_probs(queries, keys_block, seg_block, own_segment, log_total, score_scale)
            probs_low = probs.astype(jnp.bfloat16)
            rest_low = (probs - lax.optimization_barrier(probs_low).astype(jnp.float32)).astype(
                jnp.bfloat16
            )
            mixed = mixed + jnp.einsum(
                "hqk,khd->qhd", probs_low, values_block, preferred_element_type=jnp.float32
            )
            extra = extra + jnp.einsum(
                "hqk,khd->qhd", rest_low, values_block, preferred_element_type=jnp.float32
            )
            return (mixed, extra)

        return (lax.cond(alive, mix_compute, keep_same, carry), None)

    zeros_mix = jnp.zeros((row_count, head_count, head_dim), jnp.float32)
    (mixed, extra), unused = lax.scan(
        mix_step, (zeros_mix, zeros_mix), (window_keys, window_values, window_segment, live_block)
    )
    return (log_total, mixed, mixed + extra)


def attend_backward(
    queries,
    window_keys,
    window_values,
    window_segment,
    live_block,
    own_segment,
    log_total,
    delta,
    grad_low,
    score_scale,
):

    def grad_step(query_grad, items):
        keys_block, values_block, seg_block, alive = items

        def grad_compute(carried):
            probs = block_probs(queries, keys_block, seg_block, own_segment, log_total, score_scale)
            prob_grad = jnp.einsum(
                "qhd,khd->hqk", grad_low, values_block, preferred_element_type=jnp.float32
            )
            score_low = (probs * (prob_grad - delta[:, :, None])).astype(jnp.bfloat16)
            carried = carried + jnp.einsum(
                "hqk,khd->qhd", score_low, keys_block, preferred_element_type=jnp.float32
            )
            probs_low = probs.astype(jnp.bfloat16)
            value_part = jnp.einsum(
                "hqk,qhd->khd", probs_low, grad_low, preferred_element_type=jnp.float32
            )
            key_part = jnp.einsum(
                "hqk,qhd->khd", score_low, queries, preferred_element_type=jnp.float32
            )
            return (carried, (key_part, value_part))

        def skipped(carried):
            nothing = jnp.zeros(keys_block.shape, jnp.float32)
            return (carried, (nothing, nothing))

        return lax.cond(alive, grad_compute, skipped, query_grad)

    zero_grad = jnp.zeros(queries.shape, jnp.float32)
    query_grad, key_value = lax.scan(
        grad_step, zero_grad, (window_keys, window_values, window_segment, live_block)
    )
    return (query_grad, key_value)


def on_device(
    tokens,
    cotangent,
    seq_lengths,
    seq_order,
    w_project,
    w_mixer,
    w_expand,
    w_reduce,
    biases,
    norm_gains,
):
    row_count, width = tokens.shape
    shard_count = lax.axis_size("shard")
    shard_index = lax.axis_index("shard")
    group_index = lax.axis_index("grp")
    head_dim = width // HEADS
    hidden_units = w_expand.shape[2]
    score_scale = head_dim ** (-0.5)
    longest = min(SEQ_MAX, row_count * shard_count // 4)
    reach_blocks = longest // row_count
    seq_count = seq_lengths.shape[1]
    seq_ends = group_ends(seq_lengths, seq_order, group_index)
    neighbour = shard_index + jnp.arange(-reach_blocks, reach_blocks + 1, dtype=jnp.int32)
    slot_index = neighbour[:, None] * row_count + jnp.arange(row_count, dtype=jnp.int32)[None, :]
    window_segment = slot_segments(slot_index, seq_ends)
    own_segment = window_segment[reach_blocks]
    inside = (neighbour >= 0) & (neighbour < shard_count)
    live_block = (
        inside
        & (window_segment[:, 0] <= own_segment[row_count - 1])
        & (window_segment[:, row_count - 1] >= own_segment[0])
    )
    valid_rows = (own_segment < seq_count).astype(jnp.float32)[:, None]
    hidden_state = tokens.astype(jnp.float32)
    state_low = tokens
    kept_list = []
    for layer_index in range(LAYERS):
        weights = (
            lax.all_gather(w_project[layer_index], "shard", axis=0, tiled=True),
            lax.all_gather(w_mixer[layer_index], "shard", axis=0, tiled=True),
            lax.all_gather(w_expand[layer_index], "shard", axis=0, tiled=True),
            lax.all_gather(w_reduce[layer_index], "shard", axis=0, tiled=True),
            lax.all_gather(biases[layer_index], "shard", axis=0, tiled=True),
            lax.all_gather(norm_gains[layer_index], "shard", axis=0, tiled=True),
        )
        project, mixing, expand, shrink, bias_list, gain_one, gain_two = unpack_weights(
            weights, width, hidden_units
        )
        bias_q, bias_v, bias_mix, shift_one, bias_in, bias_out, shift_two = bias_list
        projected = jnp.dot(state_low, project, preferred_element_type=jnp.float32)
        projected = projected + jnp.concatenate([bias_q, jnp.zeros_like(bias_q), bias_v])
        projected_low = projected.astype(jnp.bfloat16)
        queries = projected_low[:, :width].reshape(row_count, HEADS, head_dim)
        key_rows = projected_low[:, width : 2 * width].reshape(row_count, HEADS, head_dim)
        value_rows = projected_low[:, 2 * width :].reshape(row_count, HEADS, head_dim)
        window_keys, window_values = gather_window(key_rows, value_rows, reach_blocks)
        log_total, mixed, full_mix = attend_forward(
            queries,
            window_keys,
            window_values,
            window_segment,
            live_block,
            own_segment,
            score_scale,
        )
        mixed_low = mixed.reshape(row_count, width).astype(jnp.bfloat16)
        branch = jnp.dot(mixed_low, mixing, preferred_element_type=jnp.float32) + bias_mix
        summed_one = hidden_state + branch
        normed_one = layer_norm(summed_one, gain_one, shift_one)
        normed_low = normed_one.astype(jnp.bfloat16)
        before = jnp.dot(normed_low, expand, preferred_element_type=jnp.float32) + bias_in
        active_low = gelu_exact(before).astype(jnp.bfloat16)
        feed_out = jnp.dot(active_low, shrink, preferred_element_type=jnp.float32) + bias_out
        summed_two = normed_one + feed_out
        hidden_state = layer_norm(summed_two, gain_two, shift_two)
        kept_list.append(
            (
                state_low,
                queries,
                key_rows,
                value_rows,
                window_keys,
                window_values,
                log_total,
                full_mix,
                mixed_low,
                summed_one,
                normed_low,
                before,
                active_low,
                summed_two,
                weights,
            )
        )
        state_low = hidden_state.astype(jnp.bfloat16)
    activations = (hidden_state * valid_rows).astype(jnp.bfloat16)
    state_grad = cotangent.astype(jnp.float32) * valid_rows
    results = [None] * LAYERS
    for layer_index in reversed(range(LAYERS)):
        (
            layer_low,
            queries,
            key_rows,
            value_rows,
            window_keys,
            window_values,
            log_total,
            full_mix,
            mixed_low,
            summed_one,
            normed_low,
            before,
            active_low,
            summed_two,
            kept_weights,
        ) = kept_list[layer_index]
        weights = (
            lax.all_gather(w_project[layer_index], "shard", axis=0, tiled=True),
            lax.all_gather(w_mixer[layer_index], "shard", axis=0, tiled=True),
            lax.all_gather(w_expand[layer_index], "shard", axis=0, tiled=True),
            lax.all_gather(w_reduce[layer_index], "shard", axis=0, tiled=True),
            lax.all_gather(biases[layer_index], "shard", axis=0, tiled=True),
            lax.all_gather(norm_gains[layer_index], "shard", axis=0, tiled=True),
        )
        project, mixing, expand, shrink, bias_list, gain_one, gain_two = unpack_weights(
            weights, width, hidden_units
        )
        bias_q, bias_v, bias_mix, shift_one, bias_in, bias_out, shift_two = bias_list
        unused_two, norm_pull = jax.vjp(layer_norm, summed_two, gain_two, shift_two)
        sum_two_grad, gain_two_grad, shift_two_grad = norm_pull(state_grad)
        feed_low = sum_two_grad.astype(jnp.bfloat16)
        shrink_grad = jnp.einsum(
            "tf,td->fd", active_low, feed_low, preferred_element_type=jnp.float32
        )
        bias_out_grad = jnp.sum(feed_low, axis=0, dtype=jnp.float32)
        active_grad = jnp.einsum("td,fd->tf", feed_low, shrink, preferred_element_type=jnp.float32)
        unused_gelu, gelu_pull = jax.vjp(gelu_exact, before)
        before_low = gelu_pull(active_grad)[0].astype(jnp.bfloat16)
        expand_grad = jnp.einsum(
            "td,tf->df", normed_low, before_low, preferred_element_type=jnp.float32
        )
        bias_in_grad = jnp.sum(before_low, axis=0, dtype=jnp.float32)
        normed_grad = sum_two_grad + jnp.einsum(
            "tf,df->td", before_low, expand, preferred_element_type=jnp.float32
        )
        unused_one, first_pull = jax.vjp(layer_norm, summed_one, gain_one, shift_one)
        sum_one_grad, gain_one_grad, shift_one_grad = first_pull(normed_grad)
        branch_low = sum_one_grad.astype(jnp.bfloat16)
        mixing_grad = jnp.einsum(
            "td,te->de", mixed_low, branch_low, preferred_element_type=jnp.float32
        )
        bias_mix_grad = jnp.sum(branch_low, axis=0, dtype=jnp.float32)
        mixed_grad = jnp.einsum("te,de->td", branch_low, mixing, preferred_element_type=jnp.float32)
        mixed_grad_low = mixed_grad.astype(jnp.bfloat16).reshape(row_count, HEADS, head_dim)
        delta = jnp.sum(mixed_grad_low.astype(jnp.float32) * full_mix, axis=-1).T
        query_grad, key_value = attend_backward(
            queries,
            window_keys,
            window_values,
            window_segment,
            live_block,
            own_segment,
            log_total,
            delta,
            mixed_grad_low,
            score_scale,
        )
        key_total, value_total = return_parts(key_value[0], key_value[1], reach_blocks)
        projected_grad = jnp.concatenate(
            [
                (query_grad * score_scale).reshape(row_count, width),
                (key_total * score_scale).reshape(row_count, width),
                value_total.reshape(row_count, width),
            ],
            axis=1,
        )
        projected_low = projected_grad.astype(jnp.bfloat16)
        project_grad = jnp.einsum(
            "td,te->de", layer_low, projected_low, preferred_element_type=jnp.float32
        )
        bias_q_grad = jnp.sum(projected_low[:, :width], axis=0, dtype=jnp.float32)
        bias_v_grad = jnp.sum(projected_low[:, 2 * width :], axis=0, dtype=jnp.float32)
        state_grad = sum_one_grad + jnp.einsum(
            "te,de->td", projected_low, project, preferred_element_type=jnp.float32
        )
        bias_all = jnp.concatenate(
            [
                bias_q_grad,
                bias_v_grad,
                bias_mix_grad,
                shift_one_grad,
                bias_in_grad,
                bias_out_grad,
                shift_two_grad,
            ]
        )
        gain_all = jnp.concatenate([gain_one_grad, gain_two_grad])
        shares = (
            lax.psum_scatter(
                project_grad.astype(jnp.bfloat16), "shard", scatter_dimension=0, tiled=True
            ).astype(jnp.float32),
            lax.psum_scatter(
                mixing_grad.astype(jnp.bfloat16), "shard", scatter_dimension=0, tiled=True
            ).astype(jnp.float32),
            lax.psum_scatter(
                expand_grad.astype(jnp.bfloat16), "shard", scatter_dimension=0, tiled=True
            ).astype(jnp.float32),
            lax.psum_scatter(
                shrink_grad.astype(jnp.bfloat16), "shard", scatter_dimension=0, tiled=True
            ).astype(jnp.float32),
            lax.psum_scatter(
                bias_all.astype(jnp.bfloat16), "shard", scatter_dimension=0, tiled=True
            ).astype(jnp.float32),
            lax.psum_scatter(
                gain_all.astype(jnp.bfloat16), "shard", scatter_dimension=0, tiled=True
            ).astype(jnp.float32),
        )
        shares = (
            lax.psum(shares[0].astype(jnp.bfloat16), "grp").astype(jnp.float32),
            lax.psum(shares[1].astype(jnp.bfloat16), "grp").astype(jnp.float32),
            lax.psum(shares[2].astype(jnp.bfloat16), "grp").astype(jnp.float32),
            lax.psum(shares[3].astype(jnp.bfloat16), "grp").astype(jnp.float32),
            lax.psum(shares[4].astype(jnp.bfloat16), "grp").astype(jnp.float32),
            lax.psum(shares[5].astype(jnp.bfloat16), "grp").astype(jnp.float32),
        )
        results[layer_index] = shares
    stacked = [jnp.stack([layer_share[member] for layer_share in results]) for member in range(6)]
    return (
        activations,
        state_grad,
        stacked[0],
        stacked[1],
        stacked[2],
        stacked[3],
        stacked[4],
        stacked[5],
    )


HEAD_SCALE = 0.125


def fold_rows(values, combine):
    total = values[:8]
    for begin_at in range(8, values.shape[0], 8):
        total = combine(total, values[begin_at : begin_at + 8])
    return total


def halves_of(block):
    lane = lax.broadcasted_iota(jnp.int32, block.shape, 1)
    nothing = jnp.zeros_like(block)
    return (jnp.where(lane < 64, block, nothing), jnp.where(lane < 64, nothing, block))


def turned_dot(keys, queries):
    return lax.dot_general(
        keys, queries, (((1,), (1,)), ((), ())), preferred_element_type=jnp.float32
    )


def across_dot(weight, values):
    return lax.dot_general(
        weight, values, (((0,), (0,)), ((), ())), preferred_element_type=jnp.float32
    )


KEY_ROWS = 512
KEY_TILES = 5


def key_rows(tile):
    return pl.ds(pl.multiple_of(tile * KEY_ROWS, KEY_ROWS), KEY_ROWS)


def fill_mask(first, last, low, high, mask_scr, index):
    def mask_step(key_tile, carry):
        shape = (KEY_ROWS, low.shape[1])
        place = lax.broadcasted_iota(jnp.int32, shape, 0) + key_tile * KEY_ROWS
        allowed = (place >= low) & (place < high)
        mask_scr[index, key_rows(key_tile - first), :] = jnp.where(allowed, 0.0, NEGATIVE)
        return carry

    lax.fori_loop(first, last, mask_step, 0)


def flash_forward_kernel(
    bounds,
    a_ref,
    b_ref,
    kv_ref,
    low_ref,
    high_ref,
    a_mix,
    b_mix,
    a_wide,
    b_wide,
    lse_ref,
    mask_scr,
    score_scr,
):
    rows, width = a_ref.shape
    pairs = width // 128
    for index in range(2):
        span = slice(index * rows, (index + 1) * rows)
        fill_mask(
            bounds[2 * index],
            bounds[2 * index + 1],
            low_ref[0:1, span],
            high_ref[0:1, span],
            mask_scr,
            index,
        )

    def pair_step(pair, unused):
        lanes = pl.ds(pl.multiple_of(pair * 128, 128), 128)
        value_lanes = pl.ds(pl.multiple_of(pair * 128 + width, 128), 128)
        for index, (q_ref, mix_ref, wide_ref) in enumerate(
            ((a_ref, a_mix, a_wide), (b_ref, b_mix, b_wide))
        ):
            first, last = bounds[2 * index], bounds[2 * index + 1]
            heads = halves_of(q_ref[:, lanes] * jnp.bfloat16(HEAD_SCALE))

            def score_step(key_tile, tops, index=index, heads=heads, first=first):
                keys = kv_ref[key_rows(bounds[4 + key_tile]), lanes]
                place = key_rows(key_tile - first)
                mask = mask_scr[index, place, :]
                out = []
                for head in range(2):
                    scores = turned_dot(keys, heads[head]) + mask
                    score_scr[head, place, :] = scores
                    out.append(jnp.maximum(tops[head], fold_rows(scores, jnp.maximum)))
                return tuple(out)

            floor = jnp.full((8, rows), NEGATIVE, jnp.float32)
            tops = lax.fori_loop(first, last, score_step, (floor, floor))
            tops = [jnp.max(top, axis=0, keepdims=True) for top in tops]

            def mix_step(key_tile, carry, tops=tops, first=first):
                values = kv_ref[key_rows(bounds[4 + key_tile]), value_lanes].T
                totals, mixed = [], []
                for head in range(2):
                    weight = jnp.exp(score_scr[head, key_rows(key_tile - first), :] - tops[head])
                    totals.append(carry[head] + fold_rows(weight, jnp.add))
                    mixed.append(
                        carry[2 + head]
                        + jnp.dot(
                            values[head * 64 : (head + 1) * 64],
                            weight.astype(jnp.bfloat16),
                            preferred_element_type=jnp.float32,
                        )
                    )
                return (totals[0], totals[1], mixed[0], mixed[1])

            zero = jnp.zeros((8, rows), jnp.float32)
            nothing = jnp.zeros((64, rows), jnp.float32)
            carry = lax.fori_loop(first, last, mix_step, (zero, zero, nothing, nothing))
            totals = [jnp.sum(total, axis=0, keepdims=True) for total in carry[:2]]
            mixed = jnp.concatenate(
                [carry[2] * (1.0 / totals[0]), carry[3] * (1.0 / totals[1])], axis=0
            ).T
            wide_ref[:, lanes] = mixed
            mix_ref[:, lanes] = mixed.astype(jnp.bfloat16)
            lse_rows = [tops[head] + jnp.log(totals[head]) for head in range(2)]
            lse_ref[
                pl.ds(pl.multiple_of(pair * 8, 8), 8), index * rows : (index + 1) * rows
            ] = jnp.concatenate([jnp.broadcast_to(line, (4, rows)) for line in lse_rows])
        return unused

    lax.fori_loop(0, pairs, pair_step, 0)


def flash_backward_kernel(
    bounds,
    a_ref,
    b_ref,
    kv_ref,
    a_grad_ref,
    b_grad_ref,
    a_wide,
    b_wide,
    lse_ref,
    low_ref,
    high_ref,
    a_out,
    b_out,
    kv_out,
    mask_scr,
    k_acc,
    v_acc,
):
    rows, width = a_ref.shape
    pairs = width // 128
    tiles = kv_ref.shape[0] // KEY_ROWS
    for index in range(2):
        span = slice(index * rows, (index + 1) * rows)
        fill_mask(
            bounds[2 * index],
            bounds[2 * index + 1],
            low_ref[0:1, span],
            high_ref[0:1, span],
            mask_scr,
            index,
        )

    def pair_step(pair, unused):
        lanes = pl.ds(pl.multiple_of(pair * 128, 128), 128)
        value_lanes = pl.ds(pl.multiple_of(pair * 128 + width, 128), 128)
        lse_rows = lse_ref[pl.ds(pl.multiple_of(pair * 8, 8), 8), :]
        k_acc[...] = jnp.zeros_like(k_acc)
        v_acc[...] = jnp.zeros_like(v_acc)
        ways = (((1,), (1,)), ((), ()))
        for index, (q_ref, grad_ref, wide_ref, q_out) in enumerate(
            ((a_ref, a_grad_ref, a_wide, a_out), (b_ref, b_grad_ref, b_wide, b_out))
        ):
            first, last = bounds[2 * index], bounds[2 * index + 1]
            heads = halves_of(q_ref[:, lanes] * jnp.bfloat16(HEAD_SCALE))
            grads = halves_of(grad_ref[:, lanes])
            turned_q = (q_ref[:, lanes] * jnp.bfloat16(HEAD_SCALE)).T
            turned_grad = grad_ref[:, lanes].T
            span = slice(index * rows, (index + 1) * rows)
            lse = (lse_rows[0:1, span], lse_rows[4:5, span])

            product = (grad_ref[:, lanes].astype(jnp.float32) * wide_ref[:, lanes]).T
            deltas = (
                jnp.sum(product[:64], axis=0, keepdims=True),
                jnp.sum(product[64:], axis=0, keepdims=True),
            )

            def grad_step(
                key_tile,
                q_sum,
                index=index,
                heads=heads,
                grads=grads,
                lse=lse,
                deltas=deltas,
                first=first,
                turned_q=turned_q,
                turned_grad=turned_grad,
            ):
                source = key_rows(bounds[4 + key_tile])
                columns = key_rows(bounds[4 + key_tile])
                keys = kv_ref[source, lanes]
                turned_keys = keys.T
                values = kv_ref[source, value_lanes]
                mask = mask_scr[index, key_rows(key_tile - first), :]
                out = []
                for head in range(2):
                    part = slice(head * 64, (head + 1) * 64)
                    scores = turned_dot(keys, heads[head])
                    slope = turned_dot(values, grads[head])
                    probs = jnp.exp((scores - lse[head]) + mask)
                    low_slope = (probs * (slope - deltas[head])).astype(jnp.bfloat16)
                    v_acc[part, columns] += lax.dot_general(
                        turned_grad[part],
                        probs.astype(jnp.bfloat16),
                        ways,
                        preferred_element_type=jnp.float32,
                    )
                    k_acc[part, columns] += lax.dot_general(
                        turned_q[part], low_slope, ways, preferred_element_type=jnp.float32
                    )
                    out.append(
                        q_sum[head]
                        + jnp.dot(turned_keys[part], low_slope, preferred_element_type=jnp.float32)
                    )
                return tuple(out)

            nothing = jnp.zeros((64, rows), jnp.float32)
            q_parts = lax.fori_loop(first, last, grad_step, (nothing, nothing))
            q_part = jnp.concatenate(q_parts, axis=0).T
            q_out[:, lanes] = (q_part * HEAD_SCALE).astype(jnp.bfloat16)

        def store_step(tile, carry):
            source = key_rows(tile)
            kv_out[source, lanes] = k_acc[:, source].T.astype(jnp.bfloat16)
            kv_out[source, value_lanes] = v_acc[:, source].T.astype(jnp.bfloat16)
            return carry

        lax.fori_loop(0, tiles, store_step, 0)
        return unused

    lax.fori_loop(0, pairs, pair_step, 0)


def whole_block(shape):
    return pl.BlockSpec(shape, lambda i, b: (0,) * len(shape), pipeline_mode=pl.Buffered(1))


def flash_forward(bounds, queries, key_value, low, high):
    rows, width = queries[0].shape
    window = key_value.shape[0]
    pairs = width // 128
    own = whole_block((rows, width))
    line = whole_block((8, 2 * rows))
    return pl.pallas_call(
        flash_forward_kernel,
        out_shape=(
            jax.ShapeDtypeStruct((rows, width), jnp.bfloat16),
            jax.ShapeDtypeStruct((rows, width), jnp.bfloat16),
            jax.ShapeDtypeStruct((rows, width), jnp.float32),
            jax.ShapeDtypeStruct((rows, width), jnp.float32),
            jax.ShapeDtypeStruct((pairs * 8, 2 * rows), jnp.float32),
        ),
        grid_spec=pltpu.PrefetchScalarGridSpec(
            num_scalar_prefetch=1,
            grid=(1,),
            in_specs=[own, own, whole_block((window, 2 * width)), line, line],
            out_specs=[own, own, own, own, whole_block((pairs * 8, 2 * rows))],
            scratch_shapes=[
                pltpu.VMEM((2, KEY_TILES * KEY_ROWS, rows), jnp.float32),
                pltpu.VMEM((2, KEY_TILES * KEY_ROWS, rows), jnp.float32),
            ],
        ),
        compiler_params=pltpu.CompilerParams(vmem_limit_bytes=44 * 2**20),
        cost_estimate=pl.CostEstimate(
            flops=8 * rows * width * 2560, bytes_accessed=12 * 2**20, transcendentals=rows * 12 * 2560
        ),
        name="flash_forward",
    )(bounds, queries[0], queries[1], key_value, low, high)


def flash_backward(bounds, queries, key_value, grads, wides, lse, low, high):
    rows, width = queries[0].shape
    window = key_value.shape[0]
    pairs = width // 128
    own = whole_block((rows, width))
    wide = whole_block((window, 2 * width))
    line = whole_block((8, 2 * rows))
    return pl.pallas_call(
        flash_backward_kernel,
        out_shape=(
            jax.ShapeDtypeStruct((rows, width), jnp.bfloat16),
            jax.ShapeDtypeStruct((rows, width), jnp.bfloat16),
            jax.ShapeDtypeStruct((window, 2 * width), jnp.bfloat16),
        ),
        grid_spec=pltpu.PrefetchScalarGridSpec(
            num_scalar_prefetch=1,
            grid=(1,),
            in_specs=[own, own, wide] + [own] * 4 + [whole_block((pairs * 8, 2 * rows)), line, line],
            out_specs=[own, own, wide],
            scratch_shapes=[
                pltpu.VMEM((2, KEY_TILES * KEY_ROWS, rows), jnp.float32),
                pltpu.VMEM((128, window), jnp.float32),
                pltpu.VMEM((128, window), jnp.float32),
            ],
        ),
        compiler_params=pltpu.CompilerParams(vmem_limit_bytes=56 * 2**20),
        cost_estimate=pl.CostEstimate(
            flops=20 * rows * width * 2560,
            bytes_accessed=20 * 2**20,
            transcendentals=rows * 12 * 2560,
        ),
        name="flash_backward",
    )(bounds, *queries, key_value, *grads, *wides, lse, low, high)


GRP_Y, GRP_CORE, SHARD_Z, SHARD_X = 2, 2, 4, 2
BOTH = ("grp", "shard")


def device_pairs(place):
    pairs = []
    for y in range(GRP_Y):
        for core in range(GRP_CORE):
            for z in range(SHARD_Z):
                for x in range(SHARD_X):
                    target = place(y, core, z, x)
                    if target is not None:
                        ty, tcore, tz, tx = target
                        pairs.append(
                            (
                                (y * GRP_CORE + core) * SHARD_Z * SHARD_X + z * SHARD_X + x,
                                (ty * GRP_CORE + tcore) * SHARD_Z * SHARD_X + tz * SHARD_X + tx,
                            )
                        )
    return pairs


def send(values, place):
    return lax.ppermute(values, BOTH, device_pairs(place))


def turn_rows(values):
    return send(values, lambda y, core, z, x: (y, x, z, core))


def swap_core(values):
    return send(values, lambda y, core, z, x: (y, 1 - core, z, x))


def send_up(values):
    return send(values, lambda y, core, z, x: (y, core, z + 1, x) if z + 1 < SHARD_Z else None)


def send_down(values):
    return send(values, lambda y, core, z, x: (y, core, z - 1, x) if z > 0 else None)


def window_of(rows):
    near = jnp.concatenate([rows, send_up(rows), send_down(rows)])
    return jnp.concatenate([near, swap_core(near)])


def window_back(near, far, count):
    total = near + swap_core(far.astype(jnp.bfloat16)).astype(jnp.float32)
    below = total[count : 2 * count].astype(jnp.bfloat16)
    above = total[2 * count :].astype(jnp.bfloat16)
    return (
        total[:count]
        + send_down(below).astype(jnp.float32)
        + send_up(above).astype(jnp.float32)
    )


def half_of(values, axis, index):
    count = values.shape[axis] // 2
    return lax.dynamic_slice_in_dim(values, index * count, count, axis)


def unpack_kernel(kinds, in_ref, *outs):
    width = in_ref.shape[-1]
    share = in_ref.shape[3]
    place = 0
    for kind, ref in zip(kinds, outs):
        if kind == "columns":
            for column in range(ref.shape[-1] // width):
                ref[:, 0, :, column * width : (column + 1) * width] = in_ref[0, :, place]
                place += 1
        else:
            for piece in range(ref.shape[2] // share):
                ref[:, 0, piece * share : (piece + 1) * share, :] = in_ref[0, :, place]
                place += 1


def unpack_weights_of(pieces, begin_at, places, kinds, shapes):
    quarters, shards, unused, share, width = pieces.shape
    outs = pl.pallas_call(
        functools.partial(unpack_kernel, kinds),
        out_shape=[
            jax.ShapeDtypeStruct((shards, quarters, rows, wide), pieces.dtype)
            for rows, wide in shapes
        ],
        grid=(quarters,),
        in_specs=[
            pl.BlockSpec(
                (1, shards, places, share, width), lambda q: (q, 0, begin_at // places, 0, 0)
            )
        ],
        out_specs=[
            pl.BlockSpec((shards, 1, rows, wide), lambda q: (0, q, 0, 0)) for rows, wide in shapes
        ],
        compiler_params=pltpu.CompilerParams(vmem_limit_bytes=32 * 2**20),
        cost_estimate=pl.CostEstimate(
            flops=0, bytes_accessed=128 * places * share * width, transcendentals=0
        ),
        name="unpack_weights",
    )(pieces)
    return [out.reshape(-1, out.shape[-1]) for out in outs]


def pick_kernel(
    me, near_ref, project_ref, mixer_ref, expand_ref, reduce_ref, small_ref, a_out, b_out, c_out
):
    part, half = a_out.shape[-2:]
    for column in range(3):
        begin_at = pl.multiple_of(column * 2 * half + me[1] * half, 128)
        a_out[column] = near_ref[0, :, pl.ds(begin_at, half)]
    a_out[3] = jnp.zeros((part, half), a_out.dtype)
    a_out[3, 0:8, :] = small_ref[:, :half]
    a_out[3, 8:16, :] = small_ref[:, half:]
    share, width = b_out.shape[-2:]
    wide = expand_ref.shape[-1] // width
    for layer, ref in enumerate((b_out, c_out)):
        ref[0] = mixer_ref[layer]
        for column in range(wide):
            ref[1 + column] = expand_ref[layer, :, column * width : (column + 1) * width]
        for piece in range(reduce_ref.shape[1] // share):
            ref[1 + wide + piece] = reduce_ref[layer, piece * share : (piece + 1) * share, :]
    far = c_out.shape[0]
    for column in range(3):
        b_out[far + column] = project_ref[0, :, column * width : (column + 1) * width]


def pick_quarters(me, project, mixer, expand, reduce, small):
    share, width = mixer.shape[1] // 4, mixer.shape[2]
    far = 1 + expand.shape[2] // width + reduce.shape[1] // 4 // share

    def quarter_spec(array):
        return pl.BlockSpec(
            (LAYERS, array.shape[1] // 4, array.shape[2]),
            lambda i, me: (0, me[0] * GRP_CORE + me[1], 0),
        )

    shapes = [(4, 2 * share, width // 2), (far + 3, share, width), (far, share, width)]
    return pl.pallas_call(
        pick_kernel,
        out_shape=[jax.ShapeDtypeStruct(shape, jnp.bfloat16) for shape in shapes],
        grid_spec=pltpu.PrefetchScalarGridSpec(
            num_scalar_prefetch=1,
            grid=(1,),
            in_specs=[
                pl.BlockSpec((1, 2 * share, project.shape[2]), lambda i, me: (0, me[0], 0)),
                pl.BlockSpec(
                    (1, share, project.shape[2]), lambda i, me: (1, me[0] * GRP_CORE + me[1], 0)
                ),
            ]
            + [quarter_spec(array) for array in (mixer, expand, reduce)]
            + [pl.BlockSpec(small.shape, lambda i, me: (0, 0))],
            out_specs=[pl.BlockSpec(shape, lambda i, me: (0, 0, 0)) for shape in shapes],
        ),
        name="pick_quarters",
    )(me, project, project, mixer, expand, reduce, small)


def pack_kernel(kinds, *refs):
    ins, vector_ref, out_ref = refs[:-2], refs[-2], refs[-1]
    width = out_ref.shape[-1]
    share = out_ref.shape[3]
    place = 0
    for kind, ref in zip(kinds, ins):
        if kind == "columns":
            for column in range(ref.shape[-1] // width):
                out_ref[0, :, place] = ref[:, 0, :, column * width : (column + 1) * width]
                place += 1
        else:
            for piece in range(ref.shape[2] // share):
                out_ref[0, :, place] = ref[:, 0, piece * share : (piece + 1) * share, :]
                place += 1
    out_ref[0, :, place] = jnp.zeros_like(out_ref[0, :, place])
    out_ref[0, :, place, 0:8, :] = vector_ref[0]


def pack_terms(terms, kinds, share, width, vectors):
    places = sum(t.size for t in terms) // (32 * share * width) + 1
    views = [t.reshape(8, 4, -1, t.shape[1]) for t in terms]
    return pl.pallas_call(
        functools.partial(pack_kernel, kinds),
        out_shape=jax.ShapeDtypeStruct((4, 8, places, share, width), jnp.bfloat16),
        grid=(4,),
        in_specs=[pl.BlockSpec((8, 1) + view.shape[2:], lambda q: (0, q, 0, 0)) for view in views]
        + [pl.BlockSpec((1,) + vectors.shape[1:], lambda q: (q, 0, 0, 0))],
        out_specs=pl.BlockSpec((1, 8, places, share, width), lambda q: (q, 0, 0, 0, 0)),
        compiler_params=pltpu.CompilerParams(vmem_limit_bytes=32 * 2**20),
        cost_estimate=pl.CostEstimate(
            flops=0, bytes_accessed=4 * 32 * places * share * width, transcendentals=0
        ),
        name="pack_terms",
    )(*views, vectors)


def swap_y(values):
    return send(values, lambda y, core, z, x: (1 - y, core, z, x))


def swap_x(values):
    return send(values, lambda y, core, z, x: (y, core, z, 1 - x))


def swap_z(values, bit):
    return send(values, lambda y, core, z, x: (y, core, z ^ bit, x))


def spread_kernel(me, q_ref, kv_ref, vector_ref, out_ref):
    part, half = out_ref.shape[-2:]
    for x_bit in range(SHARD_X):
        for z_bits in range(SHARD_Z):
            shard = (z_bits ^ me[3]) * SHARD_X + (x_bit ^ me[2])
            out_ref[0, x_bit, z_bits, 0] = q_ref[shard, 0]
            out_ref[0, x_bit, z_bits, 1] = kv_ref[shard, 0, :, :half]
            out_ref[0, x_bit, z_bits, 2] = kv_ref[shard, 0, :, half:]
            out_ref[0, x_bit, z_bits, 3] = jnp.zeros((part, half), jnp.bfloat16)
            out_ref[0, x_bit, z_bits, 3, 0:8, :] = vector_ref[0, shard]


def spread_terms(me, query_term, key_value_term, vectors):
    half = query_term.shape[1]
    part = query_term.shape[0] // 16
    shape = (GRP_Y, SHARD_X, SHARD_Z, 4, part, half)

    def rows_spec(columns):
        return pl.BlockSpec((8, 1, part, columns), lambda j, me: (0, j ^ me[0], 0, 0))

    return pl.pallas_call(
        spread_kernel,
        out_shape=jax.ShapeDtypeStruct(shape, jnp.bfloat16),
        grid_spec=pltpu.PrefetchScalarGridSpec(
            num_scalar_prefetch=1,
            grid=(2,),
            in_specs=[
                rows_spec(half),
                rows_spec(2 * half),
                pl.BlockSpec((1,) + vectors.shape[1:], lambda j, me: (j ^ me[0], 0, 0, 0)),
            ],
            out_specs=pl.BlockSpec((1,) + shape[1:], lambda j, me: (j, 0, 0, 0, 0, 0)),
        ),
        name="spread_terms",
    )(
        me,
        query_term.reshape(8, 2, part, half),
        key_value_term.reshape(8, 2, part, 2 * half),
        vectors,
    )


def summed(one, other):
    return (one.astype(jnp.float32) + other.astype(jnp.float32)).astype(jnp.bfloat16)


def scatter_terms(me, query_term, key_value_term, vectors):
    spread = spread_terms(me, query_term, key_value_term, vectors)
    a_part, b_part = spread[:, :, :, :2], spread[:, :, :, 2:]
    a_next = swap_y(a_part[1])
    b_next = swap_x(b_part[:, 1])
    a_last = swap_x(summed(a_part[0, 1], a_next[1]))
    b_last = swap_y(summed(b_part[1, 0], b_next[1]))
    a_keep = summed(a_part[0, 0], a_next[0])
    b_keep = summed(b_part[0, 0], b_next[0])
    whole = jnp.concatenate([a_keep, b_keep], axis=1)
    come = jnp.concatenate([a_last, b_last], axis=1)
    far = swap_z(summed(whole[2:], come[2:]), 2)
    whole = summed(whole[:2], come[:2])
    near = swap_z(summed(whole[1], far[1]), 1)
    return summed(summed(whole[0], far[0]), near)


def gather_quarters(piece):
    pair = jnp.stack([piece, swap_y(piece)])
    return jnp.stack([pair, swap_core(pair)])


def finish_kernel(me, *refs):
    layers = len(refs) // 2 - 3
    outs = refs[2 * layers :]

    def fill(near_ref, far_ref):
        part, half = near_ref.shape[-2:]
        share, width = far_ref.shape[-2:]
        for y_bit in range(GRP_Y):
            for core_bit in range(GRP_CORE):
                y = y_bit ^ me[0]
                core = core_bit ^ me[1]
                quarter = y * GRP_CORE + core
                for column in range(3):
                    lanes = pl.ds(pl.multiple_of(column * 2 * half + core * half, 128), half)
                    outs[0][0, y, :, lanes] = near_ref[core_bit, y_bit, column].astype(jnp.float32)
                outs[4][0, quarter] = near_ref[core_bit, y_bit, 3, 0:8, :].astype(jnp.float32)
                outs[1][0, quarter] = far_ref[core_bit, y_bit, 0].astype(jnp.float32)
                place = 1
                for column in range(outs[2].shape[-1] // width):
                    lanes = slice(column * width, (column + 1) * width)
                    outs[2][0, quarter, :, lanes] = far_ref[core_bit, y_bit, place].astype(
                        jnp.float32
                    )
                    place += 1
                for piece in range(outs[3].shape[2] // share):
                    rows = slice(piece * share, (piece + 1) * share)
                    outs[3][0, quarter, rows, :] = far_ref[core_bit, y_bit, place].astype(
                        jnp.float32
                    )
                    place += 1
                outs[5][0, quarter] = far_ref[core_bit, y_bit, place, 0:8, :].astype(jnp.float32)

    for layer in range(layers):
        pl.when(pl.program_id(0) == layer)(
            functools.partial(fill, refs[2 * layer], refs[2 * layer + 1])
        )


def finish_shares(me, shares, hidden_units, deep):
    layers = len(shares)
    part, half = shares[0][0].shape[-2:]
    share, width = shares[0][1].shape[-2:]
    shapes = [
        (2, part, 3 * width),
        (4, share, width),
        (4, share, hidden_units),
        (4, deep, width),
        (4, 8, half),
        (4, 8, width),
    ]
    flat = [array for pair in shares for array in pair]
    outs = pl.pallas_call(
        finish_kernel,
        out_shape=[jax.ShapeDtypeStruct((layers,) + shape, jnp.float32) for shape in shapes],
        grid_spec=pltpu.PrefetchScalarGridSpec(
            num_scalar_prefetch=1,
            grid=(layers,),
            in_specs=[whole_block(array.shape) for array in flat],
            out_specs=[
                pl.BlockSpec((1,) + shape, lambda i, me: (i, 0, 0, 0)) for shape in shapes
            ],
        ),
        compiler_params=pltpu.CompilerParams(vmem_limit_bytes=32 * 2**20),
        name="finish_shares",
    )(me, *flat)
    return [out.reshape(layers, -1, out.shape[-1]) for out in outs[:4]] + list(outs[4:])


def row_mean(values):
    return jnp.mean(values, axis=1, keepdims=True)


def column_sum(values):
    return jnp.sum(values, axis=0, keepdims=True)


def standardized(values):
    centered = values - row_mean(values)
    scale = lax.rsqrt(row_mean(centered * centered) + EPSILON)
    return centered * scale, scale


def standard_back(grad, norm, scale, gain):
    weighted = grad * gain
    return (weighted - row_mean(weighted) - norm * row_mean(weighted * norm)) * scale


def tail_forward_kernel(
    me,
    own_ref,
    far_ref,
    state_ref,
    mixer_ref,
    expand_ref,
    reduce_ref,
    bias_in_ref,
    vector_ref,
    mix_out,
    norm_one_out,
    scale_one_out,
    low_out,
    active_out,
    slope_out,
    norm_two_out,
    scale_two_out,
    state_out,
    state_low_out,
    wide_scr,
    total_scr,
):
    step = pl.program_id(0)
    half = own_ref.shape[1]

    @pl.when(step == 0)
    def begin():
        mix_out[:, pl.ds(pl.multiple_of(me[1] * half, 128), half)] = own_ref[...]
        mix_out[:, pl.ds(pl.multiple_of((1 - me[1]) * half, 128), half)] = far_ref[...]
        branch = jnp.dot(mix_out[...], mixer_ref[...], preferred_element_type=jnp.float32)
        norm, scale = standardized(state_ref[...].astype(jnp.float32) + (branch + vector_ref[0:1]))
        norm_one_out[...] = norm
        scale_one_out[...] = jnp.broadcast_to(scale, scale_one_out.shape)
        wide = norm * vector_ref[1:2] + vector_ref[2:3]
        wide_scr[...] = wide
        low_out[...] = wide.astype(jnp.bfloat16)
        total_scr[...] = jnp.zeros_like(total_scr)

    before = (
        jnp.dot(low_out[...], expand_ref[...], preferred_element_type=jnp.float32)
        + bias_in_ref[...]
    )
    normal = 0.5 * (1.0 + lax.erf(before * 0.7071067811865476))
    density = jnp.exp(before * before * -0.5) * 0.3989422804014327
    active = (before * normal).astype(jnp.bfloat16)
    active_out[...] = active
    slope_out[...] = normal + before * density
    total_scr[...] += jnp.dot(active, reduce_ref[...], preferred_element_type=jnp.float32)

    @pl.when(step == pl.num_programs(0) - 1)
    def end():
        norm, scale = standardized(wide_scr[...] + (total_scr[...] + vector_ref[3:4]))
        norm_two_out[...] = norm
        scale_two_out[...] = jnp.broadcast_to(scale, scale_two_out.shape)
        state = norm * vector_ref[4:5] + vector_ref[5:6]
        state_out[...] = state
        state_low_out[...] = state.astype(jnp.bfloat16)


FEED_TILE = 512


def tail_forward(me, own_mix, far_mix, state, mixer, expand, reduce, bias_in, vectors):
    rows, width = state.shape
    hidden_units = expand.shape[1]
    steps = hidden_units // FEED_TILE
    whole = whole_block((rows, width))
    halves = whole_block((rows, width // 2))
    scale = whole_block((rows, 128))
    tile = pl.BlockSpec((rows, FEED_TILE), lambda j, me: (0, j))

    def shaped(columns, kind):
        return jax.ShapeDtypeStruct((rows, columns), kind)

    return pl.pallas_call(
        tail_forward_kernel,
        out_shape=[
            shaped(width, jnp.bfloat16),
            shaped(width, jnp.float32),
            shaped(128, jnp.float32),
            shaped(width, jnp.bfloat16),
            shaped(hidden_units, jnp.bfloat16),
            shaped(hidden_units, jnp.float32),
            shaped(width, jnp.float32),
            shaped(128, jnp.float32),
            shaped(width, jnp.float32),
            shaped(width, jnp.bfloat16),
        ],
        grid_spec=pltpu.PrefetchScalarGridSpec(
            num_scalar_prefetch=1,
            grid=(steps,),
            in_specs=[
                halves,
                halves,
                whole,
                whole_block((width, width)),
                pl.BlockSpec((width, FEED_TILE), lambda j, me: (0, j)),
                pl.BlockSpec((FEED_TILE, width), lambda j, me: (j, 0)),
                pl.BlockSpec((1, FEED_TILE), lambda j, me: (0, j)),
                whole_block((8, width)),
            ],
            out_specs=[whole, whole, scale, whole, tile, tile, whole, scale, whole, whole],
            scratch_shapes=[
                pltpu.VMEM((rows, width), jnp.float32),
                pltpu.VMEM((rows, width), jnp.float32),
            ],
        ),
        compiler_params=pltpu.CompilerParams(vmem_limit_bytes=44 * 2**20),
        cost_estimate=pl.CostEstimate(
            flops=2 * rows * width * (width + 2 * hidden_units),
            bytes_accessed=32 * 2**20,
            transcendentals=2 * rows * hidden_units,
        ),
        name="tail_forward",
    )(me, own_mix, far_mix, state, mixer, expand, reduce, bias_in, vectors)


def tail_backward_kernel(
    me,
    grad_ref,
    norm_two_ref,
    scale_two_ref,
    norm_one_ref,
    scale_one_ref,
    low_ref,
    mix_ref,
    slope_ref,
    active_ref,
    expand_ref,
    reduce_ref,
    mixer_ref,
    vector_ref,
    sum_out,
    own_out,
    far_out,
    mixer_out,
    expand_out,
    reduce_out,
    bias_in_out,
    vector_out,
    wide_scr,
    feed_scr,
    total_scr,
):
    step = pl.program_id(0)
    half = own_out.shape[1]

    @pl.when(step == 0)
    def begin():
        grad = grad_ref[...]
        norm = norm_two_ref[...]
        wide = standard_back(grad, norm, scale_two_ref[:, 0:1], vector_ref[4:5])
        wide_scr[...] = wide
        feed = wide.astype(jnp.bfloat16)
        feed_scr[...] = feed
        vector_out[...] = jnp.zeros_like(vector_out)
        vector_out[3:4] = column_sum(feed.astype(jnp.float32))
        vector_out[4:5] = column_sum(grad * norm)
        vector_out[5:6] = column_sum(grad)
        total_scr[...] = jnp.zeros_like(total_scr)

    feed = feed_scr[...]
    active_grad = turned_dot(feed, reduce_ref[...])
    before = (active_grad * slope_ref[...]).astype(jnp.bfloat16)
    bias_in_out[...] = column_sum(before.astype(jnp.float32))
    reduce_out[...] = across_dot(active_ref[...], feed).astype(jnp.bfloat16)
    expand_out[...] = across_dot(low_ref[...], before).astype(jnp.bfloat16)
    total_scr[...] += turned_dot(before, expand_ref[...])

    @pl.when(step == pl.num_programs(0) - 1)
    def end():
        grad = wide_scr[...] + total_scr[...]
        norm = norm_one_ref[...]
        wide = standard_back(grad, norm, scale_one_ref[:, 0:1], vector_ref[1:2])
        sum_out[...] = wide
        branch = wide.astype(jnp.bfloat16)
        vector_out[0:1] = column_sum(branch.astype(jnp.float32))
        vector_out[1:2] = column_sum(grad * norm)
        vector_out[2:3] = column_sum(grad)
        mixer_out[...] = across_dot(mix_ref[...], branch).astype(jnp.bfloat16)
        mixed = turned_dot(branch, mixer_ref[...]).astype(jnp.bfloat16)
        total_scr[...] = mixed.astype(jnp.float32)
        own = total_scr[:, pl.ds(pl.multiple_of(me[1] * half, 128), half)]
        far = total_scr[:, pl.ds(pl.multiple_of((1 - me[1]) * half, 128), half)]
        own_out[...] = own.astype(jnp.bfloat16)
        far_out[...] = far.astype(jnp.bfloat16)


def tail_backward(me, grad, kept, weights, vectors):
    norm_two, scale_two, norm_one, scale_one, low, mixed, slope, active = kept
    mixer, expand, reduce = weights
    rows, width = grad.shape
    hidden_units = expand.shape[1]
    steps = hidden_units // FEED_TILE
    whole = whole_block((rows, width))
    halves = whole_block((rows, width // 2))
    scale = whole_block((rows, 128))
    square = whole_block((width, width))
    tile = pl.BlockSpec((rows, FEED_TILE), lambda j, me: (0, j))
    across = pl.BlockSpec((width, FEED_TILE), lambda j, me: (0, j))
    down = pl.BlockSpec((FEED_TILE, width), lambda j, me: (j, 0))
    line = pl.BlockSpec((1, FEED_TILE), lambda j, me: (0, j))

    def shaped(rows, columns, kind):
        return jax.ShapeDtypeStruct((rows, columns), kind)

    return pl.pallas_call(
        tail_backward_kernel,
        out_shape=[
            shaped(rows, width, jnp.float32),
            shaped(rows, width // 2, jnp.bfloat16),
            shaped(rows, width // 2, jnp.bfloat16),
            shaped(width, width, jnp.bfloat16),
            shaped(width, hidden_units, jnp.bfloat16),
            shaped(hidden_units, width, jnp.bfloat16),
            shaped(1, hidden_units, jnp.float32),
            shaped(8, width, jnp.float32),
        ],
        grid_spec=pltpu.PrefetchScalarGridSpec(
            num_scalar_prefetch=1,
            grid=(steps,),
            in_specs=[whole, whole, scale, whole, scale, whole, whole, tile, tile, across, down]
            + [square, whole_block((8, width))],
            out_specs=[whole, halves, halves, square, across, down, line, whole_block((8, width))],
            scratch_shapes=[
                pltpu.VMEM((rows, width), jnp.float32),
                pltpu.VMEM((rows, width), jnp.bfloat16),
                pltpu.VMEM((rows, width), jnp.float32),
            ],
        ),
        compiler_params=pltpu.CompilerParams(vmem_limit_bytes=48 * 2**20),
        cost_estimate=pl.CostEstimate(
            flops=2 * rows * width * (2 * width + 4 * hidden_units),
            bytes_accessed=40 * 2**20,
            transcendentals=0,
        ),
        name="tail_backward",
    )(
        me,
        grad,
        norm_two,
        scale_two,
        norm_one,
        scale_one,
        low,
        mixed,
        slope,
        active,
        expand,
        reduce,
        mixer,
        vectors,
    )


def gather_all(local):
    places, share, width = local.shape
    gathered = lax.all_gather(local.reshape(-1, width), BOTH, axis=0, tiled=False)
    return gathered.reshape(4, 8, places, share, width)


def join_kernel(me, a_ref, b_ref, project_ref, small_ref):
    half = a_ref.shape[-1]
    for y_bit in range(GRP_Y):
        y = y_bit ^ me[0]
        for x_bit in range(SHARD_X):
            for z_bits in range(SHARD_Z):
                shard = (z_bits ^ me[3]) * SHARD_X + (x_bit ^ me[2])
                project_ref[shard, y, :, :half] = a_ref[y_bit, x_bit, z_bits, 0]
                project_ref[shard, y, :, half : 2 * half] = a_ref[y_bit, x_bit, z_bits, 1]
                project_ref[shard, y, :, 2 * half :] = b_ref[x_bit, y_bit, z_bits, 0]
                if y_bit == 0:
                    small_ref[shard, :, :half] = b_ref[x_bit, y_bit, z_bits, 1, 0:8, :]
                    small_ref[shard, :, half:] = b_ref[x_bit, y_bit, z_bits, 1, 8:16, :]


def gather_first(me, local, rows):
    part, half = local.shape[1:]
    pair = jnp.stack([local, swap_z(local, 1)])
    pair, rows = lax.optimization_barrier((pair, rows))
    window = window_of(rows)
    four = jnp.concatenate([pair, swap_z(pair, 2)])
    a_part, b_part = four[:, :2], four[:, 2:]
    a_two = jnp.stack([a_part, swap_x(a_part)])
    b_two = jnp.stack([b_part, swap_y(b_part)])
    a_four = jnp.stack([a_two, swap_y(a_two)])
    b_four = jnp.stack([b_two, swap_x(b_two)])
    project, small = pl.pallas_call(
        join_kernel,
        out_shape=[
            jax.ShapeDtypeStruct((8, 2, part, 3 * half), local.dtype),
            jax.ShapeDtypeStruct((8, 8, 2 * half), local.dtype),
        ],
        grid_spec=pltpu.PrefetchScalarGridSpec(
            num_scalar_prefetch=1,
            grid=(1,),
            in_specs=[whole_block(a_four.shape)] * 2,
            out_specs=[whole_block((8, 2, part, 3 * half)), whole_block((8, 8, 2 * half))],
        ),
        compiler_params=pltpu.CompilerParams(vmem_limit_bytes=24 * 2**20),
        name="join_projection",
    )(me, a_four, b_four)
    return project.reshape(-1, 3 * half), small, four, rows, window


def on_device_turned(
    tokens,
    cotangent,
    seq_lengths,
    seq_order,
    w_project,
    w_mixer,
    w_expand,
    w_reduce,
    biases,
    norm_gains,
):
    row_count, width = tokens.shape
    shard_index = lax.axis_index("shard")
    quarter = lax.axis_index("grp")
    z, x = shard_index // SHARD_X, shard_index % SHARD_X
    y, core = quarter // GRP_CORE, quarter % GRP_CORE
    me = jnp.stack([y, core, x, z]).astype(jnp.int32)
    hidden_units = w_expand.shape[2]
    group_slots = row_count * 8
    seq_count = seq_lengths.shape[1]
    seq_ends = group_ends(seq_lengths, seq_order, y * GRP_CORE + x)
    block_index = z * GRP_CORE + jnp.stack([core, 1 - core])
    slot_index = block_index[:, None] * row_count + jnp.arange(row_count, dtype=jnp.int32)[None, :]
    slot_index = slot_index.reshape(-1)
    before_slot = seq_ends[None, :] <= slot_index[:, None]
    own_segment = jnp.sum(before_slot[:row_count].astype(jnp.int32), axis=1, dtype=jnp.int32)
    starts = jnp.max(jnp.where(before_slot, seq_ends[None, :], 0), axis=1)
    stops = jnp.min(jnp.where(before_slot, group_slots, seq_ends[None, :]), axis=1)
    window_begin = (z - 1) * GRP_CORE * row_count
    low = starts - window_begin
    high = stops - window_begin
    low_line = jnp.broadcast_to(low[None, :], (8, 2 * row_count))
    high_line = jnp.broadcast_to(high[None, :], (8, 2 * row_count))
    places = [(1, 0, 2)[t // 2] + ((t % 2) ^ core) * 3 for t in range(6)]
    bounds = jnp.stack(
        [
            low[0] // KEY_ROWS,
            (high[row_count - 1] + KEY_ROWS - 1) // KEY_ROWS,
            low[row_count] // KEY_ROWS,
            (high[2 * row_count - 1] + KEY_ROWS - 1) // KEY_ROWS,
        ]
        + places
    ).astype(jnp.int32)
    valid_rows = (own_segment < seq_count).astype(jnp.float32)[:, None]

    small = jnp.concatenate(
        [jnp.concatenate([biases[i], norm_gains[i]]) for i in range(LAYERS)]
    ).reshape(-1, width)
    share = w_project.shape[1] // 4
    deep = w_reduce.shape[1] // 4
    bias_count = biases.shape[1]
    small_rows = small.shape[0]
    small = jnp.concatenate([small, jnp.zeros((8 - small_rows, width), small.dtype)])
    near_first, far_first, far_last = pick_quarters(
        me, w_project, w_mixer, w_expand, w_reduce, small
    )
    state_low = turn_rows(tokens)
    state_grad = turn_rows(cotangent)
    project_first, small_all, arrived, state_low, first_window = gather_first(
        me, near_first, state_low
    )
    far_first, arrived = lax.optimization_barrier((far_first, arrived))
    far_kinds = ("columns", "columns", "rows")
    far_shapes = [(share, width), (share, hidden_units), (deep, width)]
    far_count = far_last.shape[0]
    pieces = gather_all(far_first)
    first_whole = [project_first] + unpack_weights_of(pieces, 0, far_count, far_kinds, far_shapes)
    project_last = unpack_weights_of(pieces, far_count, 3, ("columns",), [(share, 3 * width)])[0]
    project_last = jnp.concatenate(
        [half_of(project_last[:, i * width : (i + 1) * width], 1, core) for i in range(3)], axis=1
    )
    last_whole = [project_last] + unpack_weights_of(
        gather_all(far_last), 0, far_count, far_kinds, far_shapes
    )
    small_all = small_all[:, :small_rows].reshape(8, LAYERS, -1)
    weights = []
    for layer_index, whole in enumerate([first_whole, last_whole]):
        bias_vec = small_all[:, layer_index, :bias_count].reshape(-1)
        gain_vec = small_all[:, layer_index, bias_count:].reshape(-1)
        weights.append(unpack_weights(whole + [bias_vec, gain_vec], width, hidden_units))

    hidden_state = state_low.astype(jnp.float32)
    kept_list = []
    for layer_index in range(LAYERS):
        project, mixing, expand, shrink, bias_list, gain_one, gain_two = weights[layer_index]
        bias_q, bias_v, bias_mix, shift_one, bias_in, bias_out, shift_two = bias_list
        state_window = first_window if layer_index == 0 else window_of(state_low)
        half = width // 2
        far_begin = 3 * row_count
        queries = [
            (
                jnp.dot(
                    state_window[begin_at : begin_at + row_count],
                    project[:, :half],
                    preferred_element_type=jnp.float32,
                )
                + half_of(bias_q, 0, core)
            ).astype(jnp.bfloat16)
            for begin_at in (0, far_begin)
        ]
        key_value = (
            jnp.dot(state_window, project[:, half:], preferred_element_type=jnp.float32)
            + jnp.concatenate([jnp.zeros((half,), jnp.float32), half_of(bias_v, 0, core)])
        ).astype(jnp.bfloat16)
        own_mix, far_mix, own_wide, far_wide, lse = flash_forward(bounds, queries, key_value, low_line, high_line)
        far_mix = swap_core(far_mix)
        tail_vectors = jnp.stack(
            [bias_mix, gain_one, shift_one, bias_out, gain_two, shift_two, bias_mix, bias_mix]
        )
        (
            mixed_low,
            norm_one,
            scale_one,
            normed_low,
            active_low,
            slope,
            norm_two,
            scale_two,
            hidden_state,
            next_low,
        ) = tail_forward(
            me, own_mix, far_mix, hidden_state, mixing, expand, shrink, bias_in[None], tail_vectors
        )
        kept_list.append(
            (
                state_low,
                state_window,
                queries,
                key_value,
                (own_wide, far_wide),
                lse,
                (norm_two, scale_two, norm_one, scale_one, normed_low, mixed_low, slope, active_low),
                tail_vectors,
            )
        )
        state_low = next_low
    activations = turn_rows((hidden_state * valid_rows).astype(jnp.bfloat16))
    state_grad = state_grad.astype(jnp.float32) * valid_rows
    results = [None] * LAYERS
    for layer_index in reversed(range(LAYERS)):
        layer_low, state_window, queries, key_value, wides, lse, kept, tail_vectors = kept_list[
            layer_index
        ]
        project, mixing, expand, shrink, *unused = weights[layer_index]
        (
            sum_one_grad,
            own_mix_grad,
            far_mix_grad,
            mixing_grad,
            expand_grad,
            shrink_grad,
            bias_in_grad,
            vector_grads,
        ) = tail_backward(me, state_grad, kept, (mixing, expand, shrink), tail_vectors)
        bias_mix_grad, gain_one_grad, shift_one_grad, bias_out_grad, gain_two_grad, shift_two_grad = [
            vector_grads[i] for i in range(6)
        ]
        mixed_grads = (own_mix_grad, swap_core(far_mix_grad))
        own_grad, far_grad, key_value_grad = flash_backward(
            bounds, queries, key_value, mixed_grads, wides, lse, low_line, high_line
        )
        query_term = jnp.einsum(
            "td,te->de", layer_low, own_grad, preferred_element_type=jnp.float32
        ) + jnp.einsum(
            "td,te->de",
            state_window[far_begin : far_begin + row_count],
            far_grad,
            preferred_element_type=jnp.float32,
        )
        key_value_term = jnp.einsum(
            "td,te->de", state_window, key_value_grad, preferred_element_type=jnp.float32
        )
        bias_q_grad = jnp.sum(own_grad, axis=0, dtype=jnp.float32) + jnp.sum(
            far_grad, axis=0, dtype=jnp.float32
        )
        bias_v_grad = jnp.sum(key_value_grad[:, half:], axis=0, dtype=jnp.float32)
        window_grad = jnp.einsum(
            "te,de->td", key_value_grad, project[:, half:], preferred_element_type=jnp.float32
        )
        own_part = jnp.einsum(
            "te,de->td", own_grad, project[:, :half], preferred_element_type=jnp.float32
        )
        far_part = jnp.einsum(
            "te,de->td", far_grad, project[:, :half], preferred_element_type=jnp.float32
        )
        near_terms = jnp.concatenate(
            [window_grad[:row_count] + own_part, window_grad[row_count:far_begin]]
        )
        far_terms = jnp.concatenate(
            [
                window_grad[far_begin : far_begin + row_count] + far_part,
                window_grad[far_begin + row_count :],
            ]
        )
        state_grad = sum_one_grad + window_back(near_terms, far_terms, row_count)
        zeros_two = jnp.zeros((2 * width,), jnp.float32)
        vectors = jnp.concatenate(
            [
                zeros_two,
                bias_mix_grad,
                shift_one_grad,
                bias_in_grad[0],
                bias_out_grad,
                shift_two_grad,
            ]
        ).reshape(8, -1)
        gains = jnp.concatenate([gain_one_grad, gain_two_grad]).reshape(8, -1)
        vectors = jnp.concatenate([vectors, gains], axis=1).astype(jnp.bfloat16)
        vectors = vectors.reshape(8, 4, 1, -1).transpose(1, 0, 2, 3)
        vectors = jnp.pad(vectors, ((0, 0), (0, 0), (0, 7), (0, width - vectors.shape[3])))
        terms = (mixing_grad, expand_grad, shrink_grad)
        pieces = pack_terms(terms, far_kinds, share, width, vectors)
        fed = lax.psum_scatter(
            pieces.reshape(32, -1, width), BOTH, scatter_dimension=0, tiled=True
        ).reshape(-1, share, width)
        lines = jnp.zeros((8 * bias_count,), jnp.float32)
        lines = lax.dynamic_update_slice(lines, bias_q_grad, (core * half,))
        lines = lax.dynamic_update_slice(lines, bias_v_grad, (width + core * half,))
        lines = lines.reshape(8, 2, -1).transpose(1, 0, 2).astype(jnp.bfloat16)
        lines = jnp.pad(lines, ((0, 0), (0, 0), (0, width - lines.shape[2])))
        lines = jnp.pad(lines.reshape(2, 8, 2, half), ((0, 0), (0, 0), (0, 6), (0, 0)))
        attended = scatter_terms(
            me, query_term.astype(jnp.bfloat16), key_value_term.astype(jnp.bfloat16), lines
        )
        results[layer_index] = (gather_quarters(attended), gather_quarters(fed))
    outs = finish_shares(me, results, hidden_units, deep)
    quarter_len = (bias_count + norm_gains.shape[1]) // 4
    vectors = outs[5][:, :, 0, :quarter_len].reshape(LAYERS, -1)
    lines = outs[4][:, :, :2].reshape(LAYERS, GRP_Y, GRP_CORE, width)[..., : bias_count // 2]
    lines = jnp.sum(lines, axis=2).reshape(LAYERS, bias_count)
    input_grad = turn_rows(state_grad.astype(jnp.bfloat16)).astype(jnp.float32)
    return (
        activations,
        input_grad,
        outs[0],
        outs[1],
        outs[2],
        outs[3],
        vectors[:, :bias_count] + lines,
        vectors[:, bias_count:],
    )


def solution(mesh):
    in_specs = (
        P(("grp", "shard"), None),
        P(("grp", "shard"), None),
        P(),
        P(),
        P(None, "shard", None),
        P(None, "shard", None),
        P(None, "shard", None),
        P(None, "shard", None),
        P(None, "shard"),
        P(None, "shard"),
    )
    out_specs = (
        P(("grp", "shard"), None),
        P(("grp", "shard"), None),
        P(None, "shard", None),
        P(None, "shard", None),
        P(None, "shard", None),
        P(None, "shard", None),
        P(None, "shard"),
        P(None, "shard"),
    )
    body = on_device_turned if mesh.shape["shard"] == 8 and mesh.shape["grp"] == 4 else on_device
    return jax.shard_map(
        body, mesh=mesh, in_specs=in_specs, out_specs=out_specs, check_vma=False
    )
```

```python
import functools

import jax
import jax.numpy as jnp
from jax import lax
from jax.experimental import pallas as pl
from jax.experimental.pallas import tpu as pltpu
from jax.sharding import PartitionSpec as P

HEADS = 12
LAYERS = 2
SEQ_MAX = 2048


EPSILON = 1e-12
NEGATIVE = -1e30


def passed_along(shard, axis, by):
    size = lax.axis_size(axis)
    pairs = [(i, i + by) for i in range(size) if 0 <= i + by < size]
    return lax.ppermute(shard, axis, pairs)


def layer_norm(values, gain, shift):
    middle = jnp.mean(values, axis=-1, keepdims=True)
    centered = values - middle
    spread = jnp.mean(centered * centered, axis=-1, keepdims=True)
    return centered * lax.rsqrt(spread + EPSILON) * gain + shift


def gelu_exact(values):
    return jax.nn.gelu(values, approximate=False)


def keep_same(carried):
    return carried


def group_ends(seq_lengths, seq_order, group_index):
    lengths_row = lax.dynamic_index_in_dim(seq_lengths, group_index, 0, keepdims=False)
    order_row = lax.dynamic_index_in_dim(seq_order, group_index, 0, keepdims=False)
    places = jnp.arange(lengths_row.shape[0], dtype=jnp.int32)
    picked = order_row[:, None] == places[None, :]
    placed = jnp.sum(jnp.where(picked, lengths_row[None, :], 0), axis=1, dtype=jnp.int32)
    return jnp.cumsum(placed, dtype=jnp.int32)


def slot_segments(slot_index, seq_ends):
    flattened = slot_index.reshape(-1)
    counted = jnp.sum(
        (seq_ends[None, :] <= flattened[:, None]).astype(jnp.int32), axis=1, dtype=jnp.int32
    )
    return counted.reshape(slot_index.shape)


def unpack_weights(weights, width, hidden_units):
    bias_vec = weights[4].astype(jnp.float32)
    gain_vec = weights[5].astype(jnp.float32)
    piece_lens = [width, width, width, width, hidden_units, width, width]
    bias_list = []
    begin_at = 0
    for piece_len in piece_lens:
        bias_list.append(bias_vec[begin_at : begin_at + piece_len])
        begin_at = begin_at + piece_len
    return (
        weights[0],
        weights[1],
        weights[2],
        weights[3],
        bias_list,
        gain_vec[:width],
        gain_vec[width:],
    )


def block_probs(queries, keys_block, seg_block, own_segment, log_total, score_scale):
    raw_scores = jnp.einsum("qhd,khd->hqk", queries, keys_block, preferred_element_type=jnp.float32)
    allowed = (own_segment[:, None] == seg_block[None, :])[None]
    return jnp.where(allowed, jnp.exp(raw_scores * score_scale - log_total[:, :, None]), 0.0)


def gather_window(key_rows, value_rows, reach_blocks):
    key_list = []
    value_list = []
    for step_offset in range(-reach_blocks, reach_blocks + 1):
        if step_offset == 0:
            moved = (key_rows, value_rows)
        else:
            moved = passed_along((key_rows, value_rows), "shard", -step_offset)
        key_list.append(moved[0])
        value_list.append(moved[1])
    return (jnp.stack(key_list), jnp.stack(value_list))


def return_parts(key_parts, value_parts, reach_blocks):
    key_total = key_parts[reach_blocks]
    value_total = value_parts[reach_blocks]
    for step_offset in range(-reach_blocks, reach_blocks + 1):
        if step_offset != 0:
            arrived = (
                passed_along(
                    key_parts[step_offset + reach_blocks].astype(jnp.bfloat16), "shard", step_offset
                ).astype(jnp.float32),
                passed_along(
                    value_parts[step_offset + reach_blocks].astype(jnp.bfloat16),
                    "shard",
                    step_offset,
                ).astype(jnp.float32),
            )
            key_total = key_total + arrived[0]
            value_total = value_total + arrived[1]
    return (key_total, value_total)


def attend_forward(
    queries, window_keys, window_values, window_segment, live_block, own_segment, score_scale
):
    row_count, head_count, head_dim = queries.shape

    def stats_step(carry, items):
        keys_block, seg_block, alive = items

        def stats_compute(state_pair):
            running_top, running_sum = state_pair
            allowed = (own_segment[:, None] == seg_block[None, :])[None]
            raw_scores = jnp.einsum(
                "qhd,khd->hqk", queries, keys_block, preferred_element_type=jnp.float32
            )
            scores = jnp.where(allowed, raw_scores * score_scale, NEGATIVE)
            new_top = jnp.maximum(running_top, jnp.max(scores, axis=-1))
            weighted = jnp.where(allowed, jnp.exp(scores - new_top[:, :, None]), 0.0)
            return (
                new_top,
                running_sum * jnp.exp(running_top - new_top) + jnp.sum(weighted, axis=-1),
            )

        return (lax.cond(alive, stats_compute, keep_same, carry), None)

    begin_stats = (
        jnp.full((head_count, row_count), NEGATIVE, jnp.float32),
        jnp.zeros((head_count, row_count), jnp.float32),
    )
    (running_top, running_sum), unused = lax.scan(
        stats_step, begin_stats, (window_keys, window_segment, live_block)
    )
    log_total = running_top + jnp.log(running_sum)

    def mix_step(carry, items):
        keys_block, values_block, seg_block, alive = items

        def mix_compute(state_pair):
            mixed, extra = state_pair
            probs = block_probs(queries, keys_block, seg_block, own_segment, log_total, score_scale)
            probs_low = probs.astype(jnp.bfloat16)
            rest_low = (probs - lax.optimization_barrier(probs_low).astype(jnp.float32)).astype(
                jnp.bfloat16
            )
            mixed = mixed + jnp.einsum(
                "hqk,khd->qhd", probs_low, values_block, preferred_element_type=jnp.float32
            )
            extra = extra + jnp.einsum(
                "hqk,khd->qhd", rest_low, values_block, preferred_element_type=jnp.float32
            )
            return (mixed, extra)

        return (lax.cond(alive, mix_compute, keep_same, carry), None)

    zeros_mix = jnp.zeros((row_count, head_count, head_dim), jnp.float32)
    (mixed, extra), unused = lax.scan(
        mix_step, (zeros_mix, zeros_mix), (window_keys, window_values, window_segment, live_block)
    )
    return (log_total, mixed, mixed + extra)


def attend_backward(
    queries,
    window_keys,
    window_values,
    window_segment,
    live_block,
    own_segment,
    log_total,
    delta,
    grad_low,
    score_scale,
):

    def grad_step(query_grad, items):
        keys_block, values_block, seg_block, alive = items

        def grad_compute(carried):
            probs = block_probs(queries, keys_block, seg_block, own_segment, log_total, score_scale)
            prob_grad = jnp.einsum(
                "qhd,khd->hqk", grad_low, values_block, preferred_element_type=jnp.float32
            )
            score_low = (probs * (prob_grad - delta[:, :, None])).astype(jnp.bfloat16)
            carried = carried + jnp.einsum(
                "hqk,khd->qhd", score_low, keys_block, preferred_element_type=jnp.float32
            )
            probs_low = probs.astype(jnp.bfloat16)
            value_part = jnp.einsum(
                "hqk,qhd->khd", probs_low, grad_low, preferred_element_type=jnp.float32
            )
            key_part = jnp.einsum(
                "hqk,qhd->khd", score_low, queries, preferred_element_type=jnp.float32
            )
            return (carried, (key_part, value_part))

        def skipped(carried):
            nothing = jnp.zeros(keys_block.shape, jnp.float32)
            return (carried, (nothing, nothing))

        return lax.cond(alive, grad_compute, skipped, query_grad)

    zero_grad = jnp.zeros(queries.shape, jnp.float32)
    query_grad, key_value = lax.scan(
        grad_step, zero_grad, (window_keys, window_values, window_segment, live_block)
    )
    return (query_grad, key_value)


def on_device(
    tokens,
    cotangent,
    seq_lengths,
    seq_order,
    w_project,
    w_mixer,
    w_expand,
    w_reduce,
    biases,
    norm_gains,
):
    row_count, width = tokens.shape
    shard_count = lax.axis_size("shard")
    shard_index = lax.axis_index("shard")
    group_index = lax.axis_index("grp")
    head_dim = width // HEADS
    hidden_units = w_expand.shape[2]
    score_scale = head_dim ** (-0.5)
    longest = min(SEQ_MAX, row_count * shard_count // 4)
    reach_blocks = longest // row_count
    seq_count = seq_lengths.shape[1]
    seq_ends = group_ends(seq_lengths, seq_order, group_index)
    neighbour = shard_index + jnp.arange(-reach_blocks, reach_blocks + 1, dtype=jnp.int32)
    slot_index = neighbour[:, None] * row_count + jnp.arange(row_count, dtype=jnp.int32)[None, :]
    window_segment = slot_segments(slot_index, seq_ends)
    own_segment = window_segment[reach_blocks]
    inside = (neighbour >= 0) & (neighbour < shard_count)
    live_block = (
        inside
        & (window_segment[:, 0] <= own_segment[row_count - 1])
        & (window_segment[:, row_count - 1] >= own_segment[0])
    )
    valid_rows = (own_segment < seq_count).astype(jnp.float32)[:, None]
    hidden_state = tokens.astype(jnp.float32)
    state_low = tokens
    kept_list = []
    for layer_index in range(LAYERS):
        weights = (
            lax.all_gather(w_project[layer_index], "shard", axis=0, tiled=True),
            lax.all_gather(w_mixer[layer_index], "shard", axis=0, tiled=True),
            lax.all_gather(w_expand[layer_index], "shard", axis=0, tiled=True),
            lax.all_gather(w_reduce[layer_index], "shard", axis=0, tiled=True),
            lax.all_gather(biases[layer_index], "shard", axis=0, tiled=True),
            lax.all_gather(norm_gains[layer_index], "shard", axis=0, tiled=True),
        )
        project, mixing, expand, shrink, bias_list, gain_one, gain_two = unpack_weights(
            weights, width, hidden_units
        )
        bias_q, bias_v, bias_mix, shift_one, bias_in, bias_out, shift_two = bias_list
        projected = jnp.dot(state_low, project, preferred_element_type=jnp.float32)
        projected = projected + jnp.concatenate([bias_q, jnp.zeros_like(bias_q), bias_v])
        projected_low = projected.astype(jnp.bfloat16)
        queries = projected_low[:, :width].reshape(row_count, HEADS, head_dim)
        key_rows = projected_low[:, width : 2 * width].reshape(row_count, HEADS, head_dim)
        value_rows = projected_low[:, 2 * width :].reshape(row_count, HEADS, head_dim)
        window_keys, window_values = gather_window(key_rows, value_rows, reach_blocks)
        log_total, mixed, full_mix = attend_forward(
            queries,
            window_keys,
            window_values,
            window_segment,
            live_block,
            own_segment,
            score_scale,
        )
        mixed_low = mixed.reshape(row_count, width).astype(jnp.bfloat16)
        branch = jnp.dot(mixed_low, mixing, preferred_element_type=jnp.float32) + bias_mix
        summed_one = hidden_state + branch
        normed_one = layer_norm(summed_one, gain_one, shift_one)
        normed_low = normed_one.astype(jnp.bfloat16)
        before = jnp.dot(normed_low, expand, preferred_element_type=jnp.float32) + bias_in
        active_low = gelu_exact(before).astype(jnp.bfloat16)
        feed_out = jnp.dot(active_low, shrink, preferred_element_type=jnp.float32) + bias_out
        summed_two = normed_one + feed_out
        hidden_state = layer_norm(summed_two, gain_two, shift_two)
        kept_list.append(
            (
                state_low,
                queries,
                key_rows,
                value_rows,
                window_keys,
                window_values,
                log_total,
                full_mix,
                mixed_low,
                summed_one,
                normed_low,
                before,
                active_low,
                summed_two,
                weights,
            )
        )
        state_low = hidden_state.astype(jnp.bfloat16)
    activations = (hidden_state * valid_rows).astype(jnp.bfloat16)
    state_grad = cotangent.astype(jnp.float32) * valid_rows
    results = [None] * LAYERS
    for layer_index in reversed(range(LAYERS)):
        (
            layer_low,
            queries,
            key_rows,
            value_rows,
            window_keys,
            window_values,
            log_total,
            full_mix,
            mixed_low,
            summed_one,
            normed_low,
            before,
            active_low,
            summed_two,
            kept_weights,
        ) = kept_list[layer_index]
        weights = (
            lax.all_gather(w_project[layer_index], "shard", axis=0, tiled=True),
            lax.all_gather(w_mixer[layer_index], "shard", axis=0, tiled=True),
            lax.all_gather(w_expand[layer_index], "shard", axis=0, tiled=True),
            lax.all_gather(w_reduce[layer_index], "shard", axis=0, tiled=True),
            lax.all_gather(biases[layer_index], "shard", axis=0, tiled=True),
            lax.all_gather(norm_gains[layer_index], "shard", axis=0, tiled=True),
        )
        project, mixing, expand, shrink, bias_list, gain_one, gain_two = unpack_weights(
            weights, width, hidden_units
        )
        bias_q, bias_v, bias_mix, shift_one, bias_in, bias_out, shift_two = bias_list
        unused_two, norm_pull = jax.vjp(layer_norm, summed_two, gain_two, shift_two)
        sum_two_grad, gain_two_grad, shift_two_grad = norm_pull(state_grad)
        feed_low = sum_two_grad.astype(jnp.bfloat16)
        shrink_grad = jnp.einsum(
            "tf,td->fd", active_low, feed_low, preferred_element_type=jnp.float32
        )
        bias_out_grad = jnp.sum(feed_low, axis=0, dtype=jnp.float32)
        active_grad = jnp.einsum("td,fd->tf", feed_low, shrink, preferred_element_type=jnp.float32)
        unused_gelu, gelu_pull = jax.vjp(gelu_exact, before)
        before_low = gelu_pull(active_grad)[0].astype(jnp.bfloat16)
        expand_grad = jnp.einsum(
            "td,tf->df", normed_low, before_low, preferred_element_type=jnp.float32
        )
        bias_in_grad = jnp.sum(before_low, axis=0, dtype=jnp.float32)
        normed_grad = sum_two_grad + jnp.einsum(
            "tf,df->td", before_low, expand, preferred_element_type=jnp.float32
        )
        unused_one, first_pull = jax.vjp(layer_norm, summed_one, gain_one, shift_one)
        sum_one_grad, gain_one_grad, shift_one_grad = first_pull(normed_grad)
        branch_low = sum_one_grad.astype(jnp.bfloat16)
        mixing_grad = jnp.einsum(
            "td,te->de", mixed_low, branch_low, preferred_element_type=jnp.float32
        )
        bias_mix_grad = jnp.sum(branch_low, axis=0, dtype=jnp.float32)
        mixed_grad = jnp.einsum("te,de->td", branch_low, mixing, preferred_element_type=jnp.float32)
        mixed_grad_low = mixed_grad.astype(jnp.bfloat16).reshape(row_count, HEADS, head_dim)
        delta = jnp.sum(mixed_grad_low.astype(jnp.float32) * full_mix, axis=-1).T
        query_grad, key_value = attend_backward(
            queries,
            window_keys,
            window_values,
            window_segment,
            live_block,
            own_segment,
            log_total,
            delta,
            mixed_grad_low,
            score_scale,
        )
        key_total, value_total = return_parts(key_value[0], key_value[1], reach_blocks)
        projected_grad = jnp.concatenate(
            [
                (query_grad * score_scale).reshape(row_count, width),
                (key_total * score_scale).reshape(row_count, width),
                value_total.reshape(row_count, width),
            ],
            axis=1,
        )
        projected_low = projected_grad.astype(jnp.bfloat16)
        project_grad = jnp.einsum(
            "td,te->de", layer_low, projected_low, preferred_element_type=jnp.float32
        )
        bias_q_grad = jnp.sum(projected_low[:, :width], axis=0, dtype=jnp.float32)
        bias_v_grad = jnp.sum(projected_low[:, 2 * width :], axis=0, dtype=jnp.float32)
        state_grad = sum_one_grad + jnp.einsum(
            "te,de->td", projected_low, project, preferred_element_type=jnp.float32
        )
        bias_all = jnp.concatenate(
            [
                bias_q_grad,
                bias_v_grad,
                bias_mix_grad,
                shift_one_grad,
                bias_in_grad,
                bias_out_grad,
                shift_two_grad,
            ]
        )
        gain_all = jnp.concatenate([gain_one_grad, gain_two_grad])
        shares = (
            lax.psum_scatter(
                project_grad.astype(jnp.bfloat16), "shard", scatter_dimension=0, tiled=True
            ).astype(jnp.float32),
            lax.psum_scatter(
                mixing_grad.astype(jnp.bfloat16), "shard", scatter_dimension=0, tiled=True
            ).astype(jnp.float32),
            lax.psum_scatter(
                expand_grad.astype(jnp.bfloat16), "shard", scatter_dimension=0, tiled=True
            ).astype(jnp.float32),
            lax.psum_scatter(
                shrink_grad.astype(jnp.bfloat16), "shard", scatter_dimension=0, tiled=True
            ).astype(jnp.float32),
            lax.psum_scatter(
                bias_all.astype(jnp.bfloat16), "shard", scatter_dimension=0, tiled=True
            ).astype(jnp.float32),
            lax.psum_scatter(
                gain_all.astype(jnp.bfloat16), "shard", scatter_dimension=0, tiled=True
            ).astype(jnp.float32),
        )
        shares = (
            lax.psum(shares[0].astype(jnp.bfloat16), "grp").astype(jnp.float32),
            lax.psum(shares[1].astype(jnp.bfloat16), "grp").astype(jnp.float32),
            lax.psum(shares[2].astype(jnp.bfloat16), "grp").astype(jnp.float32),
            lax.psum(shares[3].astype(jnp.bfloat16), "grp").astype(jnp.float32),
            lax.psum(shares[4].astype(jnp.bfloat16), "grp").astype(jnp.float32),
            lax.psum(shares[5].astype(jnp.bfloat16), "grp").astype(jnp.float32),
        )
        results[layer_index] = shares
    stacked = [jnp.stack([layer_share[member] for layer_share in results]) for member in range(6)]
    return (
        activations,
        state_grad,
        stacked[0],
        stacked[1],
        stacked[2],
        stacked[3],
        stacked[4],
        stacked[5],
    )


HEAD_SCALE = 0.125


def in_main(array):
    return pltpu.with_memory_space_constraint(array, pltpu.HBM)


def fold_rows(values, combine):
    total = values[:8]
    for begin_at in range(8, values.shape[0], 8):
        total = combine(total, values[begin_at : begin_at + 8])
    return total


def halves_of(block):
    lane = lax.broadcasted_iota(jnp.int32, block.shape, 1)
    nothing = jnp.zeros_like(block)
    return (jnp.where(lane < 64, block, nothing), jnp.where(lane < 64, nothing, block))


def turned_dot(keys, queries):
    return lax.dot_general(
        keys, queries, (((1,), (1,)), ((), ())), preferred_element_type=jnp.float32
    )


def across_dot(weight, values):
    return lax.dot_general(
        weight, values, (((0,), (0,)), ((), ())), preferred_element_type=jnp.float32
    )


KEY_ROWS = 512
KEY_TILES = 5


def key_rows(tile):
    return pl.ds(pl.multiple_of(tile * KEY_ROWS, KEY_ROWS), KEY_ROWS)


def fill_mask(first, last, low, high, mask_scr, index):
    def mask_step(key_tile, carry):
        shape = (KEY_ROWS, low.shape[1])
        place = lax.broadcasted_iota(jnp.int32, shape, 0) + key_tile * KEY_ROWS
        allowed = (place >= low) & (place < high)
        mask_scr[index, key_rows(key_tile - first), :] = jnp.where(allowed, 0.0, NEGATIVE)
        return carry

    lax.fori_loop(first, last, mask_step, 0)


def flash_forward_kernel(
    bounds,
    a_ref,
    b_ref,
    kv_ref,
    low_ref,
    high_ref,
    a_mix,
    b_mix,
    a_wide,
    b_wide,
    lse_ref,
    mask_scr,
    score_scr,
):
    rows, width = a_ref.shape
    pairs = width // 128
    for index in range(2):
        span = slice(index * rows, (index + 1) * rows)
        fill_mask(
            bounds[2 * index],
            bounds[2 * index + 1],
            low_ref[0:1, span],
            high_ref[0:1, span],
            mask_scr,
            index,
        )

    def pair_step(pair, unused):
        lanes = pl.ds(pl.multiple_of(pair * 128, 128), 128)
        value_lanes = pl.ds(pl.multiple_of(pair * 128 + width, 128), 128)
        for index, (q_ref, mix_ref, wide_ref) in enumerate(
            ((a_ref, a_mix, a_wide), (b_ref, b_mix, b_wide))
        ):
            first, last = bounds[2 * index], bounds[2 * index + 1]
            heads = halves_of(q_ref[:, lanes] * jnp.bfloat16(HEAD_SCALE))

            def score_step(key_tile, tops, index=index, heads=heads, first=first):
                keys = kv_ref[key_rows(bounds[4 + key_tile]), lanes]
                place = key_rows(key_tile - first)
                mask = mask_scr[index, place, :]
                out = []
                for head in range(2):
                    scores = turned_dot(keys, heads[head]) + mask
                    score_scr[head, place, :] = scores
                    out.append(jnp.maximum(tops[head], fold_rows(scores, jnp.maximum)))
                return tuple(out)

            floor = jnp.full((8, rows), NEGATIVE, jnp.float32)
            tops = lax.fori_loop(first, last, score_step, (floor, floor))
            tops = [jnp.max(top, axis=0, keepdims=True) for top in tops]

            def mix_step(key_tile, carry, tops=tops, first=first):
                values = kv_ref[key_rows(bounds[4 + key_tile]), value_lanes].T
                totals, mixed = [], []
                for head in range(2):
                    weight = jnp.exp(score_scr[head, key_rows(key_tile - first), :] - tops[head])
                    totals.append(carry[head] + fold_rows(weight, jnp.add))
                    mixed.append(
                        carry[2 + head]
                        + jnp.dot(
                            values[head * 64 : (head + 1) * 64],
                            weight.astype(jnp.bfloat16),
                            preferred_element_type=jnp.float32,
                        )
                    )
                return (totals[0], totals[1], mixed[0], mixed[1])

            zero = jnp.zeros((8, rows), jnp.float32)
            nothing = jnp.zeros((64, rows), jnp.float32)
            carry = lax.fori_loop(first, last, mix_step, (zero, zero, nothing, nothing))
            totals = [jnp.sum(total, axis=0, keepdims=True) for total in carry[:2]]
            mixed = jnp.concatenate(
                [carry[2] * (1.0 / totals[0]), carry[3] * (1.0 / totals[1])], axis=0
            ).T
            wide_ref[:, lanes] = mixed
            mix_ref[:, lanes] = mixed.astype(jnp.bfloat16)
            lse_rows = [tops[head] + jnp.log(totals[head]) for head in range(2)]
            lse_ref[
                pl.ds(pl.multiple_of(pair * 8, 8), 8), index * rows : (index + 1) * rows
            ] = jnp.concatenate([jnp.broadcast_to(line, (4, rows)) for line in lse_rows])
        return unused

    lax.fori_loop(0, pairs, pair_step, 0)


def flash_backward_kernel(
    bounds,
    a_ref,
    b_ref,
    kv_ref,
    a_grad_ref,
    b_grad_ref,
    a_wide,
    b_wide,
    lse_ref,
    low_ref,
    high_ref,
    a_out,
    b_out,
    kv_out,
    mask_scr,
    k_acc,
    v_acc,
):
    rows, width = a_ref.shape
    pairs = width // 128
    tiles = kv_ref.shape[0] // KEY_ROWS
    for index in range(2):
        span = slice(index * rows, (index + 1) * rows)
        fill_mask(
            bounds[2 * index],
            bounds[2 * index + 1],
            low_ref[0:1, span],
            high_ref[0:1, span],
            mask_scr,
            index,
        )

    def pair_step(pair, unused):
        lanes = pl.ds(pl.multiple_of(pair * 128, 128), 128)
        value_lanes = pl.ds(pl.multiple_of(pair * 128 + width, 128), 128)
        lse_rows = lse_ref[pl.ds(pl.multiple_of(pair * 8, 8), 8), :]
        k_acc[...] = jnp.zeros_like(k_acc)
        v_acc[...] = jnp.zeros_like(v_acc)
        ways = (((1,), (1,)), ((), ()))
        for index, (q_ref, grad_ref, wide_ref, q_out) in enumerate(
            ((a_ref, a_grad_ref, a_wide, a_out), (b_ref, b_grad_ref, b_wide, b_out))
        ):
            first, last = bounds[2 * index], bounds[2 * index + 1]
            heads = halves_of(q_ref[:, lanes] * jnp.bfloat16(HEAD_SCALE))
            grads = halves_of(grad_ref[:, lanes])
            turned_q = (q_ref[:, lanes] * jnp.bfloat16(HEAD_SCALE)).T
            turned_grad = grad_ref[:, lanes].T
            span = slice(index * rows, (index + 1) * rows)
            lse = (lse_rows[0:1, span], lse_rows[4:5, span])

            product = (grad_ref[:, lanes].astype(jnp.float32) * wide_ref[:, lanes]).T
            deltas = (
                jnp.sum(product[:64], axis=0, keepdims=True),
                jnp.sum(product[64:], axis=0, keepdims=True),
            )

            def grad_step(
                key_tile,
                q_sum,
                index=index,
                heads=heads,
                grads=grads,
                lse=lse,
                deltas=deltas,
                first=first,
                turned_q=turned_q,
                turned_grad=turned_grad,
            ):
                source = key_rows(bounds[4 + key_tile])
                columns = key_rows(bounds[4 + key_tile])
                keys = kv_ref[source, lanes]
                turned_keys = keys.T
                values = kv_ref[source, value_lanes]
                mask = mask_scr[index, key_rows(key_tile - first), :]
                out = []
                for head in range(2):
                    part = slice(head * 64, (head + 1) * 64)
                    scores = turned_dot(keys, heads[head])
                    slope = turned_dot(values, grads[head])
                    probs = jnp.exp((scores - lse[head]) + mask)
                    low_slope = (probs * (slope - deltas[head])).astype(jnp.bfloat16)
                    v_acc[part, columns] += lax.dot_general(
                        turned_grad[part],
                        probs.astype(jnp.bfloat16),
                        ways,
                        preferred_element_type=jnp.float32,
                    )
                    k_acc[part, columns] += lax.dot_general(
                        turned_q[part], low_slope, ways, preferred_element_type=jnp.float32
                    )
                    out.append(
                        q_sum[head]
                        + jnp.dot(turned_keys[part], low_slope, preferred_element_type=jnp.float32)
                    )
                return tuple(out)

            nothing = jnp.zeros((64, rows), jnp.float32)
            q_parts = lax.fori_loop(first, last, grad_step, (nothing, nothing))
            q_part = jnp.concatenate(q_parts, axis=0).T
            q_out[:, lanes] = (q_part * HEAD_SCALE).astype(jnp.bfloat16)

        def store_step(tile, carry):
            source = key_rows(tile)
            kv_out[source, lanes] = k_acc[:, source].T.astype(jnp.bfloat16)
            kv_out[source, value_lanes] = v_acc[:, source].T.astype(jnp.bfloat16)
            return carry

        lax.fori_loop(0, tiles, store_step, 0)
        return unused

    lax.fori_loop(0, pairs, pair_step, 0)


def whole_block(shape):
    return pl.BlockSpec(shape, lambda i, b: (0,) * len(shape), pipeline_mode=pl.Buffered(1))


def flash_forward(bounds, queries, key_value, low, high):
    rows, width = queries[0].shape
    window = key_value.shape[0]
    pairs = width // 128
    own = whole_block((rows, width))
    line = whole_block((8, 2 * rows))
    return pl.pallas_call(
        flash_forward_kernel,
        out_shape=(
            jax.ShapeDtypeStruct((rows, width), jnp.bfloat16),
            jax.ShapeDtypeStruct((rows, width), jnp.bfloat16),
            jax.ShapeDtypeStruct((rows, width), jnp.float32),
            jax.ShapeDtypeStruct((rows, width), jnp.float32),
            jax.ShapeDtypeStruct((pairs * 8, 2 * rows), jnp.float32),
        ),
        grid_spec=pltpu.PrefetchScalarGridSpec(
            num_scalar_prefetch=1,
            grid=(1,),
            in_specs=[own, own, whole_block((window, 2 * width)), line, line],
            out_specs=[own, own, own, own, whole_block((pairs * 8, 2 * rows))],
            scratch_shapes=[
                pltpu.VMEM((2, KEY_TILES * KEY_ROWS, rows), jnp.float32),
                pltpu.VMEM((2, KEY_TILES * KEY_ROWS, rows), jnp.float32),
            ],
        ),
        compiler_params=pltpu.CompilerParams(vmem_limit_bytes=44 * 2**20),
        cost_estimate=pl.CostEstimate(
            flops=8 * rows * width * 2560, bytes_accessed=12 * 2**20, transcendentals=rows * 12 * 2560
        ),
        name="flash_forward",
    )(bounds, queries[0], queries[1], key_value, low, high)


def flash_backward(bounds, queries, key_value, grads, wides, lse, low, high):
    rows, width = queries[0].shape
    window = key_value.shape[0]
    pairs = width // 128
    own = whole_block((rows, width))
    wide = whole_block((window, 2 * width))
    line = whole_block((8, 2 * rows))
    return pl.pallas_call(
        flash_backward_kernel,
        out_shape=(
            jax.ShapeDtypeStruct((rows, width), jnp.bfloat16),
            jax.ShapeDtypeStruct((rows, width), jnp.bfloat16),
            jax.ShapeDtypeStruct((window, 2 * width), jnp.bfloat16),
        ),
        grid_spec=pltpu.PrefetchScalarGridSpec(
            num_scalar_prefetch=1,
            grid=(1,),
            in_specs=[own, own, wide] + [own] * 4 + [whole_block((pairs * 8, 2 * rows)), line, line],
            out_specs=[own, own, wide],
            scratch_shapes=[
                pltpu.VMEM((2, KEY_TILES * KEY_ROWS, rows), jnp.float32),
                pltpu.VMEM((128, window), jnp.float32),
                pltpu.VMEM((128, window), jnp.float32),
            ],
        ),
        compiler_params=pltpu.CompilerParams(vmem_limit_bytes=56 * 2**20),
        cost_estimate=pl.CostEstimate(
            flops=20 * rows * width * 2560,
            bytes_accessed=20 * 2**20,
            transcendentals=rows * 12 * 2560,
        ),
        name="flash_backward",
    )(bounds, *queries, key_value, *grads, *wides, lse, low, high)


GRP_Y, GRP_CORE, SHARD_Z, SHARD_X = 2, 2, 4, 2
BOTH = ("grp", "shard")


def device_pairs(place):
    pairs = []
    for y in range(GRP_Y):
        for core in range(GRP_CORE):
            for z in range(SHARD_Z):
                for x in range(SHARD_X):
                    target = place(y, core, z, x)
                    if target is not None:
                        ty, tcore, tz, tx = target
                        pairs.append(
                            (
                                (y * GRP_CORE + core) * SHARD_Z * SHARD_X + z * SHARD_X + x,
                                (ty * GRP_CORE + tcore) * SHARD_Z * SHARD_X + tz * SHARD_X + tx,
                            )
                        )
    return pairs


def send(values, place):
    return lax.ppermute(values, BOTH, device_pairs(place))


def turn_rows(values):
    return send(values, lambda y, core, z, x: (y, x, z, core))


def swap_core(values):
    return send(values, lambda y, core, z, x: (y, 1 - core, z, x))


def send_up(values):
    return send(values, lambda y, core, z, x: (y, core, z + 1, x) if z + 1 < SHARD_Z else None)


def send_down(values):
    return send(values, lambda y, core, z, x: (y, core, z - 1, x) if z > 0 else None)


def window_of(rows):
    near = jnp.concatenate([rows, send_up(rows), send_down(rows)])
    return jnp.concatenate([near, swap_core(near)])


def window_back(near, far, count):
    total = near + swap_core(far.astype(jnp.bfloat16)).astype(jnp.float32)
    below = total[count : 2 * count].astype(jnp.bfloat16)
    above = total[2 * count :].astype(jnp.bfloat16)
    return (
        total[:count]
        + send_down(below).astype(jnp.float32)
        + send_up(above).astype(jnp.float32)
    )


def half_of(values, axis, index):
    count = values.shape[axis] // 2
    return lax.dynamic_slice_in_dim(values, index * count, count, axis)


def unpack_kernel(kinds, in_ref, *outs):
    width = in_ref.shape[-1]
    share = in_ref.shape[3]
    place = 0
    for kind, ref in zip(kinds, outs):
        if kind == "columns":
            for column in range(ref.shape[-1] // width):
                ref[:, 0, :, column * width : (column + 1) * width] = in_ref[0, :, place]
                place += 1
        else:
            for piece in range(ref.shape[2] // share):
                ref[:, 0, piece * share : (piece + 1) * share, :] = in_ref[0, :, place]
                place += 1


def unpack_weights_of(pieces, begin_at, places, kinds, shapes):
    quarters, shards, unused, share, width = pieces.shape
    outs = pl.pallas_call(
        functools.partial(unpack_kernel, kinds),
        out_shape=[
            pltpu.HBM((shards, quarters, rows, wide), pieces.dtype) for rows, wide in shapes
        ],
        grid=(quarters,),
        in_specs=[
            pl.BlockSpec(
                (1, shards, places, share, width), lambda q: (q, 0, begin_at // places, 0, 0)
            )
        ],
        out_specs=[
            pl.BlockSpec((shards, 1, rows, wide), lambda q: (0, q, 0, 0)) for rows, wide in shapes
        ],
        compiler_params=pltpu.CompilerParams(vmem_limit_bytes=32 * 2**20),
        cost_estimate=pl.CostEstimate(
            flops=0, bytes_accessed=128 * places * share * width, transcendentals=0
        ),
        name="unpack_weights",
    )(in_main(pieces))
    return [out.reshape(-1, out.shape[-1]) for out in outs]


def pick_kernel(
    me, near_ref, project_ref, mixer_ref, expand_ref, reduce_ref, small_ref, a_out, b_out, c_out
):
    part, half = a_out.shape[-2:]
    for column in range(3):
        begin_at = pl.multiple_of(column * 2 * half + me[1] * half, 128)
        a_out[column] = near_ref[0, :, pl.ds(begin_at, half)]
    a_out[3] = jnp.zeros((part, half), a_out.dtype)
    a_out[3, 0:8, :] = small_ref[:, :half]
    a_out[3, 8:16, :] = small_ref[:, half:]
    share, width = b_out.shape[-2:]
    wide = expand_ref.shape[-1] // width
    for layer, ref in enumerate((b_out, c_out)):
        ref[0] = mixer_ref[layer]
        for column in range(wide):
            ref[1 + column] = expand_ref[layer, :, column * width : (column + 1) * width]
        for piece in range(reduce_ref.shape[1] // share):
            ref[1 + wide + piece] = reduce_ref[layer, piece * share : (piece + 1) * share, :]
    far = c_out.shape[0]
    for column in range(3):
        b_out[far + column] = project_ref[0, :, column * width : (column + 1) * width]


def pick_quarters(me, project, mixer, expand, reduce, small):
    share, width = mixer.shape[1] // 4, mixer.shape[2]
    far = 1 + expand.shape[2] // width + reduce.shape[1] // 4 // share

    def quarter_spec(array):
        return pl.BlockSpec(
            (LAYERS, array.shape[1] // 4, array.shape[2]),
            lambda i, me: (0, me[0] * GRP_CORE + me[1], 0),
        )

    shapes = [(4, 2 * share, width // 2), (far + 3, share, width), (far, share, width)]
    return pl.pallas_call(
        pick_kernel,
        out_shape=[jax.ShapeDtypeStruct(shape, jnp.bfloat16) for shape in shapes],
        grid_spec=pltpu.PrefetchScalarGridSpec(
            num_scalar_prefetch=1,
            grid=(1,),
            in_specs=[
                pl.BlockSpec((1, 2 * share, project.shape[2]), lambda i, me: (0, me[0], 0)),
                pl.BlockSpec(
                    (1, share, project.shape[2]), lambda i, me: (1, me[0] * GRP_CORE + me[1], 0)
                ),
            ]
            + [quarter_spec(array) for array in (mixer, expand, reduce)]
            + [pl.BlockSpec(small.shape, lambda i, me: (0, 0))],
            out_specs=[pl.BlockSpec(shape, lambda i, me: (0, 0, 0)) for shape in shapes],
        ),
        name="pick_quarters",
    )(me, project, project, mixer, expand, reduce, small)


def pack_kernel(kinds, *refs):
    ins, vector_ref, out_ref = refs[:-2], refs[-2], refs[-1]
    width = out_ref.shape[-1]
    share = ins[0].shape[2]
    begin_at = 0
    for kind, ref in zip(kinds, ins):
        if kind == "columns":
            for column in range(ref.shape[-1] // width):
                lanes = slice(column * width, (column + 1) * width)
                out_ref[0, :, begin_at : begin_at + share, :] = ref[:, 0, :, lanes]
                begin_at += share
        else:
            out_ref[0, :, begin_at : begin_at + ref.shape[2], :] = ref[:, 0]
            begin_at += ref.shape[2]
    out_ref[0, :, begin_at : begin_at + 8, :] = vector_ref[0]


def pack_terms(terms, kinds, width, vectors):
    rows = sum(t.size for t in terms) // (32 * width) + 8
    views = [t.reshape(8, 4, -1, t.shape[1]) for t in terms]
    return pl.pallas_call(
        functools.partial(pack_kernel, kinds),
        out_shape=pltpu.HBM((4, 8, rows, width), jnp.bfloat16),
        grid=(4,),
        in_specs=[pl.BlockSpec((8, 1) + view.shape[2:], lambda q: (0, q, 0, 0)) for view in views]
        + [pl.BlockSpec((1,) + vectors.shape[1:], lambda q: (q, 0, 0, 0))],
        out_specs=pl.BlockSpec((1, 8, rows, width), lambda q: (q, 0, 0, 0)),
        compiler_params=pltpu.CompilerParams(vmem_limit_bytes=32 * 2**20),
        cost_estimate=pl.CostEstimate(
            flops=0, bytes_accessed=128 * rows * width, transcendentals=0
        ),
        name="pack_terms",
    )(*[in_main(view) for view in views], vectors)


def swap_y(values):
    return send(values, lambda y, core, z, x: (1 - y, core, z, x))


def swap_x(values):
    return send(values, lambda y, core, z, x: (y, core, z, 1 - x))


def swap_z(values, bit):
    return send(values, lambda y, core, z, x: (y, core, z ^ bit, x))


def spread_kernel(me, q_ref, kv_ref, vector_ref, out_ref):
    part, half = out_ref.shape[-2:]
    for x_bit in range(SHARD_X):
        for z_bits in range(SHARD_Z):
            shard = (z_bits ^ me[3]) * SHARD_X + (x_bit ^ me[2])
            out_ref[0, x_bit, z_bits, 0] = q_ref[shard, 0]
            out_ref[0, x_bit, z_bits, 1] = kv_ref[shard, 0, :, :half]
            out_ref[0, x_bit, z_bits, 2] = kv_ref[shard, 0, :, half:]
            out_ref[0, x_bit, z_bits, 3] = jnp.zeros((part, half), jnp.bfloat16)
            out_ref[0, x_bit, z_bits, 3, 0:8, :] = vector_ref[0, shard]


def spread_terms(me, query_term, key_value_term, vectors):
    half = query_term.shape[1]
    part = query_term.shape[0] // 16
    shape = (GRP_Y, SHARD_X, SHARD_Z, 4, part, half)

    def rows_spec(columns):
        return pl.BlockSpec((8, 1, part, columns), lambda j, me: (0, j ^ me[0], 0, 0))

    return pl.pallas_call(
        spread_kernel,
        out_shape=jax.ShapeDtypeStruct(shape, jnp.bfloat16),
        grid_spec=pltpu.PrefetchScalarGridSpec(
            num_scalar_prefetch=1,
            grid=(2,),
            in_specs=[
                rows_spec(half),
                rows_spec(2 * half),
                pl.BlockSpec((1,) + vectors.shape[1:], lambda j, me: (j ^ me[0], 0, 0, 0)),
            ],
            out_specs=pl.BlockSpec((1,) + shape[1:], lambda j, me: (j, 0, 0, 0, 0, 0)),
        ),
        name="spread_terms",
    )(
        me,
        query_term.reshape(8, 2, part, half),
        key_value_term.reshape(8, 2, part, 2 * half),
        vectors,
    )


def summed(one, other):
    return (one.astype(jnp.float32) + other.astype(jnp.float32)).astype(jnp.bfloat16)


def scatter_terms(a_part, b_part, b_next):
    a_next = swap_y(a_part[1])
    a_last = swap_x(summed(a_part[0, 1], a_next[1]))
    b_last = swap_y(summed(b_part[1, 0], b_next[1]))
    a_keep = summed(a_part[0, 0], a_next[0])
    b_keep = summed(b_part[0, 0], b_next[0])
    whole = jnp.concatenate([a_keep, b_keep], axis=1)
    come = jnp.concatenate([a_last, b_last], axis=1)
    far = swap_z(summed(whole[2:], come[2:]), 2)
    whole = summed(whole[:2], come[:2])
    near = swap_z(summed(whole[1], far[1]), 1)
    return summed(summed(whole[0], far[0]), near)


def gather_quarters(piece):
    pair = jnp.stack([piece, swap_y(piece)])
    return jnp.stack([pair, swap_core(pair)])


def finish_kernel(me, *refs):
    layers = len(refs) // 2 - 3
    outs = refs[2 * layers :]

    def fill(near_ref, far_ref):
        part, half = near_ref.shape[-2:]
        share, width = part // 2, 2 * half
        for y_bit in range(GRP_Y):
            for core_bit in range(GRP_CORE):
                y = y_bit ^ me[0]
                core = core_bit ^ me[1]
                quarter = y * GRP_CORE + core
                for column in range(3):
                    lanes = pl.ds(pl.multiple_of(column * 2 * half + core * half, 128), half)
                    outs[0][0, y, :, lanes] = near_ref[core_bit, y_bit, column].astype(jnp.float32)
                outs[4][0, quarter] = near_ref[core_bit, y_bit, 3, 0:8, :].astype(jnp.float32)
                pieces = far_ref.at[core_bit, y_bit]
                outs[1][0, quarter] = pieces[:share, :].astype(jnp.float32)
                begin_at = share
                for column in range(outs[2].shape[-1] // width):
                    lanes = slice(column * width, (column + 1) * width)
                    rows = slice(begin_at, begin_at + share)
                    outs[2][0, quarter, :, lanes] = pieces[rows, :].astype(jnp.float32)
                    begin_at += share
                deep = outs[3].shape[2]
                outs[3][0, quarter] = pieces[begin_at : begin_at + deep, :].astype(jnp.float32)
                begin_at += deep
                outs[5][0, quarter] = pieces[begin_at : begin_at + 8, :].astype(jnp.float32)

    for layer in range(layers):
        pl.when(pl.program_id(0) == layer)(
            functools.partial(fill, refs[2 * layer], refs[2 * layer + 1])
        )


def finish_shares(me, shares, hidden_units, deep):
    layers = len(shares)
    part, half = shares[0][0].shape[-2:]
    share, width = part // 2, 2 * half
    shapes = [
        (2, part, 3 * width),
        (4, share, width),
        (4, share, hidden_units),
        (4, deep, width),
        (4, 8, half),
        (4, 8, width),
    ]
    flat = [array for pair in shares for array in pair]
    outs = pl.pallas_call(
        finish_kernel,
        out_shape=[jax.ShapeDtypeStruct((layers,) + shape, jnp.float32) for shape in shapes],
        grid_spec=pltpu.PrefetchScalarGridSpec(
            num_scalar_prefetch=1,
            grid=(layers,),
            in_specs=[whole_block(array.shape) for array in flat],
            out_specs=[
                pl.BlockSpec((1,) + shape, lambda i, me: (i, 0, 0, 0)) for shape in shapes
            ],
        ),
        compiler_params=pltpu.CompilerParams(vmem_limit_bytes=32 * 2**20),
        name="finish_shares",
    )(me, *flat)
    return [out.reshape(layers, -1, out.shape[-1]) for out in outs[:4]] + list(outs[4:])


def row_mean(values):
    return jnp.mean(values, axis=1, keepdims=True)


def column_sum(values):
    return jnp.sum(values, axis=0, keepdims=True)


def standardized(values):
    centered = values - row_mean(values)
    scale = lax.rsqrt(row_mean(centered * centered) + EPSILON)
    return centered * scale, scale


def standard_back(grad, norm, scale, gain):
    weighted = grad * gain
    return (weighted - row_mean(weighted) - norm * row_mean(weighted * norm)) * scale


def tail_forward_kernel(
    me,
    own_ref,
    far_ref,
    state_ref,
    mixer_ref,
    expand_ref,
    reduce_ref,
    bias_in_ref,
    vector_ref,
    mix_out,
    norm_one_out,
    scale_one_out,
    low_out,
    active_out,
    slope_out,
    norm_two_out,
    scale_two_out,
    state_out,
    state_low_out,
    wide_scr,
    total_scr,
):
    step = pl.program_id(0)
    half = own_ref.shape[1]

    @pl.when(step == 0)
    def begin():
        mix_out[:, pl.ds(pl.multiple_of(me[1] * half, 128), half)] = own_ref[...]
        mix_out[:, pl.ds(pl.multiple_of((1 - me[1]) * half, 128), half)] = far_ref[...]
        branch = jnp.dot(mix_out[...], mixer_ref[...], preferred_element_type=jnp.float32)
        norm, scale = standardized(state_ref[...].astype(jnp.float32) + (branch + vector_ref[0:1]))
        norm_one_out[...] = norm
        scale_one_out[...] = jnp.broadcast_to(scale, scale_one_out.shape)
        wide = norm * vector_ref[1:2] + vector_ref[2:3]
        wide_scr[...] = wide
        low_out[...] = wide.astype(jnp.bfloat16)
        total_scr[...] = jnp.zeros_like(total_scr)

    before = (
        jnp.dot(low_out[...], expand_ref[...], preferred_element_type=jnp.float32)
        + bias_in_ref[...]
    )
    normal = 0.5 * (1.0 + lax.erf(before * 0.7071067811865476))
    density = jnp.exp(before * before * -0.5) * 0.3989422804014327
    active = (before * normal).astype(jnp.bfloat16)
    active_out[...] = active
    slope_out[...] = normal + before * density
    total_scr[...] += jnp.dot(active, reduce_ref[...], preferred_element_type=jnp.float32)

    @pl.when(step == pl.num_programs(0) - 1)
    def end():
        norm, scale = standardized(wide_scr[...] + (total_scr[...] + vector_ref[3:4]))
        norm_two_out[...] = norm
        scale_two_out[...] = jnp.broadcast_to(scale, scale_two_out.shape)
        state = norm * vector_ref[4:5] + vector_ref[5:6]
        state_out[...] = state
        state_low_out[...] = state.astype(jnp.bfloat16)


FEED_TILE = 512


def tail_forward(me, own_mix, far_mix, state, mixer, expand, reduce, bias_in, vectors):
    rows, width = state.shape
    hidden_units = expand.shape[1]
    steps = hidden_units // FEED_TILE
    whole = whole_block((rows, width))
    halves = whole_block((rows, width // 2))
    scale = whole_block((rows, 128))
    tile = pl.BlockSpec((rows, FEED_TILE), lambda j, me: (0, j))

    def shaped(columns, kind):
        return jax.ShapeDtypeStruct((rows, columns), kind)

    return pl.pallas_call(
        tail_forward_kernel,
        out_shape=[
            shaped(width, jnp.bfloat16),
            shaped(width, jnp.float32),
            shaped(128, jnp.float32),
            shaped(width, jnp.bfloat16),
            shaped(hidden_units, jnp.bfloat16),
            shaped(hidden_units, jnp.float32),
            shaped(width, jnp.float32),
            shaped(128, jnp.float32),
            shaped(width, jnp.float32),
            shaped(width, jnp.bfloat16),
        ],
        grid_spec=pltpu.PrefetchScalarGridSpec(
            num_scalar_prefetch=1,
            grid=(steps,),
            in_specs=[
                halves,
                halves,
                whole,
                whole_block((width, width)),
                pl.BlockSpec((width, FEED_TILE), lambda j, me: (0, j)),
                pl.BlockSpec((FEED_TILE, width), lambda j, me: (j, 0)),
                pl.BlockSpec((1, FEED_TILE), lambda j, me: (0, j)),
                whole_block((8, width)),
            ],
            out_specs=[whole, whole, scale, whole, tile, tile, whole, scale, whole, whole],
            scratch_shapes=[
                pltpu.VMEM((rows, width), jnp.float32),
                pltpu.VMEM((rows, width), jnp.float32),
            ],
        ),
        compiler_params=pltpu.CompilerParams(vmem_limit_bytes=44 * 2**20),
        cost_estimate=pl.CostEstimate(
            flops=2 * rows * width * (width + 2 * hidden_units),
            bytes_accessed=32 * 2**20,
            transcendentals=2 * rows * hidden_units,
        ),
        name="tail_forward",
    )(me, own_mix, far_mix, state, mixer, expand, reduce, bias_in, vectors)


def tail_backward_kernel(
    me,
    grad_ref,
    norm_two_ref,
    scale_two_ref,
    norm_one_ref,
    scale_one_ref,
    low_ref,
    mix_ref,
    slope_ref,
    active_ref,
    expand_ref,
    reduce_ref,
    mixer_ref,
    vector_ref,
    sum_out,
    own_out,
    far_out,
    mixer_out,
    expand_out,
    reduce_out,
    bias_in_out,
    vector_out,
    wide_scr,
    feed_scr,
    total_scr,
):
    step = pl.program_id(0)
    half = own_out.shape[1]

    @pl.when(step == 0)
    def begin():
        grad = grad_ref[...]
        norm = norm_two_ref[...]
        wide = standard_back(grad, norm, scale_two_ref[:, 0:1], vector_ref[4:5])
        wide_scr[...] = wide
        feed = wide.astype(jnp.bfloat16)
        feed_scr[...] = feed
        vector_out[...] = jnp.zeros_like(vector_out)
        vector_out[3:4] = column_sum(feed.astype(jnp.float32))
        vector_out[4:5] = column_sum(grad * norm)
        vector_out[5:6] = column_sum(grad)
        total_scr[...] = jnp.zeros_like(total_scr)

    feed = feed_scr[...]
    active_grad = turned_dot(feed, reduce_ref[...])
    before = (active_grad * slope_ref[...]).astype(jnp.bfloat16)
    bias_in_out[...] = column_sum(before.astype(jnp.float32))
    reduce_out[...] = across_dot(active_ref[...], feed).astype(jnp.bfloat16)
    expand_out[...] = across_dot(low_ref[...], before).astype(jnp.bfloat16)
    total_scr[...] += turned_dot(before, expand_ref[...])

    @pl.when(step == pl.num_programs(0) - 1)
    def end():
        grad = wide_scr[...] + total_scr[...]
        norm = norm_one_ref[...]
        wide = standard_back(grad, norm, scale_one_ref[:, 0:1], vector_ref[1:2])
        sum_out[...] = wide
        branch = wide.astype(jnp.bfloat16)
        vector_out[0:1] = column_sum(branch.astype(jnp.float32))
        vector_out[1:2] = column_sum(grad * norm)
        vector_out[2:3] = column_sum(grad)
        mixer_out[...] = across_dot(mix_ref[...], branch).astype(jnp.bfloat16)
        mixed = turned_dot(branch, mixer_ref[...]).astype(jnp.bfloat16)
        total_scr[...] = mixed.astype(jnp.float32)
        own = total_scr[:, pl.ds(pl.multiple_of(me[1] * half, 128), half)]
        far = total_scr[:, pl.ds(pl.multiple_of((1 - me[1]) * half, 128), half)]
        own_out[...] = own.astype(jnp.bfloat16)
        far_out[...] = far.astype(jnp.bfloat16)


def tail_backward(me, grad, kept, weights, vectors):
    norm_two, scale_two, norm_one, scale_one, low, mixed, slope, active = kept
    mixer, expand, reduce = weights
    rows, width = grad.shape
    hidden_units = expand.shape[1]
    steps = hidden_units // FEED_TILE
    whole = whole_block((rows, width))
    halves = whole_block((rows, width // 2))
    scale = whole_block((rows, 128))
    square = whole_block((width, width))
    tile = pl.BlockSpec((rows, FEED_TILE), lambda j, me: (0, j))
    across = pl.BlockSpec((width, FEED_TILE), lambda j, me: (0, j))
    down = pl.BlockSpec((FEED_TILE, width), lambda j, me: (j, 0))
    line = pl.BlockSpec((1, FEED_TILE), lambda j, me: (0, j))

    def shaped(rows, columns, kind):
        return jax.ShapeDtypeStruct((rows, columns), kind)

    return pl.pallas_call(
        tail_backward_kernel,
        out_shape=[
            shaped(rows, width, jnp.float32),
            shaped(rows, width // 2, jnp.bfloat16),
            shaped(rows, width // 2, jnp.bfloat16),
            shaped(width, width, jnp.bfloat16),
            shaped(width, hidden_units, jnp.bfloat16),
            shaped(hidden_units, width, jnp.bfloat16),
            shaped(1, hidden_units, jnp.float32),
            shaped(8, width, jnp.float32),
        ],
        grid_spec=pltpu.PrefetchScalarGridSpec(
            num_scalar_prefetch=1,
            grid=(steps,),
            in_specs=[whole, whole, scale, whole, scale, whole, whole, tile, tile, across, down]
            + [square, whole_block((8, width))],
            out_specs=[whole, halves, halves, square, across, down, line, whole_block((8, width))],
            scratch_shapes=[
                pltpu.VMEM((rows, width), jnp.float32),
                pltpu.VMEM((rows, width), jnp.bfloat16),
                pltpu.VMEM((rows, width), jnp.float32),
            ],
        ),
        compiler_params=pltpu.CompilerParams(vmem_limit_bytes=48 * 2**20),
        cost_estimate=pl.CostEstimate(
            flops=2 * rows * width * (2 * width + 4 * hidden_units),
            bytes_accessed=40 * 2**20,
            transcendentals=0,
        ),
        name="tail_backward",
    )(
        me,
        grad,
        norm_two,
        scale_two,
        norm_one,
        scale_one,
        low,
        mixed,
        slope,
        active,
        expand,
        reduce,
        mixer,
        vectors,
    )


def gather_all(local):
    places, share, width = local.shape
    gathered = lax.all_gather(local.reshape(-1, width), BOTH, axis=0, tiled=False)
    return gathered.reshape(4, 8, places, share, width)


def join_kernel(me, a_ref, b_ref, project_ref, small_ref):
    half = a_ref.shape[-1]
    for y_bit in range(GRP_Y):
        y = y_bit ^ me[0]
        for x_bit in range(SHARD_X):
            for z_bits in range(SHARD_Z):
                shard = (z_bits ^ me[3]) * SHARD_X + (x_bit ^ me[2])
                project_ref[shard, y, :, :half] = a_ref[y_bit, x_bit, z_bits, 0]
                project_ref[shard, y, :, half : 2 * half] = a_ref[y_bit, x_bit, z_bits, 1]
                project_ref[shard, y, :, 2 * half :] = b_ref[x_bit, y_bit, z_bits, 0]
                if y_bit == 0:
                    small_ref[shard, :, :half] = b_ref[x_bit, y_bit, z_bits, 1, 0:8, :]
                    small_ref[shard, :, half:] = b_ref[x_bit, y_bit, z_bits, 1, 8:16, :]


def gather_first(me, local, rows):
    part, half = local.shape[1:]
    pair = jnp.stack([local, swap_z(local, 1)])
    pair, rows = lax.optimization_barrier((pair, rows))
    window = window_of(rows)
    four = jnp.concatenate([pair, swap_z(pair, 2)])
    a_part, b_part = four[:, :2], four[:, 2:]
    a_two = jnp.stack([a_part, swap_x(a_part)])
    b_two = jnp.stack([b_part, swap_y(b_part)])
    a_four = jnp.stack([a_two, swap_y(a_two)])
    b_four = jnp.stack([b_two, swap_x(b_two)])
    project, small = pl.pallas_call(
        join_kernel,
        out_shape=[
            jax.ShapeDtypeStruct((8, 2, part, 3 * half), local.dtype),
            jax.ShapeDtypeStruct((8, 8, 2 * half), local.dtype),
        ],
        grid_spec=pltpu.PrefetchScalarGridSpec(
            num_scalar_prefetch=1,
            grid=(1,),
            in_specs=[whole_block(a_four.shape)] * 2,
            out_specs=[whole_block((8, 2, part, 3 * half)), whole_block((8, 8, 2 * half))],
        ),
        compiler_params=pltpu.CompilerParams(vmem_limit_bytes=24 * 2**20),
        name="join_projection",
    )(me, a_four, b_four)
    return project.reshape(-1, 3 * half), small, four, rows, window


def on_device_turned(
    tokens,
    cotangent,
    seq_lengths,
    seq_order,
    w_project,
    w_mixer,
    w_expand,
    w_reduce,
    biases,
    norm_gains,
):
    row_count, width = tokens.shape
    shard_index = lax.axis_index("shard")
    quarter = lax.axis_index("grp")
    z, x = shard_index // SHARD_X, shard_index % SHARD_X
    y, core = quarter // GRP_CORE, quarter % GRP_CORE
    me = jnp.stack([y, core, x, z]).astype(jnp.int32)
    hidden_units = w_expand.shape[2]
    group_slots = row_count * 8
    seq_count = seq_lengths.shape[1]
    seq_ends = group_ends(seq_lengths, seq_order, y * GRP_CORE + x)
    block_index = z * GRP_CORE + jnp.stack([core, 1 - core])
    slot_index = block_index[:, None] * row_count + jnp.arange(row_count, dtype=jnp.int32)[None, :]
    slot_index = slot_index.reshape(-1)
    before_slot = seq_ends[None, :] <= slot_index[:, None]
    own_segment = jnp.sum(before_slot[:row_count].astype(jnp.int32), axis=1, dtype=jnp.int32)
    starts = jnp.max(jnp.where(before_slot, seq_ends[None, :], 0), axis=1)
    stops = jnp.min(jnp.where(before_slot, group_slots, seq_ends[None, :]), axis=1)
    window_begin = (z - 1) * GRP_CORE * row_count
    low = starts - window_begin
    high = stops - window_begin
    low_line = jnp.broadcast_to(low[None, :], (8, 2 * row_count))
    high_line = jnp.broadcast_to(high[None, :], (8, 2 * row_count))
    places = [(1, 0, 2)[t // 2] + ((t % 2) ^ core) * 3 for t in range(6)]
    bounds = jnp.stack(
        [
            low[0] // KEY_ROWS,
            (high[row_count - 1] + KEY_ROWS - 1) // KEY_ROWS,
            low[row_count] // KEY_ROWS,
            (high[2 * row_count - 1] + KEY_ROWS - 1) // KEY_ROWS,
        ]
        + places
    ).astype(jnp.int32)
    valid_rows = (own_segment < seq_count).astype(jnp.float32)[:, None]

    small = jnp.concatenate(
        [jnp.concatenate([biases[i], norm_gains[i]]) for i in range(LAYERS)]
    ).reshape(-1, width)
    share = w_project.shape[1] // 4
    deep = w_reduce.shape[1] // 4
    bias_count = biases.shape[1]
    small_rows = small.shape[0]
    small = jnp.concatenate([small, jnp.zeros((8 - small_rows, width), small.dtype)])
    near_first, far_first, far_last = pick_quarters(
        me, w_project, w_mixer, w_expand, w_reduce, small
    )
    state_low = turn_rows(tokens)
    state_grad = turn_rows(cotangent)
    project_first, small_all, arrived, state_low, first_window = gather_first(
        me, near_first, state_low
    )
    far_first, arrived = lax.optimization_barrier((far_first, arrived))
    far_kinds = ("columns", "columns", "rows")
    far_shapes = [(share, width), (share, hidden_units), (deep, width)]
    far_count = far_last.shape[0]
    pieces = gather_all(far_first)
    first_whole = [project_first] + unpack_weights_of(pieces, 0, far_count, far_kinds, far_shapes)
    project_last = unpack_weights_of(pieces, far_count, 3, ("columns",), [(share, 3 * width)])[0]
    project_last = jnp.concatenate(
        [half_of(project_last[:, i * width : (i + 1) * width], 1, core) for i in range(3)], axis=1
    )
    last_whole = [project_last] + unpack_weights_of(
        gather_all(far_last), 0, far_count, far_kinds, far_shapes
    )
    small_all = small_all[:, :small_rows].reshape(8, LAYERS, -1)
    weights = []
    for layer_index, whole in enumerate([first_whole, last_whole]):
        bias_vec = small_all[:, layer_index, :bias_count].reshape(-1)
        gain_vec = small_all[:, layer_index, bias_count:].reshape(-1)
        weights.append(unpack_weights(whole + [bias_vec, gain_vec], width, hidden_units))

    hidden_state = state_low.astype(jnp.float32)
    kept_list = []
    for layer_index in range(LAYERS):
        project, mixing, expand, shrink, bias_list, gain_one, gain_two = weights[layer_index]
        bias_q, bias_v, bias_mix, shift_one, bias_in, bias_out, shift_two = bias_list
        state_window = first_window if layer_index == 0 else window_of(state_low)
        half = width // 2
        far_begin = 3 * row_count
        queries = [
            (
                jnp.dot(
                    state_window[begin_at : begin_at + row_count],
                    project[:, :half],
                    preferred_element_type=jnp.float32,
                )
                + half_of(bias_q, 0, core)
            ).astype(jnp.bfloat16)
            for begin_at in (0, far_begin)
        ]
        key_value = (
            jnp.dot(state_window, project[:, half:], preferred_element_type=jnp.float32)
            + jnp.concatenate([jnp.zeros((half,), jnp.float32), half_of(bias_v, 0, core)])
        ).astype(jnp.bfloat16)
        own_mix, far_mix, own_wide, far_wide, lse = flash_forward(bounds, queries, key_value, low_line, high_line)
        far_mix = swap_core(far_mix)
        tail_vectors = jnp.stack(
            [bias_mix, gain_one, shift_one, bias_out, gain_two, shift_two, bias_mix, bias_mix]
        )
        (
            mixed_low,
            norm_one,
            scale_one,
            normed_low,
            active_low,
            slope,
            norm_two,
            scale_two,
            hidden_state,
            next_low,
        ) = tail_forward(
            me, own_mix, far_mix, hidden_state, mixing, expand, shrink, bias_in[None], tail_vectors
        )
        kept_list.append(
            (
                state_low,
                state_window,
                queries,
                key_value,
                (own_wide, far_wide),
                lse,
                (norm_two, scale_two, norm_one, scale_one, normed_low, mixed_low, slope, active_low),
                tail_vectors,
            )
        )
        state_low = next_low
    activations = turn_rows((hidden_state * valid_rows).astype(jnp.bfloat16))
    state_grad = state_grad.astype(jnp.float32) * valid_rows
    results = [None] * LAYERS
    spreads = [None] * LAYERS
    for layer_index in reversed(range(LAYERS)):
        layer_low, state_window, queries, key_value, wides, lse, kept, tail_vectors = kept_list[
            layer_index
        ]
        project, mixing, expand, shrink, *unused = weights[layer_index]
        (
            sum_one_grad,
            own_mix_grad,
            far_mix_grad,
            mixing_grad,
            expand_grad,
            shrink_grad,
            bias_in_grad,
            vector_grads,
        ) = tail_backward(me, state_grad, kept, (mixing, expand, shrink), tail_vectors)
        bias_mix_grad, gain_one_grad, shift_one_grad, bias_out_grad, gain_two_grad, shift_two_grad = [
            vector_grads[i] for i in range(6)
        ]
        mixed_grads = (own_mix_grad, swap_core(far_mix_grad))
        own_grad, far_grad, key_value_grad = flash_backward(
            bounds, queries, key_value, mixed_grads, wides, lse, low_line, high_line
        )
        if layer_index == 0:
            key_value_grad, started = lax.optimization_barrier((key_value_grad, started))
        query_term = jnp.einsum(
            "td,te->de", layer_low, own_grad, preferred_element_type=jnp.float32
        ) + jnp.einsum(
            "td,te->de",
            state_window[far_begin : far_begin + row_count],
            far_grad,
            preferred_element_type=jnp.float32,
        )
        key_value_term = jnp.einsum(
            "td,te->de", state_window, key_value_grad, preferred_element_type=jnp.float32
        )
        bias_q_grad = jnp.sum(own_grad, axis=0, dtype=jnp.float32) + jnp.sum(
            far_grad, axis=0, dtype=jnp.float32
        )
        bias_v_grad = jnp.sum(key_value_grad[:, half:], axis=0, dtype=jnp.float32)
        window_grad = jnp.einsum(
            "te,de->td", key_value_grad, project[:, half:], preferred_element_type=jnp.float32
        )
        own_part = jnp.einsum(
            "te,de->td", own_grad, project[:, :half], preferred_element_type=jnp.float32
        )
        far_part = jnp.einsum(
            "te,de->td", far_grad, project[:, :half], preferred_element_type=jnp.float32
        )
        near_terms = jnp.concatenate(
            [window_grad[:row_count] + own_part, window_grad[row_count:far_begin]]
        )
        far_terms = jnp.concatenate(
            [
                window_grad[far_begin : far_begin + row_count] + far_part,
                window_grad[far_begin + row_count :],
            ]
        )
        state_grad = sum_one_grad + window_back(near_terms, far_terms, row_count)
        zeros_two = jnp.zeros((2 * width,), jnp.float32)
        vectors = jnp.concatenate(
            [
                zeros_two,
                bias_mix_grad,
                shift_one_grad,
                bias_in_grad[0],
                bias_out_grad,
                shift_two_grad,
            ]
        ).reshape(8, -1)
        gains = jnp.concatenate([gain_one_grad, gain_two_grad]).reshape(8, -1)
        vectors = jnp.concatenate([vectors, gains], axis=1).astype(jnp.bfloat16)
        vectors = vectors.reshape(8, 4, 1, -1).transpose(1, 0, 2, 3)
        vectors = jnp.pad(vectors, ((0, 0), (0, 0), (0, 7), (0, width - vectors.shape[3])))
        terms = (mixing_grad, expand_grad, shrink_grad)
        pieces = pack_terms(terms, far_kinds, width, vectors)
        fed = lax.psum_scatter(
            pieces.reshape(32, -1, width), BOTH, scatter_dimension=0, tiled=True
        )[0]
        lines = jnp.zeros((8 * bias_count,), jnp.float32)
        lines = lax.dynamic_update_slice(lines, bias_q_grad, (core * half,))
        lines = lax.dynamic_update_slice(lines, bias_v_grad, (width + core * half,))
        lines = lines.reshape(8, 2, -1).transpose(1, 0, 2).astype(jnp.bfloat16)
        lines = jnp.pad(lines, ((0, 0), (0, 0), (0, width - lines.shape[2])))
        lines = jnp.pad(lines.reshape(2, 8, 2, half), ((0, 0), (0, 0), (0, 6), (0, 0)))
        query_term = query_term.astype(jnp.bfloat16)
        key_value_term = key_value_term.astype(jnp.bfloat16)
        if layer_index > 0:
            state_grad, query_term, key_value_term = lax.optimization_barrier(
                (state_grad, query_term, key_value_term)
            )
        spreads[layer_index] = spread_terms(me, query_term, key_value_term, lines)
        if layer_index > 0:
            started = swap_x(spreads[layer_index][:, 1])
        results[layer_index] = gather_quarters(fed)
    attended = gather_quarters(scatter_terms(*spreads, started))
    results = [
        (attended[:, :, 4 * layer_index : 4 * (layer_index + 1)], results[layer_index])
        for layer_index in range(LAYERS)
    ]
    outs = finish_shares(me, results, hidden_units, deep)
    quarter_len = (bias_count + norm_gains.shape[1]) // 4
    vectors = outs[5][:, :, 0, :quarter_len].reshape(LAYERS, -1)
    lines = outs[4][:, :, :2].reshape(LAYERS, GRP_Y, GRP_CORE, width)[..., : bias_count // 2]
    lines = jnp.sum(lines, axis=2).reshape(LAYERS, bias_count)
    input_grad = turn_rows(state_grad.astype(jnp.bfloat16)).astype(jnp.float32)
    return (
        activations,
        input_grad,
        outs[0],
        outs[1],
        outs[2],
        outs[3],
        vectors[:, :bias_count] + lines,
        vectors[:, bias_count:],
    )


def solution(mesh):
    in_specs = (
        P(("grp", "shard"), None),
        P(("grp", "shard"), None),
        P(),
        P(),
        P(None, "shard", None),
        P(None, "shard", None),
        P(None, "shard", None),
        P(None, "shard", None),
        P(None, "shard"),
        P(None, "shard"),
    )
    out_specs = (
        P(("grp", "shard"), None),
        P(("grp", "shard"), None),
        P(None, "shard", None),
        P(None, "shard", None),
        P(None, "shard", None),
        P(None, "shard", None),
        P(None, "shard"),
        P(None, "shard"),
    )
    body = on_device_turned if mesh.shape["shard"] == 8 and mesh.shape["grp"] == 4 else on_device
    return jax.shard_map(
        body, mesh=mesh, in_specs=in_specs, out_specs=out_specs, check_vma=False
    )
```

```python
import functools

import jax
import jax.numpy as jnp
from jax import lax
from jax.experimental import pallas as pl
from jax.experimental.pallas import tpu as pltpu
from jax.sharding import PartitionSpec as P

HEADS = 12
LAYERS = 2
SEQ_MAX = 2048


EPSILON = 1e-12
NEGATIVE = -1e30


def passed_along(shard, axis, by):
    size = lax.axis_size(axis)
    pairs = [(i, i + by) for i in range(size) if 0 <= i + by < size]
    return lax.ppermute(shard, axis, pairs)


def layer_norm(values, gain, shift):
    middle = jnp.mean(values, axis=-1, keepdims=True)
    centered = values - middle
    spread = jnp.mean(centered * centered, axis=-1, keepdims=True)
    return centered * lax.rsqrt(spread + EPSILON) * gain + shift


def gelu_exact(values):
    return jax.nn.gelu(values, approximate=False)


def keep_same(carried):
    return carried


def group_ends(seq_lengths, seq_order, group_index):
    lengths_row = lax.dynamic_index_in_dim(seq_lengths, group_index, 0, keepdims=False)
    order_row = lax.dynamic_index_in_dim(seq_order, group_index, 0, keepdims=False)
    places = jnp.arange(lengths_row.shape[0], dtype=jnp.int32)
    picked = order_row[:, None] == places[None, :]
    placed = jnp.sum(jnp.where(picked, lengths_row[None, :], 0), axis=1, dtype=jnp.int32)
    return jnp.cumsum(placed, dtype=jnp.int32)


def slot_segments(slot_index, seq_ends):
    flattened = slot_index.reshape(-1)
    counted = jnp.sum(
        (seq_ends[None, :] <= flattened[:, None]).astype(jnp.int32), axis=1, dtype=jnp.int32
    )
    return counted.reshape(slot_index.shape)


def unpack_weights(weights, width, hidden_units):
    bias_vec = weights[4].astype(jnp.float32)
    gain_vec = weights[5].astype(jnp.float32)
    piece_lens = [width, width, width, width, hidden_units, width, width]
    bias_list = []
    begin_at = 0
    for piece_len in piece_lens:
        bias_list.append(bias_vec[begin_at : begin_at + piece_len])
        begin_at = begin_at + piece_len
    return (
        weights[0],
        weights[1],
        weights[2],
        weights[3],
        bias_list,
        gain_vec[:width],
        gain_vec[width:],
    )


def block_probs(queries, keys_block, seg_block, own_segment, log_total, score_scale):
    raw_scores = jnp.einsum("qhd,khd->hqk", queries, keys_block, preferred_element_type=jnp.float32)
    allowed = (own_segment[:, None] == seg_block[None, :])[None]
    return jnp.where(allowed, jnp.exp(raw_scores * score_scale - log_total[:, :, None]), 0.0)


def gather_window(key_rows, value_rows, reach_blocks):
    key_list = []
    value_list = []
    for step_offset in range(-reach_blocks, reach_blocks + 1):
        if step_offset == 0:
            moved = (key_rows, value_rows)
        else:
            moved = passed_along((key_rows, value_rows), "shard", -step_offset)
        key_list.append(moved[0])
        value_list.append(moved[1])
    return (jnp.stack(key_list), jnp.stack(value_list))


def return_parts(key_parts, value_parts, reach_blocks):
    key_total = key_parts[reach_blocks]
    value_total = value_parts[reach_blocks]
    for step_offset in range(-reach_blocks, reach_blocks + 1):
        if step_offset != 0:
            arrived = (
                passed_along(
                    key_parts[step_offset + reach_blocks].astype(jnp.bfloat16), "shard", step_offset
                ).astype(jnp.float32),
                passed_along(
                    value_parts[step_offset + reach_blocks].astype(jnp.bfloat16),
                    "shard",
                    step_offset,
                ).astype(jnp.float32),
            )
            key_total = key_total + arrived[0]
            value_total = value_total + arrived[1]
    return (key_total, value_total)


def attend_forward(
    queries, window_keys, window_values, window_segment, live_block, own_segment, score_scale
):
    row_count, head_count, head_dim = queries.shape

    def stats_step(carry, items):
        keys_block, seg_block, alive = items

        def stats_compute(state_pair):
            running_top, running_sum = state_pair
            allowed = (own_segment[:, None] == seg_block[None, :])[None]
            raw_scores = jnp.einsum(
                "qhd,khd->hqk", queries, keys_block, preferred_element_type=jnp.float32
            )
            scores = jnp.where(allowed, raw_scores * score_scale, NEGATIVE)
            new_top = jnp.maximum(running_top, jnp.max(scores, axis=-1))
            weighted = jnp.where(allowed, jnp.exp(scores - new_top[:, :, None]), 0.0)
            return (
                new_top,
                running_sum * jnp.exp(running_top - new_top) + jnp.sum(weighted, axis=-1),
            )

        return (lax.cond(alive, stats_compute, keep_same, carry), None)

    begin_stats = (
        jnp.full((head_count, row_count), NEGATIVE, jnp.float32),
        jnp.zeros((head_count, row_count), jnp.float32),
    )
    (running_top, running_sum), unused = lax.scan(
        stats_step, begin_stats, (window_keys, window_segment, live_block)
    )
    log_total = running_top + jnp.log(running_sum)

    def mix_step(carry, items):
        keys_block, values_block, seg_block, alive = items

        def mix_compute(state_pair):
            mixed, extra = state_pair
            probs = block_probs(queries, keys_block, seg_block, own_segment, log_total, score_scale)
            probs_low = probs.astype(jnp.bfloat16)
            rest_low = (probs - lax.optimization_barrier(probs_low).astype(jnp.float32)).astype(
                jnp.bfloat16
            )
            mixed = mixed + jnp.einsum(
                "hqk,khd->qhd", probs_low, values_block, preferred_element_type=jnp.float32
            )
            extra = extra + jnp.einsum(
                "hqk,khd->qhd", rest_low, values_block, preferred_element_type=jnp.float32
            )
            return (mixed, extra)

        return (lax.cond(alive, mix_compute, keep_same, carry), None)

    zeros_mix = jnp.zeros((row_count, head_count, head_dim), jnp.float32)
    (mixed, extra), unused = lax.scan(
        mix_step, (zeros_mix, zeros_mix), (window_keys, window_values, window_segment, live_block)
    )
    return (log_total, mixed, mixed + extra)


def attend_backward(
    queries,
    window_keys,
    window_values,
    window_segment,
    live_block,
    own_segment,
    log_total,
    delta,
    grad_low,
    score_scale,
):

    def grad_step(query_grad, items):
        keys_block, values_block, seg_block, alive = items

        def grad_compute(carried):
            probs = block_probs(queries, keys_block, seg_block, own_segment, log_total, score_scale)
            prob_grad = jnp.einsum(
                "qhd,khd->hqk", grad_low, values_block, preferred_element_type=jnp.float32
            )
            score_low = (probs * (prob_grad - delta[:, :, None])).astype(jnp.bfloat16)
            carried = carried + jnp.einsum(
                "hqk,khd->qhd", score_low, keys_block, preferred_element_type=jnp.float32
            )
            probs_low = probs.astype(jnp.bfloat16)
            value_part = jnp.einsum(
                "hqk,qhd->khd", probs_low, grad_low, preferred_element_type=jnp.float32
            )
            key_part = jnp.einsum(
                "hqk,qhd->khd", score_low, queries, preferred_element_type=jnp.float32
            )
            return (carried, (key_part, value_part))

        def skipped(carried):
            nothing = jnp.zeros(keys_block.shape, jnp.float32)
            return (carried, (nothing, nothing))

        return lax.cond(alive, grad_compute, skipped, query_grad)

    zero_grad = jnp.zeros(queries.shape, jnp.float32)
    query_grad, key_value = lax.scan(
        grad_step, zero_grad, (window_keys, window_values, window_segment, live_block)
    )
    return (query_grad, key_value)


def on_device(
    tokens,
    cotangent,
    seq_lengths,
    seq_order,
    w_project,
    w_mixer,
    w_expand,
    w_reduce,
    biases,
    norm_gains,
):
    row_count, width = tokens.shape
    shard_count = lax.axis_size("shard")
    shard_index = lax.axis_index("shard")
    group_index = lax.axis_index("grp")
    head_dim = width // HEADS
    hidden_units = w_expand.shape[2]
    score_scale = head_dim ** (-0.5)
    longest = min(SEQ_MAX, row_count * shard_count // 4)
    reach_blocks = longest // row_count
    seq_count = seq_lengths.shape[1]
    seq_ends = group_ends(seq_lengths, seq_order, group_index)
    neighbour = shard_index + jnp.arange(-reach_blocks, reach_blocks + 1, dtype=jnp.int32)
    slot_index = neighbour[:, None] * row_count + jnp.arange(row_count, dtype=jnp.int32)[None, :]
    window_segment = slot_segments(slot_index, seq_ends)
    own_segment = window_segment[reach_blocks]
    inside = (neighbour >= 0) & (neighbour < shard_count)
    live_block = (
        inside
        & (window_segment[:, 0] <= own_segment[row_count - 1])
        & (window_segment[:, row_count - 1] >= own_segment[0])
    )
    valid_rows = (own_segment < seq_count).astype(jnp.float32)[:, None]
    hidden_state = tokens.astype(jnp.float32)
    state_low = tokens
    kept_list = []
    for layer_index in range(LAYERS):
        weights = (
            lax.all_gather(w_project[layer_index], "shard", axis=0, tiled=True),
            lax.all_gather(w_mixer[layer_index], "shard", axis=0, tiled=True),
            lax.all_gather(w_expand[layer_index], "shard", axis=0, tiled=True),
            lax.all_gather(w_reduce[layer_index], "shard", axis=0, tiled=True),
            lax.all_gather(biases[layer_index], "shard", axis=0, tiled=True),
            lax.all_gather(norm_gains[layer_index], "shard", axis=0, tiled=True),
        )
        project, mixing, expand, shrink, bias_list, gain_one, gain_two = unpack_weights(
            weights, width, hidden_units
        )
        bias_q, bias_v, bias_mix, shift_one, bias_in, bias_out, shift_two = bias_list
        projected = jnp.dot(state_low, project, preferred_element_type=jnp.float32)
        projected = projected + jnp.concatenate([bias_q, jnp.zeros_like(bias_q), bias_v])
        projected_low = projected.astype(jnp.bfloat16)
        queries = projected_low[:, :width].reshape(row_count, HEADS, head_dim)
        key_rows = projected_low[:, width : 2 * width].reshape(row_count, HEADS, head_dim)
        value_rows = projected_low[:, 2 * width :].reshape(row_count, HEADS, head_dim)
        window_keys, window_values = gather_window(key_rows, value_rows, reach_blocks)
        log_total, mixed, full_mix = attend_forward(
            queries,
            window_keys,
            window_values,
            window_segment,
            live_block,
            own_segment,
            score_scale,
        )
        mixed_low = mixed.reshape(row_count, width).astype(jnp.bfloat16)
        branch = jnp.dot(mixed_low, mixing, preferred_element_type=jnp.float32) + bias_mix
        summed_one = hidden_state + branch
        normed_one = layer_norm(summed_one, gain_one, shift_one)
        normed_low = normed_one.astype(jnp.bfloat16)
        before = jnp.dot(normed_low, expand, preferred_element_type=jnp.float32) + bias_in
        active_low = gelu_exact(before).astype(jnp.bfloat16)
        feed_out = jnp.dot(active_low, shrink, preferred_element_type=jnp.float32) + bias_out
        summed_two = normed_one + feed_out
        hidden_state = layer_norm(summed_two, gain_two, shift_two)
        kept_list.append(
            (
                state_low,
                queries,
                key_rows,
                value_rows,
                window_keys,
                window_values,
                log_total,
                full_mix,
                mixed_low,
                summed_one,
                normed_low,
                before,
                active_low,
                summed_two,
                weights,
            )
        )
        state_low = hidden_state.astype(jnp.bfloat16)
    activations = (hidden_state * valid_rows).astype(jnp.bfloat16)
    state_grad = cotangent.astype(jnp.float32) * valid_rows
    results = [None] * LAYERS
    for layer_index in reversed(range(LAYERS)):
        (
            layer_low,
            queries,
            key_rows,
            value_rows,
            window_keys,
            window_values,
            log_total,
            full_mix,
            mixed_low,
            summed_one,
            normed_low,
            before,
            active_low,
            summed_two,
            kept_weights,
        ) = kept_list[layer_index]
        weights = (
            lax.all_gather(w_project[layer_index], "shard", axis=0, tiled=True),
            lax.all_gather(w_mixer[layer_index], "shard", axis=0, tiled=True),
            lax.all_gather(w_expand[layer_index], "shard", axis=0, tiled=True),
            lax.all_gather(w_reduce[layer_index], "shard", axis=0, tiled=True),
            lax.all_gather(biases[layer_index], "shard", axis=0, tiled=True),
            lax.all_gather(norm_gains[layer_index], "shard", axis=0, tiled=True),
        )
        project, mixing, expand, shrink, bias_list, gain_one, gain_two = unpack_weights(
            weights, width, hidden_units
        )
        bias_q, bias_v, bias_mix, shift_one, bias_in, bias_out, shift_two = bias_list
        unused_two, norm_pull = jax.vjp(layer_norm, summed_two, gain_two, shift_two)
        sum_two_grad, gain_two_grad, shift_two_grad = norm_pull(state_grad)
        feed_low = sum_two_grad.astype(jnp.bfloat16)
        shrink_grad = jnp.einsum(
            "tf,td->fd", active_low, feed_low, preferred_element_type=jnp.float32
        )
        bias_out_grad = jnp.sum(feed_low, axis=0, dtype=jnp.float32)
        active_grad = jnp.einsum("td,fd->tf", feed_low, shrink, preferred_element_type=jnp.float32)
        unused_gelu, gelu_pull = jax.vjp(gelu_exact, before)
        before_low = gelu_pull(active_grad)[0].astype(jnp.bfloat16)
        expand_grad = jnp.einsum(
            "td,tf->df", normed_low, before_low, preferred_element_type=jnp.float32
        )
        bias_in_grad = jnp.sum(before_low, axis=0, dtype=jnp.float32)
        normed_grad = sum_two_grad + jnp.einsum(
            "tf,df->td", before_low, expand, preferred_element_type=jnp.float32
        )
        unused_one, first_pull = jax.vjp(layer_norm, summed_one, gain_one, shift_one)
        sum_one_grad, gain_one_grad, shift_one_grad = first_pull(normed_grad)
        branch_low = sum_one_grad.astype(jnp.bfloat16)
        mixing_grad = jnp.einsum(
            "td,te->de", mixed_low, branch_low, preferred_element_type=jnp.float32
        )
        bias_mix_grad = jnp.sum(branch_low, axis=0, dtype=jnp.float32)
        mixed_grad = jnp.einsum("te,de->td", branch_low, mixing, preferred_element_type=jnp.float32)
        mixed_grad_low = mixed_grad.astype(jnp.bfloat16).reshape(row_count, HEADS, head_dim)
        delta = jnp.sum(mixed_grad_low.astype(jnp.float32) * full_mix, axis=-1).T
        query_grad, key_value = attend_backward(
            queries,
            window_keys,
            window_values,
            window_segment,
            live_block,
            own_segment,
            log_total,
            delta,
            mixed_grad_low,
            score_scale,
        )
        key_total, value_total = return_parts(key_value[0], key_value[1], reach_blocks)
        projected_grad = jnp.concatenate(
            [
                (query_grad * score_scale).reshape(row_count, width),
                (key_total * score_scale).reshape(row_count, width),
                value_total.reshape(row_count, width),
            ],
            axis=1,
        )
        projected_low = projected_grad.astype(jnp.bfloat16)
        project_grad = jnp.einsum(
            "td,te->de", layer_low, projected_low, preferred_element_type=jnp.float32
        )
        bias_q_grad = jnp.sum(projected_low[:, :width], axis=0, dtype=jnp.float32)
        bias_v_grad = jnp.sum(projected_low[:, 2 * width :], axis=0, dtype=jnp.float32)
        state_grad = sum_one_grad + jnp.einsum(
            "te,de->td", projected_low, project, preferred_element_type=jnp.float32
        )
        bias_all = jnp.concatenate(
            [
                bias_q_grad,
                bias_v_grad,
                bias_mix_grad,
                shift_one_grad,
                bias_in_grad,
                bias_out_grad,
                shift_two_grad,
            ]
        )
        gain_all = jnp.concatenate([gain_one_grad, gain_two_grad])
        shares = (
            lax.psum_scatter(
                project_grad.astype(jnp.bfloat16), "shard", scatter_dimension=0, tiled=True
            ).astype(jnp.float32),
            lax.psum_scatter(
                mixing_grad.astype(jnp.bfloat16), "shard", scatter_dimension=0, tiled=True
            ).astype(jnp.float32),
            lax.psum_scatter(
                expand_grad.astype(jnp.bfloat16), "shard", scatter_dimension=0, tiled=True
            ).astype(jnp.float32),
            lax.psum_scatter(
                shrink_grad.astype(jnp.bfloat16), "shard", scatter_dimension=0, tiled=True
            ).astype(jnp.float32),
            lax.psum_scatter(
                bias_all.astype(jnp.bfloat16), "shard", scatter_dimension=0, tiled=True
            ).astype(jnp.float32),
            lax.psum_scatter(
                gain_all.astype(jnp.bfloat16), "shard", scatter_dimension=0, tiled=True
            ).astype(jnp.float32),
        )
        shares = (
            lax.psum(shares[0].astype(jnp.bfloat16), "grp").astype(jnp.float32),
            lax.psum(shares[1].astype(jnp.bfloat16), "grp").astype(jnp.float32),
            lax.psum(shares[2].astype(jnp.bfloat16), "grp").astype(jnp.float32),
            lax.psum(shares[3].astype(jnp.bfloat16), "grp").astype(jnp.float32),
            lax.psum(shares[4].astype(jnp.bfloat16), "grp").astype(jnp.float32),
            lax.psum(shares[5].astype(jnp.bfloat16), "grp").astype(jnp.float32),
        )
        results[layer_index] = shares
    stacked = [jnp.stack([layer_share[member] for layer_share in results]) for member in range(6)]
    return (
        activations,
        state_grad,
        stacked[0],
        stacked[1],
        stacked[2],
        stacked[3],
        stacked[4],
        stacked[5],
    )


HEAD_SCALE = 0.125


def in_main(array):
    return pltpu.with_memory_space_constraint(array, pltpu.HBM)


def fold_rows(values, combine):
    total = values[:8]
    for begin_at in range(8, values.shape[0], 8):
        total = combine(total, values[begin_at : begin_at + 8])
    return total


def halves_of(block):
    lane = lax.broadcasted_iota(jnp.int32, block.shape, 1)
    nothing = jnp.zeros_like(block)
    return (jnp.where(lane < 64, block, nothing), jnp.where(lane < 64, nothing, block))


def turned_dot(keys, queries):
    return lax.dot_general(
        keys, queries, (((1,), (1,)), ((), ())), preferred_element_type=jnp.float32
    )


def across_dot(weight, values):
    return lax.dot_general(
        weight, values, (((0,), (0,)), ((), ())), preferred_element_type=jnp.float32
    )


KEY_ROWS = 512
KEY_TILES = 5


def key_rows(tile):
    return pl.ds(pl.multiple_of(tile * KEY_ROWS, KEY_ROWS), KEY_ROWS)


def fill_mask(first, last, low, high, mask_scr, index):
    def mask_step(key_tile, carry):
        shape = (KEY_ROWS, low.shape[1])
        place = lax.broadcasted_iota(jnp.int32, shape, 0) + key_tile * KEY_ROWS
        allowed = (place >= low) & (place < high)
        mask_scr[index, key_rows(key_tile - first), :] = jnp.where(allowed, 0.0, NEGATIVE)
        return carry

    lax.fori_loop(first, last, mask_step, 0)


def flash_forward_kernel(
    bounds,
    a_ref,
    b_ref,
    kv_ref,
    low_ref,
    high_ref,
    a_mix,
    b_mix,
    a_wide,
    b_wide,
    lse_ref,
    mask_scr,
    score_scr,
):
    rows, width = a_ref.shape
    pairs = width // 128
    for index in range(2):
        span = slice(index * rows, (index + 1) * rows)
        fill_mask(
            bounds[2 * index],
            bounds[2 * index + 1],
            low_ref[0:1, span],
            high_ref[0:1, span],
            mask_scr,
            index,
        )

    def pair_step(pair, unused):
        lanes = pl.ds(pl.multiple_of(pair * 128, 128), 128)
        value_lanes = pl.ds(pl.multiple_of(pair * 128 + width, 128), 128)
        for index, (q_ref, mix_ref, wide_ref) in enumerate(
            ((a_ref, a_mix, a_wide), (b_ref, b_mix, b_wide))
        ):
            first, last = bounds[2 * index], bounds[2 * index + 1]
            heads = halves_of(q_ref[:, lanes] * jnp.bfloat16(HEAD_SCALE))

            def score_step(key_tile, tops, index=index, heads=heads, first=first):
                keys = kv_ref[key_rows(bounds[4 + key_tile]), lanes]
                place = key_rows(key_tile - first)
                mask = mask_scr[index, place, :]
                out = []
                for head in range(2):
                    scores = turned_dot(keys, heads[head]) + mask
                    score_scr[head, place, :] = scores
                    out.append(jnp.maximum(tops[head], fold_rows(scores, jnp.maximum)))
                return tuple(out)

            floor = jnp.full((8, rows), NEGATIVE, jnp.float32)
            tops = lax.fori_loop(first, last, score_step, (floor, floor))
            tops = [jnp.max(top, axis=0, keepdims=True) for top in tops]

            def mix_step(key_tile, carry, tops=tops, first=first):
                values = kv_ref[key_rows(bounds[4 + key_tile]), value_lanes].T
                totals, mixed = [], []
                for head in range(2):
                    weight = jnp.exp(score_scr[head, key_rows(key_tile - first), :] - tops[head])
                    totals.append(carry[head] + fold_rows(weight, jnp.add))
                    mixed.append(
                        carry[2 + head]
                        + jnp.dot(
                            values[head * 64 : (head + 1) * 64],
                            weight.astype(jnp.bfloat16),
                            preferred_element_type=jnp.float32,
                        )
                    )
                return (totals[0], totals[1], mixed[0], mixed[1])

            zero = jnp.zeros((8, rows), jnp.float32)
            nothing = jnp.zeros((64, rows), jnp.float32)
            carry = lax.fori_loop(first, last, mix_step, (zero, zero, nothing, nothing))
            totals = [jnp.sum(total, axis=0, keepdims=True) for total in carry[:2]]
            mixed = jnp.concatenate(
                [carry[2] * (1.0 / totals[0]), carry[3] * (1.0 / totals[1])], axis=0
            ).T
            wide_ref[:, lanes] = mixed
            mix_ref[:, lanes] = mixed.astype(jnp.bfloat16)
            lse_rows = [tops[head] + jnp.log(totals[head]) for head in range(2)]
            lse_ref[
                pl.ds(pl.multiple_of(pair * 8, 8), 8), index * rows : (index + 1) * rows
            ] = jnp.concatenate([jnp.broadcast_to(line, (4, rows)) for line in lse_rows])
        return unused

    lax.fori_loop(0, pairs, pair_step, 0)


def flash_backward_kernel(
    bounds,
    a_ref,
    b_ref,
    kv_ref,
    a_grad_ref,
    b_grad_ref,
    a_wide,
    b_wide,
    lse_ref,
    low_ref,
    high_ref,
    a_out,
    b_out,
    kv_out,
    mask_scr,
    k_acc,
    v_acc,
):
    rows, width = a_ref.shape
    pairs = width // 128
    tiles = kv_ref.shape[0] // KEY_ROWS
    for index in range(2):
        span = slice(index * rows, (index + 1) * rows)
        fill_mask(
            bounds[2 * index],
            bounds[2 * index + 1],
            low_ref[0:1, span],
            high_ref[0:1, span],
            mask_scr,
            index,
        )

    def pair_step(pair, unused):
        lanes = pl.ds(pl.multiple_of(pair * 128, 128), 128)
        value_lanes = pl.ds(pl.multiple_of(pair * 128 + width, 128), 128)
        lse_rows = lse_ref[pl.ds(pl.multiple_of(pair * 8, 8), 8), :]
        k_acc[...] = jnp.zeros_like(k_acc)
        v_acc[...] = jnp.zeros_like(v_acc)
        ways = (((1,), (1,)), ((), ()))
        for index, (q_ref, grad_ref, wide_ref, q_out) in enumerate(
            ((a_ref, a_grad_ref, a_wide, a_out), (b_ref, b_grad_ref, b_wide, b_out))
        ):
            first, last = bounds[2 * index], bounds[2 * index + 1]
            heads = halves_of(q_ref[:, lanes] * jnp.bfloat16(HEAD_SCALE))
            grads = halves_of(grad_ref[:, lanes])
            turned_q = (q_ref[:, lanes] * jnp.bfloat16(HEAD_SCALE)).T
            turned_grad = grad_ref[:, lanes].T
            span = slice(index * rows, (index + 1) * rows)
            lse = (lse_rows[0:1, span], lse_rows[4:5, span])

            product = (grad_ref[:, lanes].astype(jnp.float32) * wide_ref[:, lanes]).T
            deltas = (
                jnp.sum(product[:64], axis=0, keepdims=True),
                jnp.sum(product[64:], axis=0, keepdims=True),
            )

            def grad_step(
                key_tile,
                q_sum,
                index=index,
                heads=heads,
                grads=grads,
                lse=lse,
                deltas=deltas,
                first=first,
                turned_q=turned_q,
                turned_grad=turned_grad,
            ):
                source = key_rows(bounds[4 + key_tile])
                columns = key_rows(bounds[4 + key_tile])
                keys = kv_ref[source, lanes]
                turned_keys = keys.T
                values = kv_ref[source, value_lanes]
                mask = mask_scr[index, key_rows(key_tile - first), :]
                out = []
                for head in range(2):
                    part = slice(head * 64, (head + 1) * 64)
                    scores = turned_dot(keys, heads[head])
                    slope = turned_dot(values, grads[head])
                    probs = jnp.exp((scores - lse[head]) + mask)
                    low_slope = (probs * (slope - deltas[head])).astype(jnp.bfloat16)
                    v_acc[part, columns] += lax.dot_general(
                        turned_grad[part],
                        probs.astype(jnp.bfloat16),
                        ways,
                        preferred_element_type=jnp.float32,
                    )
                    k_acc[part, columns] += lax.dot_general(
                        turned_q[part], low_slope, ways, preferred_element_type=jnp.float32
                    )
                    out.append(
                        q_sum[head]
                        + jnp.dot(turned_keys[part], low_slope, preferred_element_type=jnp.float32)
                    )
                return tuple(out)

            nothing = jnp.zeros((64, rows), jnp.float32)
            q_parts = lax.fori_loop(first, last, grad_step, (nothing, nothing))
            q_part = jnp.concatenate(q_parts, axis=0).T
            q_out[:, lanes] = (q_part * HEAD_SCALE).astype(jnp.bfloat16)

        def store_step(tile, carry):
            source = key_rows(tile)
            kv_out[source, lanes] = k_acc[:, source].T.astype(jnp.bfloat16)
            kv_out[source, value_lanes] = v_acc[:, source].T.astype(jnp.bfloat16)
            return carry

        lax.fori_loop(0, tiles, store_step, 0)
        return unused

    lax.fori_loop(0, pairs, pair_step, 0)


def whole_block(shape):
    return pl.BlockSpec(shape, lambda i, b: (0,) * len(shape), pipeline_mode=pl.Buffered(1))


def flash_forward(bounds, queries, key_value, low, high):
    rows, width = queries[0].shape
    window = key_value.shape[0]
    pairs = width // 128
    own = whole_block((rows, width))
    line = whole_block((8, 2 * rows))
    return pl.pallas_call(
        flash_forward_kernel,
        out_shape=(
            jax.ShapeDtypeStruct((rows, width), jnp.bfloat16),
            jax.ShapeDtypeStruct((rows, width), jnp.bfloat16),
            jax.ShapeDtypeStruct((rows, width), jnp.float32),
            jax.ShapeDtypeStruct((rows, width), jnp.float32),
            jax.ShapeDtypeStruct((pairs * 8, 2 * rows), jnp.float32),
        ),
        grid_spec=pltpu.PrefetchScalarGridSpec(
            num_scalar_prefetch=1,
            grid=(1,),
            in_specs=[own, own, whole_block((window, 2 * width)), line, line],
            out_specs=[own, own, own, own, whole_block((pairs * 8, 2 * rows))],
            scratch_shapes=[
                pltpu.VMEM((2, KEY_TILES * KEY_ROWS, rows), jnp.float32),
                pltpu.VMEM((2, KEY_TILES * KEY_ROWS, rows), jnp.float32),
            ],
        ),
        compiler_params=pltpu.CompilerParams(vmem_limit_bytes=44 * 2**20),
        cost_estimate=pl.CostEstimate(
            flops=8 * rows * width * 2560, bytes_accessed=12 * 2**20, transcendentals=rows * 12 * 2560
        ),
        name="flash_forward",
    )(bounds, queries[0], queries[1], key_value, low, high)


def flash_backward(bounds, queries, key_value, grads, wides, lse, low, high):
    rows, width = queries[0].shape
    window = key_value.shape[0]
    pairs = width // 128
    own = whole_block((rows, width))
    wide = whole_block((window, 2 * width))
    line = whole_block((8, 2 * rows))
    return pl.pallas_call(
        flash_backward_kernel,
        out_shape=(
            jax.ShapeDtypeStruct((rows, width), jnp.bfloat16),
            jax.ShapeDtypeStruct((rows, width), jnp.bfloat16),
            jax.ShapeDtypeStruct((window, 2 * width), jnp.bfloat16),
        ),
        grid_spec=pltpu.PrefetchScalarGridSpec(
            num_scalar_prefetch=1,
            grid=(1,),
            in_specs=[own, own, wide] + [own] * 4 + [whole_block((pairs * 8, 2 * rows)), line, line],
            out_specs=[own, own, wide],
            scratch_shapes=[
                pltpu.VMEM((2, KEY_TILES * KEY_ROWS, rows), jnp.float32),
                pltpu.VMEM((128, window), jnp.float32),
                pltpu.VMEM((128, window), jnp.float32),
            ],
        ),
        compiler_params=pltpu.CompilerParams(vmem_limit_bytes=56 * 2**20),
        cost_estimate=pl.CostEstimate(
            flops=20 * rows * width * 2560,
            bytes_accessed=20 * 2**20,
            transcendentals=rows * 12 * 2560,
        ),
        name="flash_backward",
    )(bounds, *queries, key_value, *grads, *wides, lse, low, high)


GRP_Y, GRP_CORE, SHARD_Z, SHARD_X = 2, 2, 4, 2
BOTH = ("grp", "shard")


def device_pairs(place):
    pairs = []
    for y in range(GRP_Y):
        for core in range(GRP_CORE):
            for z in range(SHARD_Z):
                for x in range(SHARD_X):
                    target = place(y, core, z, x)
                    if target is not None:
                        ty, tcore, tz, tx = target
                        pairs.append(
                            (
                                (y * GRP_CORE + core) * SHARD_Z * SHARD_X + z * SHARD_X + x,
                                (ty * GRP_CORE + tcore) * SHARD_Z * SHARD_X + tz * SHARD_X + tx,
                            )
                        )
    return pairs


def send(values, place):
    return lax.ppermute(values, BOTH, device_pairs(place))


def turn_rows(values):
    return send(values, lambda y, core, z, x: (y, x, z, core))


def swap_core(values):
    return send(values, lambda y, core, z, x: (y, 1 - core, z, x))


def send_up(values):
    return send(values, lambda y, core, z, x: (y, core, z + 1, x) if z + 1 < SHARD_Z else None)


def send_down(values):
    return send(values, lambda y, core, z, x: (y, core, z - 1, x) if z > 0 else None)


def window_of(rows):
    near = jnp.concatenate([rows, send_up(rows), send_down(rows)])
    return jnp.concatenate([near, swap_core(near)])


def window_back(near, far, count):
    total = near + swap_core(far.astype(jnp.bfloat16)).astype(jnp.float32)
    below = total[count : 2 * count].astype(jnp.bfloat16)
    above = total[2 * count :].astype(jnp.bfloat16)
    return (
        total[:count]
        + send_down(below).astype(jnp.float32)
        + send_up(above).astype(jnp.float32)
    )


def half_of(values, axis, index):
    count = values.shape[axis] // 2
    return lax.dynamic_slice_in_dim(values, index * count, count, axis)


def unpack_kernel(kinds, in_ref, *outs):
    width = in_ref.shape[-1]
    share = in_ref.shape[3]
    place = 0
    for kind, ref in zip(kinds, outs):
        if kind == "columns":
            for column in range(ref.shape[-1] // width):
                ref[:, 0, :, column * width : (column + 1) * width] = in_ref[0, :, place]
                place += 1
        else:
            for piece in range(ref.shape[2] // share):
                ref[:, 0, piece * share : (piece + 1) * share, :] = in_ref[0, :, place]
                place += 1


def unpack_weights_of(pieces, begin_at, places, kinds, shapes):
    quarters, shards, unused, share, width = pieces.shape
    outs = pl.pallas_call(
        functools.partial(unpack_kernel, kinds),
        out_shape=[
            pltpu.HBM((shards, quarters, rows, wide), pieces.dtype) for rows, wide in shapes
        ],
        grid=(quarters,),
        in_specs=[
            pl.BlockSpec(
                (1, shards, places, share, width), lambda q: (q, 0, begin_at // places, 0, 0)
            )
        ],
        out_specs=[
            pl.BlockSpec((shards, 1, rows, wide), lambda q: (0, q, 0, 0)) for rows, wide in shapes
        ],
        compiler_params=pltpu.CompilerParams(vmem_limit_bytes=32 * 2**20),
        cost_estimate=pl.CostEstimate(
            flops=0, bytes_accessed=128 * places * share * width, transcendentals=0
        ),
        name="unpack_weights",
    )(in_main(pieces))
    return [out.reshape(-1, out.shape[-1]) for out in outs]


def pick_kernel(
    me, near_ref, project_ref, mixer_ref, expand_ref, reduce_ref, small_ref, a_out, b_out, c_out
):
    part, half = a_out.shape[-2:]
    for column in range(3):
        begin_at = pl.multiple_of(column * 2 * half + me[1] * half, 128)
        a_out[column] = near_ref[0, :, pl.ds(begin_at, half)]
    a_out[3] = jnp.zeros((part, half), a_out.dtype)
    a_out[3, 0:8, :] = small_ref[:, :half]
    a_out[3, 8:16, :] = small_ref[:, half:]
    share, width = b_out.shape[-2:]
    wide = expand_ref.shape[-1] // width
    for layer, ref in enumerate((b_out, c_out)):
        deep = reduce_ref.shape[1] // share
        for piece in range(deep):
            ref[piece] = reduce_ref[layer, piece * share : (piece + 1) * share, :]
        for column in range(wide):
            ref[deep + column] = expand_ref[layer, :, column * width : (column + 1) * width]
        ref[deep + wide] = mixer_ref[layer]
    far = c_out.shape[0]
    for column in range(3):
        b_out[far + column] = project_ref[0, :, column * width : (column + 1) * width]


def pick_quarters(me, project, mixer, expand, reduce, small):
    share, width = mixer.shape[1] // 4, mixer.shape[2]
    far = 1 + expand.shape[2] // width + reduce.shape[1] // 4 // share

    def quarter_spec(array):
        return pl.BlockSpec(
            (LAYERS, array.shape[1] // 4, array.shape[2]),
            lambda i, me: (0, me[0] * GRP_CORE + me[1], 0),
        )

    shapes = [(4, 2 * share, width // 2), (far + 3, share, width), (far, share, width)]
    return pl.pallas_call(
        pick_kernel,
        out_shape=[jax.ShapeDtypeStruct(shape, jnp.bfloat16) for shape in shapes],
        grid_spec=pltpu.PrefetchScalarGridSpec(
            num_scalar_prefetch=1,
            grid=(1,),
            in_specs=[
                pl.BlockSpec((1, 2 * share, project.shape[2]), lambda i, me: (0, me[0], 0)),
                pl.BlockSpec(
                    (1, share, project.shape[2]), lambda i, me: (1, me[0] * GRP_CORE + me[1], 0)
                ),
            ]
            + [quarter_spec(array) for array in (mixer, expand, reduce)]
            + [pl.BlockSpec(small.shape, lambda i, me: (0, 0))],
            out_specs=[pl.BlockSpec(shape, lambda i, me: (0, 0, 0)) for shape in shapes],
        ),
        name="pick_quarters",
    )(me, project, project, mixer, expand, reduce, small)


def pack_kernel(kinds, *refs):
    ins, vector_ref, out_ref = refs[:-2], refs[-2], refs[-1]
    width = out_ref.shape[-1]
    share = ins[0].shape[2]
    begin_at = 0
    for kind, ref in zip(kinds, ins):
        if kind == "columns":
            for column in range(ref.shape[-1] // width):
                lanes = slice(column * width, (column + 1) * width)
                out_ref[0, :, begin_at : begin_at + share, :] = ref[:, 0, :, lanes]
                begin_at += share
        else:
            out_ref[0, :, begin_at : begin_at + ref.shape[2], :] = ref[:, 0]
            begin_at += ref.shape[2]
    out_ref[0, :, begin_at : begin_at + 8, :] = vector_ref[0]


def pack_terms(terms, kinds, width, vectors):
    rows = sum(t.size for t in terms) // (32 * width) + 8
    views = [t.reshape(8, 4, -1, t.shape[1]) for t in terms]
    return pl.pallas_call(
        functools.partial(pack_kernel, kinds),
        out_shape=pltpu.HBM((4, 8, rows, width), jnp.bfloat16),
        grid=(4,),
        in_specs=[pl.BlockSpec((8, 1) + view.shape[2:], lambda q: (0, q, 0, 0)) for view in views]
        + [pl.BlockSpec((1,) + vectors.shape[1:], lambda q: (q, 0, 0, 0))],
        out_specs=pl.BlockSpec((1, 8, rows, width), lambda q: (q, 0, 0, 0)),
        compiler_params=pltpu.CompilerParams(vmem_limit_bytes=32 * 2**20),
        cost_estimate=pl.CostEstimate(
            flops=0, bytes_accessed=128 * rows * width, transcendentals=0
        ),
        name="pack_terms",
    )(*[in_main(view) for view in views], vectors)


def swap_y(values):
    return send(values, lambda y, core, z, x: (1 - y, core, z, x))


def swap_x(values):
    return send(values, lambda y, core, z, x: (y, core, z, 1 - x))


def swap_z(values, bit):
    return send(values, lambda y, core, z, x: (y, core, z ^ bit, x))


def spread_kernel(me, q_ref, kv_ref, vector_ref, out_ref):
    part, half = out_ref.shape[-2:]
    for x_bit in range(SHARD_X):
        for z_bits in range(SHARD_Z):
            shard = (z_bits ^ me[3]) * SHARD_X + (x_bit ^ me[2])
            out_ref[0, x_bit, z_bits, 0] = q_ref[shard, 0]
            out_ref[0, x_bit, z_bits, 1] = kv_ref[shard, 0, :, :half]
            out_ref[0, x_bit, z_bits, 2] = kv_ref[shard, 0, :, half:]
            out_ref[0, x_bit, z_bits, 3] = jnp.zeros((part, half), jnp.bfloat16)
            out_ref[0, x_bit, z_bits, 3, 0:8, :] = vector_ref[0, shard]


def spread_terms(me, query_term, key_value_term, vectors):
    half = query_term.shape[1]
    part = query_term.shape[0] // 16
    shape = (GRP_Y, SHARD_X, SHARD_Z, 4, part, half)

    def rows_spec(columns):
        return pl.BlockSpec((8, 1, part, columns), lambda j, me: (0, j ^ me[0], 0, 0))

    return pl.pallas_call(
        spread_kernel,
        out_shape=jax.ShapeDtypeStruct(shape, jnp.bfloat16),
        grid_spec=pltpu.PrefetchScalarGridSpec(
            num_scalar_prefetch=1,
            grid=(2,),
            in_specs=[
                rows_spec(half),
                rows_spec(2 * half),
                pl.BlockSpec((1,) + vectors.shape[1:], lambda j, me: (j ^ me[0], 0, 0, 0)),
            ],
            out_specs=pl.BlockSpec((1,) + shape[1:], lambda j, me: (j, 0, 0, 0, 0, 0)),
        ),
        name="spread_terms",
    )(
        me,
        query_term.reshape(8, 2, part, half),
        key_value_term.reshape(8, 2, part, 2 * half),
        vectors,
    )


def summed(one, other):
    return (one.astype(jnp.float32) + other.astype(jnp.float32)).astype(jnp.bfloat16)


def scatter_terms(a_part, b_part, b_next):
    a_next = swap_y(a_part[1])
    a_last = swap_x(summed(a_part[0, 1], a_next[1]))
    b_last = swap_y(summed(b_part[1, 0], b_next[1]))
    a_keep = summed(a_part[0, 0], a_next[0])
    b_keep = summed(b_part[0, 0], b_next[0])
    whole = jnp.concatenate([a_keep, b_keep], axis=1)
    come = jnp.concatenate([a_last, b_last], axis=1)
    far = swap_z(summed(whole[2:], come[2:]), 2)
    whole = summed(whole[:2], come[:2])
    near = swap_z(summed(whole[1], far[1]), 1)
    return summed(summed(whole[0], far[0]), near)


def gather_quarters(piece):
    pair = jnp.stack([piece, swap_y(piece)])
    return jnp.stack([pair, swap_core(pair)])


def finish_kernel(me, *refs):
    layers = len(refs) // 2 - 3
    outs = refs[2 * layers :]

    def fill(near_ref, far_ref):
        part, half = near_ref.shape[-2:]
        share, width = part // 2, 2 * half
        for y_bit in range(GRP_Y):
            for core_bit in range(GRP_CORE):
                y = y_bit ^ me[0]
                core = core_bit ^ me[1]
                quarter = y * GRP_CORE + core
                for column in range(3):
                    lanes = pl.ds(pl.multiple_of(column * 2 * half + core * half, 128), half)
                    outs[0][0, y, :, lanes] = near_ref[core_bit, y_bit, column].astype(jnp.float32)
                outs[4][0, quarter] = near_ref[core_bit, y_bit, 3, 0:8, :].astype(jnp.float32)
                pieces = far_ref.at[core_bit, y_bit]
                outs[1][0, quarter] = pieces[:share, :].astype(jnp.float32)
                begin_at = share
                for column in range(outs[2].shape[-1] // width):
                    lanes = slice(column * width, (column + 1) * width)
                    rows = slice(begin_at, begin_at + share)
                    outs[2][0, quarter, :, lanes] = pieces[rows, :].astype(jnp.float32)
                    begin_at += share
                deep = outs[3].shape[2]
                outs[3][0, quarter] = pieces[begin_at : begin_at + deep, :].astype(jnp.float32)
                begin_at += deep
                outs[5][0, quarter] = pieces[begin_at : begin_at + 8, :].astype(jnp.float32)

    for layer in range(layers):
        pl.when(pl.program_id(0) == layer)(
            functools.partial(fill, refs[2 * layer], refs[2 * layer + 1])
        )


def finish_shares(me, shares, hidden_units, deep):
    layers = len(shares)
    part, half = shares[0][0].shape[-2:]
    share, width = part // 2, 2 * half
    shapes = [
        (2, part, 3 * width),
        (4, share, width),
        (4, share, hidden_units),
        (4, deep, width),
        (4, 8, half),
        (4, 8, width),
    ]
    flat = [array for pair in shares for array in pair]
    outs = pl.pallas_call(
        finish_kernel,
        out_shape=[jax.ShapeDtypeStruct((layers,) + shape, jnp.float32) for shape in shapes],
        grid_spec=pltpu.PrefetchScalarGridSpec(
            num_scalar_prefetch=1,
            grid=(layers,),
            in_specs=[whole_block(array.shape) for array in flat],
            out_specs=[
                pl.BlockSpec((1,) + shape, lambda i, me: (i, 0, 0, 0)) for shape in shapes
            ],
        ),
        compiler_params=pltpu.CompilerParams(vmem_limit_bytes=32 * 2**20),
        name="finish_shares",
    )(me, *flat)
    return [out.reshape(layers, -1, out.shape[-1]) for out in outs[:4]] + list(outs[4:])


def row_mean(values):
    return jnp.mean(values, axis=1, keepdims=True)


def column_sum(values):
    return jnp.sum(values, axis=0, keepdims=True)


def standardized(values):
    centered = values - row_mean(values)
    scale = lax.rsqrt(row_mean(centered * centered) + EPSILON)
    return centered * scale, scale


def standard_back(grad, norm, scale, gain):
    weighted = grad * gain
    return (weighted - row_mean(weighted) - norm * row_mean(weighted * norm)) * scale


def join_rows(ref, whole_scr):
    quarters, shards, pieces, share, unused = ref.shape
    for shard in range(shards):
        for quarter in range(quarters):
            for piece in range(pieces):
                begin_at = ((shard * quarters + quarter) * pieces + piece) * share
                whole_scr[begin_at : begin_at + share, :] = ref[quarter, shard, piece]


def piece_specs(pieces, steps):
    quarters, shards, unused, share, width = pieces.shape
    deep = steps
    return [
        pl.BlockSpec((quarters, shards, 1, share, width), lambda j, me: (0, 0, deep + j, 0, 0)),
        pl.BlockSpec((quarters, shards // steps, deep, share, width), lambda j, me: (0, j, 0, 0, 0)),
        pl.BlockSpec((quarters, shards, 1, share, width), lambda j, me: (0, 0, deep + steps, 0, 0)),
    ]


def tail_forward_kernel(
    me,
    own_ref,
    far_ref,
    state_ref,
    expand_ref,
    reduce_ref,
    mixer_ref,
    bias_in_ref,
    vector_ref,
    mix_out,
    norm_one_out,
    scale_one_out,
    low_out,
    active_out,
    slope_out,
    norm_two_out,
    scale_two_out,
    state_out,
    state_low_out,
    wide_scr,
    total_scr,
    one_scr,
    two_scr,
):
    step = pl.program_id(0)
    half = own_ref.shape[1]

    @pl.when(step == 0)
    def begin():
        mix_out[:, pl.ds(pl.multiple_of(me[1] * half, 128), half)] = own_ref[...]
        mix_out[:, pl.ds(pl.multiple_of((1 - me[1]) * half, 128), half)] = far_ref[...]
        join_rows(mixer_ref, one_scr)
        branch = jnp.dot(mix_out[...], one_scr[...], preferred_element_type=jnp.float32)
        norm, scale = standardized(state_ref[...].astype(jnp.float32) + (branch + vector_ref[2:3]))
        norm_one_out[...] = norm
        scale_one_out[...] = jnp.broadcast_to(scale, scale_one_out.shape)
        wide = norm * vector_ref[10:11] + vector_ref[3:4]
        wide_scr[...] = wide
        low_out[...] = wide.astype(jnp.bfloat16)
        total_scr[...] = jnp.zeros_like(total_scr)

    join_rows(expand_ref, one_scr)
    join_rows(reduce_ref, two_scr)
    before = (
        jnp.dot(low_out[...], one_scr[...], preferred_element_type=jnp.float32)
        + bias_in_ref[...]
    )
    normal = 0.5 * (1.0 + lax.erf(before * 0.7071067811865476))
    density = jnp.exp(before * before * -0.5) * 0.3989422804014327
    active = (before * normal).astype(jnp.bfloat16)
    active_out[...] = active
    slope_out[...] = normal + before * density
    total_scr[...] += jnp.dot(active, two_scr[...], preferred_element_type=jnp.float32)

    @pl.when(step == pl.num_programs(0) - 1)
    def end():
        norm, scale = standardized(wide_scr[...] + (total_scr[...] + vector_ref[8:9]))
        norm_two_out[...] = norm
        scale_two_out[...] = jnp.broadcast_to(scale, scale_two_out.shape)
        state = norm * vector_ref[11:12] + vector_ref[9:10]
        state_out[...] = state
        state_low_out[...] = state.astype(jnp.bfloat16)


def tail_forward(me, own_mix, far_mix, state, pieces, bias_in, vectors):
    rows, width = state.shape
    hidden_units = bias_in.shape[1]
    steps = hidden_units // width
    whole = whole_block((rows, width))
    halves = whole_block((rows, width // 2))
    scale = whole_block((rows, 128))
    tile = pl.BlockSpec((rows, width), lambda j, me: (0, j))

    def shaped(columns, kind):
        return jax.ShapeDtypeStruct((rows, columns), kind)

    return pl.pallas_call(
        tail_forward_kernel,
        out_shape=[
            shaped(width, jnp.bfloat16),
            shaped(width, jnp.float32),
            shaped(128, jnp.float32),
            shaped(width, jnp.bfloat16),
            shaped(hidden_units, jnp.bfloat16),
            shaped(hidden_units, jnp.float32),
            shaped(width, jnp.float32),
            shaped(128, jnp.float32),
            shaped(width, jnp.float32),
            shaped(width, jnp.bfloat16),
        ],
        grid_spec=pltpu.PrefetchScalarGridSpec(
            num_scalar_prefetch=1,
            grid=(steps,),
            in_specs=[
                halves,
                halves,
                whole,
            ]
            + piece_specs(pieces, steps)
            + [pl.BlockSpec((1, width), lambda j, me: (0, j)), whole_block(vectors.shape)],
            out_specs=[whole, whole, scale, whole, tile, tile, whole, scale, whole, whole],
            scratch_shapes=[
                pltpu.VMEM((rows, width), jnp.float32),
                pltpu.VMEM((rows, width), jnp.float32),
                pltpu.VMEM((width, width), jnp.bfloat16),
                pltpu.VMEM((width, width), jnp.bfloat16),
            ],
        ),
        compiler_params=pltpu.CompilerParams(vmem_limit_bytes=44 * 2**20),
        cost_estimate=pl.CostEstimate(
            flops=2 * rows * width * (width + 2 * hidden_units),
            bytes_accessed=32 * 2**20,
            transcendentals=2 * rows * hidden_units,
        ),
        name="tail_forward",
    )(me, own_mix, far_mix, state, *[in_main(pieces)] * 3, bias_in, vectors)


def tail_backward_kernel(
    me,
    grad_ref,
    norm_two_ref,
    scale_two_ref,
    norm_one_ref,
    scale_one_ref,
    low_ref,
    mix_ref,
    slope_ref,
    active_ref,
    expand_ref,
    reduce_ref,
    mixer_ref,
    vector_ref,
    sum_out,
    own_out,
    far_out,
    mixer_out,
    expand_out,
    reduce_out,
    bias_in_out,
    vector_out,
    wide_scr,
    feed_scr,
    total_scr,
    one_scr,
    two_scr,
):
    step = pl.program_id(0)
    half = own_out.shape[1]

    @pl.when(step == 0)
    def begin():
        grad = grad_ref[...]
        norm = norm_two_ref[...]
        wide = standard_back(grad, norm, scale_two_ref[:, 0:1], vector_ref[11:12])
        wide_scr[...] = wide
        feed = wide.astype(jnp.bfloat16)
        feed_scr[...] = feed
        vector_out[...] = jnp.zeros_like(vector_out)
        vector_out[3:4] = column_sum(feed.astype(jnp.float32))
        vector_out[4:5] = column_sum(grad * norm)
        vector_out[5:6] = column_sum(grad)
        total_scr[...] = jnp.zeros_like(total_scr)

    join_rows(expand_ref, one_scr)
    join_rows(reduce_ref, two_scr)
    feed = feed_scr[...]
    active_grad = turned_dot(feed, two_scr[...])
    before = (active_grad * slope_ref[...]).astype(jnp.bfloat16)
    bias_in_out[...] = column_sum(before.astype(jnp.float32))
    reduce_out[...] = across_dot(active_ref[...], feed).astype(jnp.bfloat16)
    expand_out[...] = across_dot(low_ref[...], before).astype(jnp.bfloat16)
    total_scr[...] += turned_dot(before, one_scr[...])

    @pl.when(step == pl.num_programs(0) - 1)
    def end():
        grad = wide_scr[...] + total_scr[...]
        norm = norm_one_ref[...]
        wide = standard_back(grad, norm, scale_one_ref[:, 0:1], vector_ref[10:11])
        sum_out[...] = wide
        branch = wide.astype(jnp.bfloat16)
        vector_out[0:1] = column_sum(branch.astype(jnp.float32))
        vector_out[1:2] = column_sum(grad * norm)
        vector_out[2:3] = column_sum(grad)
        mixer_out[...] = across_dot(mix_ref[...], branch).astype(jnp.bfloat16)
        join_rows(mixer_ref, one_scr)
        mixed = turned_dot(branch, one_scr[...]).astype(jnp.bfloat16)
        total_scr[...] = mixed.astype(jnp.float32)
        own = total_scr[:, pl.ds(pl.multiple_of(me[1] * half, 128), half)]
        far = total_scr[:, pl.ds(pl.multiple_of((1 - me[1]) * half, 128), half)]
        own_out[...] = own.astype(jnp.bfloat16)
        far_out[...] = far.astype(jnp.bfloat16)


def tail_backward(me, grad, kept, pieces, vectors):
    norm_two, scale_two, norm_one, scale_one, low, mixed, slope, active = kept
    rows, width = grad.shape
    hidden_units = active.shape[1]
    steps = hidden_units // width
    whole = whole_block((rows, width))
    halves = whole_block((rows, width // 2))
    scale = whole_block((rows, 128))
    square = whole_block((width, width))
    tile = pl.BlockSpec((rows, width), lambda j, me: (0, j))
    across = pl.BlockSpec((width, width), lambda j, me: (0, j))
    down = pl.BlockSpec((width, width), lambda j, me: (j, 0))
    line = pl.BlockSpec((1, width), lambda j, me: (0, j))

    def shaped(rows, columns, kind):
        return jax.ShapeDtypeStruct((rows, columns), kind)

    return pl.pallas_call(
        tail_backward_kernel,
        out_shape=[
            shaped(rows, width, jnp.float32),
            shaped(rows, width // 2, jnp.bfloat16),
            shaped(rows, width // 2, jnp.bfloat16),
            shaped(width, width, jnp.bfloat16),
            shaped(width, hidden_units, jnp.bfloat16),
            shaped(hidden_units, width, jnp.bfloat16),
            shaped(1, hidden_units, jnp.float32),
            shaped(8, width, jnp.float32),
        ],
        grid_spec=pltpu.PrefetchScalarGridSpec(
            num_scalar_prefetch=1,
            grid=(steps,),
            in_specs=[whole, whole, scale, whole, scale, whole, whole, tile, tile]
            + piece_specs(pieces, steps)
            + [whole_block(vectors.shape)],
            out_specs=[whole, halves, halves, square, across, down, line, whole_block((8, width))],
            scratch_shapes=[
                pltpu.VMEM((rows, width), jnp.float32),
                pltpu.VMEM((rows, width), jnp.bfloat16),
                pltpu.VMEM((rows, width), jnp.float32),
                pltpu.VMEM((width, width), jnp.bfloat16),
                pltpu.VMEM((width, width), jnp.bfloat16),
            ],
        ),
        compiler_params=pltpu.CompilerParams(vmem_limit_bytes=48 * 2**20),
        cost_estimate=pl.CostEstimate(
            flops=2 * rows * width * (2 * width + 4 * hidden_units),
            bytes_accessed=40 * 2**20,
            transcendentals=0,
        ),
        name="tail_backward",
    )(
        me,
        grad,
        norm_two,
        scale_two,
        norm_one,
        scale_one,
        low,
        mixed,
        slope,
        active,
        *[in_main(pieces)] * 3,
        vectors,
    )


def gather_all(local):
    places, share, width = local.shape
    gathered = lax.all_gather(local.reshape(-1, width), BOTH, axis=0, tiled=False)
    return gathered.reshape(4, 8, places, share, width)


def join_kernel(me, a_ref, b_ref, project_ref, small_ref):
    half = a_ref.shape[-1]
    for y_bit in range(GRP_Y):
        y = y_bit ^ me[0]
        for x_bit in range(SHARD_X):
            for z_bits in range(SHARD_Z):
                shard = (z_bits ^ me[3]) * SHARD_X + (x_bit ^ me[2])
                project_ref[shard, y, :, :half] = a_ref[y_bit, x_bit, z_bits, 0]
                project_ref[shard, y, :, half : 2 * half] = a_ref[y_bit, x_bit, z_bits, 1]
                project_ref[shard, y, :, 2 * half :] = b_ref[x_bit, y_bit, z_bits, 0]
                if y_bit == 0:
                    small_ref[shard, :, :half] = b_ref[x_bit, y_bit, z_bits, 1, 0:8, :]
                    small_ref[shard, :, half:] = b_ref[x_bit, y_bit, z_bits, 1, 8:16, :]


def gather_first(me, local, rows):
    part, half = local.shape[1:]
    pair = jnp.stack([local, swap_z(local, 1)])
    pair, rows = lax.optimization_barrier((pair, rows))
    window = window_of(rows)
    four = jnp.concatenate([pair, swap_z(pair, 2)])
    a_part, b_part = four[:, :2], four[:, 2:]
    a_two = jnp.stack([a_part, swap_x(a_part)])
    b_two = jnp.stack([b_part, swap_y(b_part)])
    a_four = jnp.stack([a_two, swap_y(a_two)])
    b_four = jnp.stack([b_two, swap_x(b_two)])
    project, small = pl.pallas_call(
        join_kernel,
        out_shape=[
            jax.ShapeDtypeStruct((8, 2, part, 3 * half), local.dtype),
            jax.ShapeDtypeStruct((8, 8, 2 * half), local.dtype),
        ],
        grid_spec=pltpu.PrefetchScalarGridSpec(
            num_scalar_prefetch=1,
            grid=(1,),
            in_specs=[whole_block(a_four.shape)] * 2,
            out_specs=[whole_block((8, 2, part, 3 * half)), whole_block((8, 8, 2 * half))],
        ),
        compiler_params=pltpu.CompilerParams(vmem_limit_bytes=24 * 2**20),
        name="join_projection",
    )(me, a_four, b_four)
    return project.reshape(-1, 3 * half), small, four, rows, window


def on_device_turned(
    tokens,
    cotangent,
    seq_lengths,
    seq_order,
    w_project,
    w_mixer,
    w_expand,
    w_reduce,
    biases,
    norm_gains,
):
    row_count, width = tokens.shape
    shard_index = lax.axis_index("shard")
    quarter = lax.axis_index("grp")
    z, x = shard_index // SHARD_X, shard_index % SHARD_X
    y, core = quarter // GRP_CORE, quarter % GRP_CORE
    me = jnp.stack([y, core, x, z]).astype(jnp.int32)
    hidden_units = w_expand.shape[2]
    group_slots = row_count * 8
    seq_count = seq_lengths.shape[1]
    seq_ends = group_ends(seq_lengths, seq_order, y * GRP_CORE + x)
    block_index = z * GRP_CORE + jnp.stack([core, 1 - core])
    slot_index = block_index[:, None] * row_count + jnp.arange(row_count, dtype=jnp.int32)[None, :]
    slot_index = slot_index.reshape(-1)
    before_slot = seq_ends[None, :] <= slot_index[:, None]
    own_segment = jnp.sum(before_slot[:row_count].astype(jnp.int32), axis=1, dtype=jnp.int32)
    starts = jnp.max(jnp.where(before_slot, seq_ends[None, :], 0), axis=1)
    stops = jnp.min(jnp.where(before_slot, group_slots, seq_ends[None, :]), axis=1)
    window_begin = (z - 1) * GRP_CORE * row_count
    low = starts - window_begin
    high = stops - window_begin
    low_line = jnp.broadcast_to(low[None, :], (8, 2 * row_count))
    high_line = jnp.broadcast_to(high[None, :], (8, 2 * row_count))
    places = [(1, 0, 2)[t // 2] + ((t % 2) ^ core) * 3 for t in range(6)]
    bounds = jnp.stack(
        [
            low[0] // KEY_ROWS,
            (high[row_count - 1] + KEY_ROWS - 1) // KEY_ROWS,
            low[row_count] // KEY_ROWS,
            (high[2 * row_count - 1] + KEY_ROWS - 1) // KEY_ROWS,
        ]
        + places
    ).astype(jnp.int32)
    valid_rows = (own_segment < seq_count).astype(jnp.float32)[:, None]

    small = jnp.concatenate(
        [jnp.concatenate([biases[i], norm_gains[i]]) for i in range(LAYERS)]
    ).reshape(-1, width)
    share = w_project.shape[1] // 4
    deep = w_reduce.shape[1] // 4
    bias_count = biases.shape[1]
    small_rows = small.shape[0]
    small = jnp.concatenate([small, jnp.zeros((8 - small_rows, width), small.dtype)])
    near_first, far_first, far_last = pick_quarters(
        me, w_project, w_mixer, w_expand, w_reduce, small
    )
    state_low = turn_rows(tokens)
    state_grad = turn_rows(cotangent)
    project_first, small_all, arrived, state_low, first_window = gather_first(
        me, near_first, state_low
    )
    far_first, arrived = lax.optimization_barrier((far_first, arrived))
    far_kinds = ("columns", "columns", "rows")
    far_shapes = [(share, width), (share, hidden_units), (deep, width)]
    far_count = far_last.shape[0]
    pieces = gather_all(far_first)
    project_last = unpack_weights_of(pieces, far_count, 3, ("columns",), [(share, 3 * width)])[0]
    project_last = jnp.concatenate(
        [half_of(project_last[:, i * width : (i + 1) * width], 1, core) for i in range(3)], axis=1
    )
    tail_pieces = [pieces, gather_all(far_last)]
    small_all = small_all[:, :small_rows].reshape(8, LAYERS, -1)
    weights = []
    vector_rows = []
    for layer_index, project in enumerate([project_first, project_last]):
        bias_vec = small_all[:, layer_index, :bias_count].reshape(-1)
        gain_vec = small_all[:, layer_index, bias_count:].reshape(-1)
        weights.append(
            unpack_weights((project, None, None, None, bias_vec, gain_vec), width, hidden_units)
        )
        vector_rows.append(
            jnp.concatenate([bias_vec, gain_vec]).astype(jnp.float32).reshape(-1, width)
        )

    hidden_state = state_low.astype(jnp.float32)
    kept_list = []
    for layer_index in range(LAYERS):
        project, mixing, expand, shrink, bias_list, gain_one, gain_two = weights[layer_index]
        bias_q, bias_v, bias_mix, shift_one, bias_in, bias_out, shift_two = bias_list
        state_window = first_window if layer_index == 0 else window_of(state_low)
        half = width // 2
        far_begin = 3 * row_count
        queries = [
            (
                jnp.dot(
                    state_window[begin_at : begin_at + row_count],
                    project[:, :half],
                    preferred_element_type=jnp.float32,
                )
                + half_of(bias_q, 0, core)
            ).astype(jnp.bfloat16)
            for begin_at in (0, far_begin)
        ]
        key_value = (
            jnp.dot(state_window, project[:, half:], preferred_element_type=jnp.float32)
            + jnp.concatenate([jnp.zeros((half,), jnp.float32), half_of(bias_v, 0, core)])
        ).astype(jnp.bfloat16)
        own_mix, far_mix, own_wide, far_wide, lse = flash_forward(bounds, queries, key_value, low_line, high_line)
        far_mix = swap_core(far_mix)
        tail_vectors = vector_rows[layer_index]
        (
            mixed_low,
            norm_one,
            scale_one,
            normed_low,
            active_low,
            slope,
            norm_two,
            scale_two,
            hidden_state,
            next_low,
        ) = tail_forward(
            me, own_mix, far_mix, hidden_state, tail_pieces[layer_index], bias_in[None], tail_vectors
        )
        kept_list.append(
            (
                state_low,
                state_window,
                queries,
                key_value,
                (own_wide, far_wide),
                lse,
                (norm_two, scale_two, norm_one, scale_one, normed_low, mixed_low, slope, active_low),
                tail_vectors,
            )
        )
        state_low = next_low
    activations = turn_rows((hidden_state * valid_rows).astype(jnp.bfloat16))
    state_grad = state_grad.astype(jnp.float32) * valid_rows
    results = [None] * LAYERS
    spreads = [None] * LAYERS
    for layer_index in reversed(range(LAYERS)):
        layer_low, state_window, queries, key_value, wides, lse, kept, tail_vectors = kept_list[
            layer_index
        ]
        project, mixing, expand, shrink, *unused = weights[layer_index]
        (
            sum_one_grad,
            own_mix_grad,
            far_mix_grad,
            mixing_grad,
            expand_grad,
            shrink_grad,
            bias_in_grad,
            vector_grads,
        ) = tail_backward(me, state_grad, kept, tail_pieces[layer_index], tail_vectors)
        bias_mix_grad, gain_one_grad, shift_one_grad, bias_out_grad, gain_two_grad, shift_two_grad = [
            vector_grads[i] for i in range(6)
        ]
        mixed_grads = (own_mix_grad, swap_core(far_mix_grad))
        own_grad, far_grad, key_value_grad = flash_backward(
            bounds, queries, key_value, mixed_grads, wides, lse, low_line, high_line
        )
        if layer_index == 0:
            key_value_grad, started = lax.optimization_barrier((key_value_grad, started))
        query_term = jnp.einsum(
            "td,te->de", layer_low, own_grad, preferred_element_type=jnp.float32
        ) + jnp.einsum(
            "td,te->de",
            state_window[far_begin : far_begin + row_count],
            far_grad,
            preferred_element_type=jnp.float32,
        )
        key_value_term = jnp.einsum(
            "td,te->de", state_window, key_value_grad, preferred_element_type=jnp.float32
        )
        bias_q_grad = jnp.sum(own_grad, axis=0, dtype=jnp.float32) + jnp.sum(
            far_grad, axis=0, dtype=jnp.float32
        )
        bias_v_grad = jnp.sum(key_value_grad[:, half:], axis=0, dtype=jnp.float32)
        window_grad = jnp.einsum(
            "te,de->td", key_value_grad, project[:, half:], preferred_element_type=jnp.float32
        )
        own_part = jnp.einsum(
            "te,de->td", own_grad, project[:, :half], preferred_element_type=jnp.float32
        )
        far_part = jnp.einsum(
            "te,de->td", far_grad, project[:, :half], preferred_element_type=jnp.float32
        )
        near_terms = jnp.concatenate(
            [window_grad[:row_count] + own_part, window_grad[row_count:far_begin]]
        )
        far_terms = jnp.concatenate(
            [
                window_grad[far_begin : far_begin + row_count] + far_part,
                window_grad[far_begin + row_count :],
            ]
        )
        state_grad = sum_one_grad + window_back(near_terms, far_terms, row_count)
        zeros_two = jnp.zeros((2 * width,), jnp.float32)
        vectors = jnp.concatenate(
            [
                zeros_two,
                bias_mix_grad,
                shift_one_grad,
                bias_in_grad[0],
                bias_out_grad,
                shift_two_grad,
            ]
        ).reshape(8, -1)
        gains = jnp.concatenate([gain_one_grad, gain_two_grad]).reshape(8, -1)
        vectors = jnp.concatenate([vectors, gains], axis=1).astype(jnp.bfloat16)
        vectors = vectors.reshape(8, 4, 1, -1).transpose(1, 0, 2, 3)
        vectors = jnp.pad(vectors, ((0, 0), (0, 0), (0, 7), (0, width - vectors.shape[3])))
        terms = (mixing_grad, expand_grad, shrink_grad)
        pieces = pack_terms(terms, far_kinds, width, vectors)
        fed = lax.psum_scatter(
            pieces.reshape(32, -1, width), BOTH, scatter_dimension=0, tiled=True
        )[0]
        lines = jnp.zeros((8 * bias_count,), jnp.float32)
        lines = lax.dynamic_update_slice(lines, bias_q_grad, (core * half,))
        lines = lax.dynamic_update_slice(lines, bias_v_grad, (width + core * half,))
        lines = lines.reshape(8, 2, -1).transpose(1, 0, 2).astype(jnp.bfloat16)
        lines = jnp.pad(lines, ((0, 0), (0, 0), (0, width - lines.shape[2])))
        lines = jnp.pad(lines.reshape(2, 8, 2, half), ((0, 0), (0, 0), (0, 6), (0, 0)))
        query_term = query_term.astype(jnp.bfloat16)
        key_value_term = key_value_term.astype(jnp.bfloat16)
        if layer_index > 0:
            state_grad, query_term, key_value_term = lax.optimization_barrier(
                (state_grad, query_term, key_value_term)
            )
        spreads[layer_index] = spread_terms(me, query_term, key_value_term, lines)
        if layer_index > 0:
            started = swap_x(spreads[layer_index][:, 1])
        results[layer_index] = gather_quarters(fed)
    attended = gather_quarters(scatter_terms(*spreads, started))
    results = [
        (attended[:, :, 4 * layer_index : 4 * (layer_index + 1)], results[layer_index])
        for layer_index in range(LAYERS)
    ]
    outs = finish_shares(me, results, hidden_units, deep)
    quarter_len = (bias_count + norm_gains.shape[1]) // 4
    vectors = outs[5][:, :, 0, :quarter_len].reshape(LAYERS, -1)
    lines = outs[4][:, :, :2].reshape(LAYERS, GRP_Y, GRP_CORE, width)[..., : bias_count // 2]
    lines = jnp.sum(lines, axis=2).reshape(LAYERS, bias_count)
    input_grad = turn_rows(state_grad.astype(jnp.bfloat16)).astype(jnp.float32)
    return (
        activations,
        input_grad,
        outs[0],
        outs[1],
        outs[2],
        outs[3],
        vectors[:, :bias_count] + lines,
        vectors[:, bias_count:],
    )


def solution(mesh):
    in_specs = (
        P(("grp", "shard"), None),
        P(("grp", "shard"), None),
        P(),
        P(),
        P(None, "shard", None),
        P(None, "shard", None),
        P(None, "shard", None),
        P(None, "shard", None),
        P(None, "shard"),
        P(None, "shard"),
    )
    out_specs = (
        P(("grp", "shard"), None),
        P(("grp", "shard"), None),
        P(None, "shard", None),
        P(None, "shard", None),
        P(None, "shard", None),
        P(None, "shard", None),
        P(None, "shard"),
        P(None, "shard"),
    )
    body = on_device_turned if mesh.shape["shard"] == 8 and mesh.shape["grp"] == 4 else on_device
    return jax.shard_map(
        body, mesh=mesh, in_specs=in_specs, out_specs=out_specs, check_vma=False
    )
```

```python
import functools

import jax
import jax.numpy as jnp
from jax import lax
from jax.experimental import pallas as pl
from jax.experimental.pallas import tpu as pltpu
from jax.sharding import PartitionSpec as P

HEADS = 12
LAYERS = 2
SEQ_MAX = 2048


EPSILON = 1e-12
NEGATIVE = -1e30


def passed_along(shard, axis, by):
    size = lax.axis_size(axis)
    pairs = [(i, i + by) for i in range(size) if 0 <= i + by < size]
    return lax.ppermute(shard, axis, pairs)


def layer_norm(values, gain, shift):
    middle = jnp.mean(values, axis=-1, keepdims=True)
    centered = values - middle
    spread = jnp.mean(centered * centered, axis=-1, keepdims=True)
    return centered * lax.rsqrt(spread + EPSILON) * gain + shift


def gelu_exact(values):
    return jax.nn.gelu(values, approximate=False)


def keep_same(carried):
    return carried


def group_ends(seq_lengths, seq_order, group_index):
    lengths_row = lax.dynamic_index_in_dim(seq_lengths, group_index, 0, keepdims=False)
    order_row = lax.dynamic_index_in_dim(seq_order, group_index, 0, keepdims=False)
    places = jnp.arange(lengths_row.shape[0], dtype=jnp.int32)
    picked = order_row[:, None] == places[None, :]
    placed = jnp.sum(jnp.where(picked, lengths_row[None, :], 0), axis=1, dtype=jnp.int32)
    return jnp.cumsum(placed, dtype=jnp.int32)


def slot_segments(slot_index, seq_ends):
    flattened = slot_index.reshape(-1)
    counted = jnp.sum(
        (seq_ends[None, :] <= flattened[:, None]).astype(jnp.int32), axis=1, dtype=jnp.int32
    )
    return counted.reshape(slot_index.shape)


def unpack_weights(weights, width, hidden_units):
    bias_vec = weights[4].astype(jnp.float32)
    gain_vec = weights[5].astype(jnp.float32)
    piece_lens = [width, width, width, width, hidden_units, width, width]
    bias_list = []
    begin_at = 0
    for piece_len in piece_lens:
        bias_list.append(bias_vec[begin_at : begin_at + piece_len])
        begin_at = begin_at + piece_len
    return (
        weights[0],
        weights[1],
        weights[2],
        weights[3],
        bias_list,
        gain_vec[:width],
        gain_vec[width:],
    )


def block_probs(queries, keys_block, seg_block, own_segment, log_total, score_scale):
    raw_scores = jnp.einsum("qhd,khd->hqk", queries, keys_block, preferred_element_type=jnp.float32)
    allowed = (own_segment[:, None] == seg_block[None, :])[None]
    return jnp.where(allowed, jnp.exp(raw_scores * score_scale - log_total[:, :, None]), 0.0)


def gather_window(key_rows, value_rows, reach_blocks):
    key_list = []
    value_list = []
    for step_offset in range(-reach_blocks, reach_blocks + 1):
        if step_offset == 0:
            moved = (key_rows, value_rows)
        else:
            moved = passed_along((key_rows, value_rows), "shard", -step_offset)
        key_list.append(moved[0])
        value_list.append(moved[1])
    return (jnp.stack(key_list), jnp.stack(value_list))


def return_parts(key_parts, value_parts, reach_blocks):
    key_total = key_parts[reach_blocks]
    value_total = value_parts[reach_blocks]
    for step_offset in range(-reach_blocks, reach_blocks + 1):
        if step_offset != 0:
            arrived = (
                passed_along(
                    key_parts[step_offset + reach_blocks].astype(jnp.bfloat16), "shard", step_offset
                ).astype(jnp.float32),
                passed_along(
                    value_parts[step_offset + reach_blocks].astype(jnp.bfloat16),
                    "shard",
                    step_offset,
                ).astype(jnp.float32),
            )
            key_total = key_total + arrived[0]
            value_total = value_total + arrived[1]
    return (key_total, value_total)


def attend_forward(
    queries, window_keys, window_values, window_segment, live_block, own_segment, score_scale
):
    row_count, head_count, head_dim = queries.shape

    def stats_step(carry, items):
        keys_block, seg_block, alive = items

        def stats_compute(state_pair):
            running_top, running_sum = state_pair
            allowed = (own_segment[:, None] == seg_block[None, :])[None]
            raw_scores = jnp.einsum(
                "qhd,khd->hqk", queries, keys_block, preferred_element_type=jnp.float32
            )
            scores = jnp.where(allowed, raw_scores * score_scale, NEGATIVE)
            new_top = jnp.maximum(running_top, jnp.max(scores, axis=-1))
            weighted = jnp.where(allowed, jnp.exp(scores - new_top[:, :, None]), 0.0)
            return (
                new_top,
                running_sum * jnp.exp(running_top - new_top) + jnp.sum(weighted, axis=-1),
            )

        return (lax.cond(alive, stats_compute, keep_same, carry), None)

    begin_stats = (
        jnp.full((head_count, row_count), NEGATIVE, jnp.float32),
        jnp.zeros((head_count, row_count), jnp.float32),
    )
    (running_top, running_sum), unused = lax.scan(
        stats_step, begin_stats, (window_keys, window_segment, live_block)
    )
    log_total = running_top + jnp.log(running_sum)

    def mix_step(carry, items):
        keys_block, values_block, seg_block, alive = items

        def mix_compute(state_pair):
            mixed, extra = state_pair
            probs = block_probs(queries, keys_block, seg_block, own_segment, log_total, score_scale)
            probs_low = probs.astype(jnp.bfloat16)
            rest_low = (probs - lax.optimization_barrier(probs_low).astype(jnp.float32)).astype(
                jnp.bfloat16
            )
            mixed = mixed + jnp.einsum(
                "hqk,khd->qhd", probs_low, values_block, preferred_element_type=jnp.float32
            )
            extra = extra + jnp.einsum(
                "hqk,khd->qhd", rest_low, values_block, preferred_element_type=jnp.float32
            )
            return (mixed, extra)

        return (lax.cond(alive, mix_compute, keep_same, carry), None)

    zeros_mix = jnp.zeros((row_count, head_count, head_dim), jnp.float32)
    (mixed, extra), unused = lax.scan(
        mix_step, (zeros_mix, zeros_mix), (window_keys, window_values, window_segment, live_block)
    )
    return (log_total, mixed, mixed + extra)


def attend_backward(
    queries,
    window_keys,
    window_values,
    window_segment,
    live_block,
    own_segment,
    log_total,
    delta,
    grad_low,
    score_scale,
):

    def grad_step(query_grad, items):
        keys_block, values_block, seg_block, alive = items

        def grad_compute(carried):
            probs = block_probs(queries, keys_block, seg_block, own_segment, log_total, score_scale)
            prob_grad = jnp.einsum(
                "qhd,khd->hqk", grad_low, values_block, preferred_element_type=jnp.float32
            )
            score_low = (probs * (prob_grad - delta[:, :, None])).astype(jnp.bfloat16)
            carried = carried + jnp.einsum(
                "hqk,khd->qhd", score_low, keys_block, preferred_element_type=jnp.float32
            )
            probs_low = probs.astype(jnp.bfloat16)
            value_part = jnp.einsum(
                "hqk,qhd->khd", probs_low, grad_low, preferred_element_type=jnp.float32
            )
            key_part = jnp.einsum(
                "hqk,qhd->khd", score_low, queries, preferred_element_type=jnp.float32
            )
            return (carried, (key_part, value_part))

        def skipped(carried):
            nothing = jnp.zeros(keys_block.shape, jnp.float32)
            return (carried, (nothing, nothing))

        return lax.cond(alive, grad_compute, skipped, query_grad)

    zero_grad = jnp.zeros(queries.shape, jnp.float32)
    query_grad, key_value = lax.scan(
        grad_step, zero_grad, (window_keys, window_values, window_segment, live_block)
    )
    return (query_grad, key_value)


def on_device(
    tokens,
    cotangent,
    seq_lengths,
    seq_order,
    w_project,
    w_mixer,
    w_expand,
    w_reduce,
    biases,
    norm_gains,
):
    row_count, width = tokens.shape
    shard_count = lax.axis_size("shard")
    shard_index = lax.axis_index("shard")
    group_index = lax.axis_index("grp")
    head_dim = width // HEADS
    hidden_units = w_expand.shape[2]
    score_scale = head_dim ** (-0.5)
    longest = min(SEQ_MAX, row_count * shard_count // 4)
    reach_blocks = longest // row_count
    seq_count = seq_lengths.shape[1]
    seq_ends = group_ends(seq_lengths, seq_order, group_index)
    neighbour = shard_index + jnp.arange(-reach_blocks, reach_blocks + 1, dtype=jnp.int32)
    slot_index = neighbour[:, None] * row_count + jnp.arange(row_count, dtype=jnp.int32)[None, :]
    window_segment = slot_segments(slot_index, seq_ends)
    own_segment = window_segment[reach_blocks]
    inside = (neighbour >= 0) & (neighbour < shard_count)
    live_block = (
        inside
        & (window_segment[:, 0] <= own_segment[row_count - 1])
        & (window_segment[:, row_count - 1] >= own_segment[0])
    )
    valid_rows = (own_segment < seq_count).astype(jnp.float32)[:, None]
    hidden_state = tokens.astype(jnp.float32)
    state_low = tokens
    kept_list = []
    for layer_index in range(LAYERS):
        weights = (
            lax.all_gather(w_project[layer_index], "shard", axis=0, tiled=True),
            lax.all_gather(w_mixer[layer_index], "shard", axis=0, tiled=True),
            lax.all_gather(w_expand[layer_index], "shard", axis=0, tiled=True),
            lax.all_gather(w_reduce[layer_index], "shard", axis=0, tiled=True),
            lax.all_gather(biases[layer_index], "shard", axis=0, tiled=True),
            lax.all_gather(norm_gains[layer_index], "shard", axis=0, tiled=True),
        )
        project, mixing, expand, shrink, bias_list, gain_one, gain_two = unpack_weights(
            weights, width, hidden_units
        )
        bias_q, bias_v, bias_mix, shift_one, bias_in, bias_out, shift_two = bias_list
        projected = jnp.dot(state_low, project, preferred_element_type=jnp.float32)
        projected = projected + jnp.concatenate([bias_q, jnp.zeros_like(bias_q), bias_v])
        projected_low = projected.astype(jnp.bfloat16)
        queries = projected_low[:, :width].reshape(row_count, HEADS, head_dim)
        key_rows = projected_low[:, width : 2 * width].reshape(row_count, HEADS, head_dim)
        value_rows = projected_low[:, 2 * width :].reshape(row_count, HEADS, head_dim)
        window_keys, window_values = gather_window(key_rows, value_rows, reach_blocks)
        log_total, mixed, full_mix = attend_forward(
            queries,
            window_keys,
            window_values,
            window_segment,
            live_block,
            own_segment,
            score_scale,
        )
        mixed_low = mixed.reshape(row_count, width).astype(jnp.bfloat16)
        branch = jnp.dot(mixed_low, mixing, preferred_element_type=jnp.float32) + bias_mix
        summed_one = hidden_state + branch
        normed_one = layer_norm(summed_one, gain_one, shift_one)
        normed_low = normed_one.astype(jnp.bfloat16)
        before = jnp.dot(normed_low, expand, preferred_element_type=jnp.float32) + bias_in
        active_low = gelu_exact(before).astype(jnp.bfloat16)
        feed_out = jnp.dot(active_low, shrink, preferred_element_type=jnp.float32) + bias_out
        summed_two = normed_one + feed_out
        hidden_state = layer_norm(summed_two, gain_two, shift_two)
        kept_list.append(
            (
                state_low,
                queries,
                key_rows,
                value_rows,
                window_keys,
                window_values,
                log_total,
                full_mix,
                mixed_low,
                summed_one,
                normed_low,
                before,
                active_low,
                summed_two,
                weights,
            )
        )
        state_low = hidden_state.astype(jnp.bfloat16)
    activations = (hidden_state * valid_rows).astype(jnp.bfloat16)
    state_grad = cotangent.astype(jnp.float32) * valid_rows
    results = [None] * LAYERS
    for layer_index in reversed(range(LAYERS)):
        (
            layer_low,
            queries,
            key_rows,
            value_rows,
            window_keys,
            window_values,
            log_total,
            full_mix,
            mixed_low,
            summed_one,
            normed_low,
            before,
            active_low,
            summed_two,
            kept_weights,
        ) = kept_list[layer_index]
        weights = (
            lax.all_gather(w_project[layer_index], "shard", axis=0, tiled=True),
            lax.all_gather(w_mixer[layer_index], "shard", axis=0, tiled=True),
            lax.all_gather(w_expand[layer_index], "shard", axis=0, tiled=True),
            lax.all_gather(w_reduce[layer_index], "shard", axis=0, tiled=True),
            lax.all_gather(biases[layer_index], "shard", axis=0, tiled=True),
            lax.all_gather(norm_gains[layer_index], "shard", axis=0, tiled=True),
        )
        project, mixing, expand, shrink, bias_list, gain_one, gain_two = unpack_weights(
            weights, width, hidden_units
        )
        bias_q, bias_v, bias_mix, shift_one, bias_in, bias_out, shift_two = bias_list
        unused_two, norm_pull = jax.vjp(layer_norm, summed_two, gain_two, shift_two)
        sum_two_grad, gain_two_grad, shift_two_grad = norm_pull(state_grad)
        feed_low = sum_two_grad.astype(jnp.bfloat16)
        shrink_grad = jnp.einsum(
            "tf,td->fd", active_low, feed_low, preferred_element_type=jnp.float32
        )
        bias_out_grad = jnp.sum(feed_low, axis=0, dtype=jnp.float32)
        active_grad = jnp.einsum("td,fd->tf", feed_low, shrink, preferred_element_type=jnp.float32)
        unused_gelu, gelu_pull = jax.vjp(gelu_exact, before)
        before_low = gelu_pull(active_grad)[0].astype(jnp.bfloat16)
        expand_grad = jnp.einsum(
            "td,tf->df", normed_low, before_low, preferred_element_type=jnp.float32
        )
        bias_in_grad = jnp.sum(before_low, axis=0, dtype=jnp.float32)
        normed_grad = sum_two_grad + jnp.einsum(
            "tf,df->td", before_low, expand, preferred_element_type=jnp.float32
        )
        unused_one, first_pull = jax.vjp(layer_norm, summed_one, gain_one, shift_one)
        sum_one_grad, gain_one_grad, shift_one_grad = first_pull(normed_grad)
        branch_low = sum_one_grad.astype(jnp.bfloat16)
        mixing_grad = jnp.einsum(
            "td,te->de", mixed_low, branch_low, preferred_element_type=jnp.float32
        )
        bias_mix_grad = jnp.sum(branch_low, axis=0, dtype=jnp.float32)
        mixed_grad = jnp.einsum("te,de->td", branch_low, mixing, preferred_element_type=jnp.float32)
        mixed_grad_low = mixed_grad.astype(jnp.bfloat16).reshape(row_count, HEADS, head_dim)
        delta = jnp.sum(mixed_grad_low.astype(jnp.float32) * full_mix, axis=-1).T
        query_grad, key_value = attend_backward(
            queries,
            window_keys,
            window_values,
            window_segment,
            live_block,
            own_segment,
            log_total,
            delta,
            mixed_grad_low,
            score_scale,
        )
        key_total, value_total = return_parts(key_value[0], key_value[1], reach_blocks)
        projected_grad = jnp.concatenate(
            [
                (query_grad * score_scale).reshape(row_count, width),
                (key_total * score_scale).reshape(row_count, width),
                value_total.reshape(row_count, width),
            ],
            axis=1,
        )
        projected_low = projected_grad.astype(jnp.bfloat16)
        project_grad = jnp.einsum(
            "td,te->de", layer_low, projected_low, preferred_element_type=jnp.float32
        )
        bias_q_grad = jnp.sum(projected_low[:, :width], axis=0, dtype=jnp.float32)
        bias_v_grad = jnp.sum(projected_low[:, 2 * width :], axis=0, dtype=jnp.float32)
        state_grad = sum_one_grad + jnp.einsum(
            "te,de->td", projected_low, project, preferred_element_type=jnp.float32
        )
        bias_all = jnp.concatenate(
            [
                bias_q_grad,
                bias_v_grad,
                bias_mix_grad,
                shift_one_grad,
                bias_in_grad,
                bias_out_grad,
                shift_two_grad,
            ]
        )
        gain_all = jnp.concatenate([gain_one_grad, gain_two_grad])
        shares = (
            lax.psum_scatter(
                project_grad.astype(jnp.bfloat16), "shard", scatter_dimension=0, tiled=True
            ).astype(jnp.float32),
            lax.psum_scatter(
                mixing_grad.astype(jnp.bfloat16), "shard", scatter_dimension=0, tiled=True
            ).astype(jnp.float32),
            lax.psum_scatter(
                expand_grad.astype(jnp.bfloat16), "shard", scatter_dimension=0, tiled=True
            ).astype(jnp.float32),
            lax.psum_scatter(
                shrink_grad.astype(jnp.bfloat16), "shard", scatter_dimension=0, tiled=True
            ).astype(jnp.float32),
            lax.psum_scatter(
                bias_all.astype(jnp.bfloat16), "shard", scatter_dimension=0, tiled=True
            ).astype(jnp.float32),
            lax.psum_scatter(
                gain_all.astype(jnp.bfloat16), "shard", scatter_dimension=0, tiled=True
            ).astype(jnp.float32),
        )
        shares = (
            lax.psum(shares[0].astype(jnp.bfloat16), "grp").astype(jnp.float32),
            lax.psum(shares[1].astype(jnp.bfloat16), "grp").astype(jnp.float32),
            lax.psum(shares[2].astype(jnp.bfloat16), "grp").astype(jnp.float32),
            lax.psum(shares[3].astype(jnp.bfloat16), "grp").astype(jnp.float32),
            lax.psum(shares[4].astype(jnp.bfloat16), "grp").astype(jnp.float32),
            lax.psum(shares[5].astype(jnp.bfloat16), "grp").astype(jnp.float32),
        )
        results[layer_index] = shares
    stacked = [jnp.stack([layer_share[member] for layer_share in results]) for member in range(6)]
    return (
        activations,
        state_grad,
        stacked[0],
        stacked[1],
        stacked[2],
        stacked[3],
        stacked[4],
        stacked[5],
    )


HEAD_SCALE = 0.125


def in_main(array):
    return pltpu.with_memory_space_constraint(array, pltpu.HBM)


def fold_rows(values, combine):
    total = values[:8]
    for begin_at in range(8, values.shape[0], 8):
        total = combine(total, values[begin_at : begin_at + 8])
    return total


def halves_of(block):
    lane = lax.broadcasted_iota(jnp.int32, block.shape, 1)
    nothing = jnp.zeros_like(block)
    return (jnp.where(lane < 64, block, nothing), jnp.where(lane < 64, nothing, block))


def turned_dot(keys, queries):
    return lax.dot_general(
        keys, queries, (((1,), (1,)), ((), ())), preferred_element_type=jnp.float32
    )


def across_dot(weight, values):
    return lax.dot_general(
        weight, values, (((0,), (0,)), ((), ())), preferred_element_type=jnp.float32
    )


KEY_ROWS = 512
KEY_TILES = 5


def key_rows(tile):
    return pl.ds(pl.multiple_of(tile * KEY_ROWS, KEY_ROWS), KEY_ROWS)


def fill_mask(first, last, low, high, mask_scr, index):
    def mask_step(key_tile, carry):
        shape = (KEY_ROWS, low.shape[1])
        place = lax.broadcasted_iota(jnp.int32, shape, 0) + key_tile * KEY_ROWS
        allowed = (place >= low) & (place < high)
        mask_scr[index, key_rows(key_tile - first), :] = jnp.where(allowed, 0.0, NEGATIVE)
        return carry

    lax.fori_loop(first, last, mask_step, 0)


def flash_forward_kernel(
    bounds,
    a_ref,
    b_ref,
    kv_ref,
    low_ref,
    high_ref,
    a_mix,
    b_mix,
    a_wide,
    b_wide,
    lse_ref,
    mask_scr,
    score_scr,
):
    rows, width = a_ref.shape
    pairs = width // 128
    for index in range(2):
        span = slice(index * rows, (index + 1) * rows)
        fill_mask(
            bounds[2 * index],
            bounds[2 * index + 1],
            low_ref[0:1, span],
            high_ref[0:1, span],
            mask_scr,
            index,
        )

    def pair_step(pair, unused):
        lanes = pl.ds(pl.multiple_of(pair * 128, 128), 128)
        value_lanes = pl.ds(pl.multiple_of(pair * 128 + width, 128), 128)
        for index, (q_ref, mix_ref, wide_ref) in enumerate(
            ((a_ref, a_mix, a_wide), (b_ref, b_mix, b_wide))
        ):
            first, last = bounds[2 * index], bounds[2 * index + 1]
            heads = halves_of(q_ref[:, lanes] * jnp.bfloat16(HEAD_SCALE))

            def score_step(key_tile, tops, index=index, heads=heads, first=first):
                keys = kv_ref[key_rows(bounds[4 + key_tile]), lanes]
                place = key_rows(key_tile - first)
                mask = mask_scr[index, place, :]
                out = []
                for head in range(2):
                    scores = turned_dot(keys, heads[head]) + mask
                    score_scr[head, place, :] = scores
                    out.append(jnp.maximum(tops[head], fold_rows(scores, jnp.maximum)))
                return tuple(out)

            floor = jnp.full((8, rows), NEGATIVE, jnp.float32)
            tops = lax.fori_loop(first, last, score_step, (floor, floor))
            tops = [jnp.max(top, axis=0, keepdims=True) for top in tops]

            def mix_step(key_tile, carry, tops=tops, first=first):
                values = kv_ref[key_rows(bounds[4 + key_tile]), value_lanes].T
                totals, mixed = [], []
                for head in range(2):
                    weight = jnp.exp(score_scr[head, key_rows(key_tile - first), :] - tops[head])
                    totals.append(carry[head] + fold_rows(weight, jnp.add))
                    mixed.append(
                        carry[2 + head]
                        + jnp.dot(
                            values[head * 64 : (head + 1) * 64],
                            weight.astype(jnp.bfloat16),
                            preferred_element_type=jnp.float32,
                        )
                    )
                return (totals[0], totals[1], mixed[0], mixed[1])

            zero = jnp.zeros((8, rows), jnp.float32)
            nothing = jnp.zeros((64, rows), jnp.float32)
            carry = lax.fori_loop(first, last, mix_step, (zero, zero, nothing, nothing))
            totals = [jnp.sum(total, axis=0, keepdims=True) for total in carry[:2]]
            mixed = jnp.concatenate(
                [carry[2] * (1.0 / totals[0]), carry[3] * (1.0 / totals[1])], axis=0
            ).T
            wide_ref[:, lanes] = mixed
            mix_ref[:, lanes] = mixed.astype(jnp.bfloat16)
            lse_rows = [tops[head] + jnp.log(totals[head]) for head in range(2)]
            lse_ref[
                pl.ds(pl.multiple_of(pair * 8, 8), 8), index * rows : (index + 1) * rows
            ] = jnp.concatenate([jnp.broadcast_to(line, (4, rows)) for line in lse_rows])
        return unused

    lax.fori_loop(0, pairs, pair_step, 0)


def flash_backward_kernel(
    bounds,
    a_ref,
    b_ref,
    kv_ref,
    a_grad_ref,
    b_grad_ref,
    a_wide,
    b_wide,
    lse_ref,
    low_ref,
    high_ref,
    a_out,
    b_out,
    kv_out,
    mask_scr,
    k_acc,
    v_acc,
):
    rows, width = a_ref.shape
    pairs = width // 128
    tiles = kv_ref.shape[0] // KEY_ROWS
    for index in range(2):
        span = slice(index * rows, (index + 1) * rows)
        fill_mask(
            bounds[2 * index],
            bounds[2 * index + 1],
            low_ref[0:1, span],
            high_ref[0:1, span],
            mask_scr,
            index,
        )

    def pair_step(pair, unused):
        lanes = pl.ds(pl.multiple_of(pair * 128, 128), 128)
        value_lanes = pl.ds(pl.multiple_of(pair * 128 + width, 128), 128)
        lse_rows = lse_ref[pl.ds(pl.multiple_of(pair * 8, 8), 8), :]
        k_acc[...] = jnp.zeros_like(k_acc)
        v_acc[...] = jnp.zeros_like(v_acc)
        ways = (((1,), (1,)), ((), ()))
        for index, (q_ref, grad_ref, wide_ref, q_out) in enumerate(
            ((a_ref, a_grad_ref, a_wide, a_out), (b_ref, b_grad_ref, b_wide, b_out))
        ):
            first, last = bounds[2 * index], bounds[2 * index + 1]
            heads = halves_of(q_ref[:, lanes] * jnp.bfloat16(HEAD_SCALE))
            grads = halves_of(grad_ref[:, lanes])
            turned_q = (q_ref[:, lanes] * jnp.bfloat16(HEAD_SCALE)).T
            turned_grad = grad_ref[:, lanes].T
            span = slice(index * rows, (index + 1) * rows)
            lse = (lse_rows[0:1, span], lse_rows[4:5, span])

            product = (grad_ref[:, lanes].astype(jnp.float32) * wide_ref[:, lanes]).T
            deltas = (
                jnp.sum(product[:64], axis=0, keepdims=True),
                jnp.sum(product[64:], axis=0, keepdims=True),
            )

            def grad_step(
                key_tile,
                q_sum,
                index=index,
                heads=heads,
                grads=grads,
                lse=lse,
                deltas=deltas,
                first=first,
                turned_q=turned_q,
                turned_grad=turned_grad,
            ):
                source = key_rows(bounds[4 + key_tile])
                columns = key_rows(bounds[4 + key_tile])
                keys = kv_ref[source, lanes]
                turned_keys = keys.T
                values = kv_ref[source, value_lanes]
                mask = mask_scr[index, key_rows(key_tile - first), :]
                out = []
                for head in range(2):
                    part = slice(head * 64, (head + 1) * 64)
                    scores = turned_dot(keys, heads[head])
                    slope = turned_dot(values, grads[head])
                    probs = jnp.exp((scores - lse[head]) + mask)
                    low_slope = (probs * (slope - deltas[head])).astype(jnp.bfloat16)
                    v_acc[part, columns] += lax.dot_general(
                        turned_grad[part],
                        probs.astype(jnp.bfloat16),
                        ways,
                        preferred_element_type=jnp.float32,
                    )
                    k_acc[part, columns] += lax.dot_general(
                        turned_q[part], low_slope, ways, preferred_element_type=jnp.float32
                    )
                    out.append(
                        q_sum[head]
                        + jnp.dot(turned_keys[part], low_slope, preferred_element_type=jnp.float32)
                    )
                return tuple(out)

            nothing = jnp.zeros((64, rows), jnp.float32)
            q_parts = lax.fori_loop(first, last, grad_step, (nothing, nothing))
            q_part = jnp.concatenate(q_parts, axis=0).T
            q_out[:, lanes] = (q_part * HEAD_SCALE).astype(jnp.bfloat16)

        def store_step(tile, carry):
            source = key_rows(tile)
            kv_out[source, lanes] = k_acc[:, source].T.astype(jnp.bfloat16)
            kv_out[source, value_lanes] = v_acc[:, source].T.astype(jnp.bfloat16)
            return carry

        lax.fori_loop(0, tiles, store_step, 0)
        return unused

    lax.fori_loop(0, pairs, pair_step, 0)


def whole_block(shape):
    return pl.BlockSpec(shape, lambda i, b: (0,) * len(shape), pipeline_mode=pl.Buffered(1))


def flash_forward(bounds, queries, key_value, low, high):
    rows, width = queries[0].shape
    window = key_value.shape[0]
    pairs = width // 128
    own = whole_block((rows, width))
    line = whole_block((8, 2 * rows))
    return pl.pallas_call(
        flash_forward_kernel,
        out_shape=(
            jax.ShapeDtypeStruct((rows, width), jnp.bfloat16),
            jax.ShapeDtypeStruct((rows, width), jnp.bfloat16),
            jax.ShapeDtypeStruct((rows, width), jnp.float32),
            jax.ShapeDtypeStruct((rows, width), jnp.float32),
            jax.ShapeDtypeStruct((pairs * 8, 2 * rows), jnp.float32),
        ),
        grid_spec=pltpu.PrefetchScalarGridSpec(
            num_scalar_prefetch=1,
            grid=(1,),
            in_specs=[own, own, whole_block((window, 2 * width)), line, line],
            out_specs=[own, own, own, own, whole_block((pairs * 8, 2 * rows))],
            scratch_shapes=[
                pltpu.VMEM((2, KEY_TILES * KEY_ROWS, rows), jnp.float32),
                pltpu.VMEM((2, KEY_TILES * KEY_ROWS, rows), jnp.float32),
            ],
        ),
        compiler_params=pltpu.CompilerParams(vmem_limit_bytes=44 * 2**20),
        cost_estimate=pl.CostEstimate(
            flops=8 * rows * width * 2560, bytes_accessed=12 * 2**20, transcendentals=rows * 12 * 2560
        ),
        name="flash_forward",
    )(bounds, queries[0], queries[1], key_value, low, high)


def flash_backward(bounds, queries, key_value, grads, wides, lse, low, high):
    rows, width = queries[0].shape
    window = key_value.shape[0]
    pairs = width // 128
    own = whole_block((rows, width))
    wide = whole_block((window, 2 * width))
    line = whole_block((8, 2 * rows))
    return pl.pallas_call(
        flash_backward_kernel,
        out_shape=(
            jax.ShapeDtypeStruct((rows, width), jnp.bfloat16),
            jax.ShapeDtypeStruct((rows, width), jnp.bfloat16),
            jax.ShapeDtypeStruct((window, 2 * width), jnp.bfloat16),
        ),
        grid_spec=pltpu.PrefetchScalarGridSpec(
            num_scalar_prefetch=1,
            grid=(1,),
            in_specs=[own, own, wide] + [own] * 4 + [whole_block((pairs * 8, 2 * rows)), line, line],
            out_specs=[own, own, wide],
            scratch_shapes=[
                pltpu.VMEM((2, KEY_TILES * KEY_ROWS, rows), jnp.float32),
                pltpu.VMEM((128, window), jnp.float32),
                pltpu.VMEM((128, window), jnp.float32),
            ],
        ),
        compiler_params=pltpu.CompilerParams(vmem_limit_bytes=56 * 2**20),
        cost_estimate=pl.CostEstimate(
            flops=20 * rows * width * 2560,
            bytes_accessed=20 * 2**20,
            transcendentals=rows * 12 * 2560,
        ),
        name="flash_backward",
    )(bounds, *queries, key_value, *grads, *wides, lse, low, high)


GRP_Y, GRP_CORE, SHARD_Z, SHARD_X = 2, 2, 4, 2
BOTH = ("grp", "shard")


def device_pairs(place):
    pairs = []
    for y in range(GRP_Y):
        for core in range(GRP_CORE):
            for z in range(SHARD_Z):
                for x in range(SHARD_X):
                    target = place(y, core, z, x)
                    if target is not None:
                        ty, tcore, tz, tx = target
                        pairs.append(
                            (
                                (y * GRP_CORE + core) * SHARD_Z * SHARD_X + z * SHARD_X + x,
                                (ty * GRP_CORE + tcore) * SHARD_Z * SHARD_X + tz * SHARD_X + tx,
                            )
                        )
    return pairs


def send(values, place):
    return lax.ppermute(values, BOTH, device_pairs(place))


def turn_rows(values):
    return send(values, lambda y, core, z, x: (y, x, z, core))


def swap_core(values):
    return send(values, lambda y, core, z, x: (y, 1 - core, z, x))


def send_up(values):
    return send(values, lambda y, core, z, x: (y, core, z + 1, x) if z + 1 < SHARD_Z else None)


def send_down(values):
    return send(values, lambda y, core, z, x: (y, core, z - 1, x) if z > 0 else None)


def window_of(rows):
    near = jnp.concatenate([rows, send_up(rows), send_down(rows)])
    return jnp.concatenate([near, swap_core(near)])


def window_back(near, far, count):
    total = near + swap_core(far.astype(jnp.bfloat16)).astype(jnp.float32)
    below = total[count : 2 * count].astype(jnp.bfloat16)
    above = total[2 * count :].astype(jnp.bfloat16)
    return (
        total[:count]
        + send_down(below).astype(jnp.float32)
        + send_up(above).astype(jnp.float32)
    )


def half_of(values, axis, index):
    count = values.shape[axis] // 2
    return lax.dynamic_slice_in_dim(values, index * count, count, axis)


def unpack_kernel(kinds, in_ref, *outs):
    width = in_ref.shape[-1]
    share = in_ref.shape[3]
    place = 0
    for kind, ref in zip(kinds, outs):
        if kind == "columns":
            for column in range(ref.shape[-1] // width):
                ref[:, 0, :, column * width : (column + 1) * width] = in_ref[0, :, place]
                place += 1
        else:
            for piece in range(ref.shape[2] // share):
                ref[:, 0, piece * share : (piece + 1) * share, :] = in_ref[0, :, place]
                place += 1


def unpack_weights_of(pieces, begin_at, places, kinds, shapes):
    quarters, shards, unused, share, width = pieces.shape
    outs = pl.pallas_call(
        functools.partial(unpack_kernel, kinds),
        out_shape=[
            pltpu.HBM((shards, quarters, rows, wide), pieces.dtype) for rows, wide in shapes
        ],
        grid=(quarters,),
        in_specs=[
            pl.BlockSpec(
                (1, shards, places, share, width), lambda q: (q, 0, begin_at // places, 0, 0)
            )
        ],
        out_specs=[
            pl.BlockSpec((shards, 1, rows, wide), lambda q: (0, q, 0, 0)) for rows, wide in shapes
        ],
        compiler_params=pltpu.CompilerParams(vmem_limit_bytes=32 * 2**20),
        cost_estimate=pl.CostEstimate(
            flops=0, bytes_accessed=128 * places * share * width, transcendentals=0
        ),
        name="unpack_weights",
    )(in_main(pieces))
    return [out.reshape(-1, out.shape[-1]) for out in outs]


def pick_kernel(
    me, near_ref, project_ref, mixer_ref, expand_ref, reduce_ref, small_ref, a_out, b_out, c_out
):
    part, half = a_out.shape[-2:]
    for column in range(3):
        begin_at = pl.multiple_of(column * 2 * half + me[1] * half, 128)
        a_out[column] = near_ref[0, :, pl.ds(begin_at, half)]
    a_out[3] = jnp.zeros((part, half), a_out.dtype)
    a_out[3, 0:8, :] = small_ref[:, :half]
    a_out[3, 8:16, :] = small_ref[:, half:]
    share, width = b_out.shape[-2:]
    wide = expand_ref.shape[-1] // width
    for layer, ref in enumerate((b_out, c_out)):
        deep = reduce_ref.shape[1] // share
        for piece in range(deep):
            ref[piece] = reduce_ref[layer, piece * share : (piece + 1) * share, :]
        for column in range(wide):
            ref[deep + column] = expand_ref[layer, :, column * width : (column + 1) * width]
        ref[deep + wide] = mixer_ref[layer]
    far = c_out.shape[0]
    for column in range(3):
        b_out[far + column] = project_ref[0, :, column * width : (column + 1) * width]


def pick_quarters(me, project, mixer, expand, reduce, small):
    share, width = mixer.shape[1] // 4, mixer.shape[2]
    far = 1 + expand.shape[2] // width + reduce.shape[1] // 4 // share

    def quarter_spec(array):
        return pl.BlockSpec(
            (LAYERS, array.shape[1] // 4, array.shape[2]),
            lambda i, me: (0, me[0] * GRP_CORE + me[1], 0),
        )

    shapes = [(4, 2 * share, width // 2), (far + 3, share, width), (far, share, width)]
    return pl.pallas_call(
        pick_kernel,
        out_shape=[jax.ShapeDtypeStruct(shape, jnp.bfloat16) for shape in shapes],
        grid_spec=pltpu.PrefetchScalarGridSpec(
            num_scalar_prefetch=1,
            grid=(1,),
            in_specs=[
                pl.BlockSpec((1, 2 * share, project.shape[2]), lambda i, me: (0, me[0], 0)),
                pl.BlockSpec(
                    (1, share, project.shape[2]), lambda i, me: (1, me[0] * GRP_CORE + me[1], 0)
                ),
            ]
            + [quarter_spec(array) for array in (mixer, expand, reduce)]
            + [pl.BlockSpec(small.shape, lambda i, me: (0, 0))],
            out_specs=[pl.BlockSpec(shape, lambda i, me: (0, 0, 0)) for shape in shapes],
        ),
        name="pick_quarters",
    )(me, project, project, mixer, expand, reduce, small)


def pack_kernel(kinds, *refs):
    ins, vector_ref, out_ref = refs[:-2], refs[-2], refs[-1]
    width = out_ref.shape[-1]
    share = ins[0].shape[2]
    begin_at = 0
    for kind, ref in zip(kinds, ins):
        if kind == "columns":
            for column in range(ref.shape[-1] // width):
                lanes = slice(column * width, (column + 1) * width)
                out_ref[0, :, begin_at : begin_at + share, :] = ref[:, 0, :, lanes]
                begin_at += share
        else:
            out_ref[0, :, begin_at : begin_at + ref.shape[2], :] = ref[:, 0]
            begin_at += ref.shape[2]
    out_ref[0, :, begin_at : begin_at + 8, :] = vector_ref[0]


def pack_terms(terms, kinds, width, vectors):
    rows = sum(t.size for t in terms) // (32 * width) + 8
    views = [t.reshape(8, 4, -1, t.shape[1]) for t in terms]
    return pl.pallas_call(
        functools.partial(pack_kernel, kinds),
        out_shape=pltpu.HBM((4, 8, rows, width), jnp.bfloat16),
        grid=(4,),
        in_specs=[pl.BlockSpec((8, 1) + view.shape[2:], lambda q: (0, q, 0, 0)) for view in views]
        + [pl.BlockSpec((1,) + vectors.shape[1:], lambda q: (q, 0, 0, 0))],
        out_specs=pl.BlockSpec((1, 8, rows, width), lambda q: (q, 0, 0, 0)),
        compiler_params=pltpu.CompilerParams(vmem_limit_bytes=32 * 2**20),
        cost_estimate=pl.CostEstimate(
            flops=0, bytes_accessed=128 * rows * width, transcendentals=0
        ),
        name="pack_terms",
    )(*[in_main(view) for view in views], vectors)


def swap_y(values):
    return send(values, lambda y, core, z, x: (1 - y, core, z, x))


def swap_x(values):
    return send(values, lambda y, core, z, x: (y, core, z, 1 - x))


def swap_z(values, bit):
    return send(values, lambda y, core, z, x: (y, core, z ^ bit, x))


def spread_kernel(me, q_ref, kv_ref, vector_ref, out_ref):
    part, half = out_ref.shape[-2:]
    for x_bit in range(SHARD_X):
        for z_bits in range(SHARD_Z):
            shard = (z_bits ^ me[3]) * SHARD_X + (x_bit ^ me[2])
            out_ref[0, x_bit, z_bits, 0] = q_ref[shard, 0]
            out_ref[0, x_bit, z_bits, 1] = kv_ref[shard, 0, :, :half]
            out_ref[0, x_bit, z_bits, 2] = kv_ref[shard, 0, :, half:]
            out_ref[0, x_bit, z_bits, 3] = jnp.zeros((part, half), jnp.bfloat16)
            out_ref[0, x_bit, z_bits, 3, 0:8, :] = vector_ref[0, shard]


def spread_terms(me, query_term, key_value_term, vectors):
    half = query_term.shape[1]
    part = query_term.shape[0] // 16
    shape = (GRP_Y, SHARD_X, SHARD_Z, 4, part, half)

    def rows_spec(columns):
        return pl.BlockSpec((8, 1, part, columns), lambda j, me: (0, j ^ me[0], 0, 0))

    return pl.pallas_call(
        spread_kernel,
        out_shape=jax.ShapeDtypeStruct(shape, jnp.bfloat16),
        grid_spec=pltpu.PrefetchScalarGridSpec(
            num_scalar_prefetch=1,
            grid=(2,),
            in_specs=[
                rows_spec(half),
                rows_spec(2 * half),
                pl.BlockSpec((1,) + vectors.shape[1:], lambda j, me: (j ^ me[0], 0, 0, 0)),
            ],
            out_specs=pl.BlockSpec((1,) + shape[1:], lambda j, me: (j, 0, 0, 0, 0, 0)),
        ),
        name="spread_terms",
    )(
        me,
        query_term.reshape(8, 2, part, half),
        key_value_term.reshape(8, 2, part, 2 * half),
        vectors,
    )


def summed(one, other):
    return (one.astype(jnp.float32) + other.astype(jnp.float32)).astype(jnp.bfloat16)


def scatter_terms(a_part, b_part, b_next):
    a_next = swap_y(a_part[1])
    a_last = swap_x(summed(a_part[0, 1], a_next[1]))
    b_last = swap_y(summed(b_part[1, 0], b_next[1]))
    a_keep = summed(a_part[0, 0], a_next[0])
    b_keep = summed(b_part[0, 0], b_next[0])
    whole = jnp.concatenate([a_keep, b_keep], axis=1)
    come = jnp.concatenate([a_last, b_last], axis=1)
    far = swap_z(summed(whole[2:], come[2:]), 2)
    whole = summed(whole[:2], come[:2])
    near = swap_z(summed(whole[1], far[1]), 1)
    return summed(summed(whole[0], far[0]), near)


def gather_quarters(piece):
    pair = jnp.stack([piece, swap_y(piece)])
    return jnp.stack([pair, swap_core(pair)])


def finish_kernel(me, *refs):
    layers = len(refs) // 2 - 3
    outs = refs[2 * layers :]

    def fill(near_ref, far_ref):
        part, half = near_ref.shape[-2:]
        share, width = part // 2, 2 * half
        for y_bit in range(GRP_Y):
            for core_bit in range(GRP_CORE):
                y = y_bit ^ me[0]
                core = core_bit ^ me[1]
                quarter = y * GRP_CORE + core
                for column in range(3):
                    lanes = pl.ds(pl.multiple_of(column * 2 * half + core * half, 128), half)
                    outs[0][0, y, :, lanes] = near_ref[core_bit, y_bit, column].astype(jnp.float32)
                outs[4][0, quarter] = near_ref[core_bit, y_bit, 3, 0:8, :].astype(jnp.float32)
                pieces = far_ref.at[core_bit, y_bit]
                outs[1][0, quarter] = pieces[:share, :].astype(jnp.float32)
                begin_at = share
                for column in range(outs[2].shape[-1] // width):
                    lanes = slice(column * width, (column + 1) * width)
                    rows = slice(begin_at, begin_at + share)
                    outs[2][0, quarter, :, lanes] = pieces[rows, :].astype(jnp.float32)
                    begin_at += share
                deep = outs[3].shape[2]
                outs[3][0, quarter] = pieces[begin_at : begin_at + deep, :].astype(jnp.float32)
                begin_at += deep
                outs[5][0, quarter] = pieces[begin_at : begin_at + 8, :].astype(jnp.float32)

    for layer in range(layers):
        pl.when(pl.program_id(0) == layer)(
            functools.partial(fill, refs[2 * layer], refs[2 * layer + 1])
        )


def finish_shares(me, shares, hidden_units, deep):
    layers = len(shares)
    part, half = shares[0][0].shape[-2:]
    share, width = part // 2, 2 * half
    shapes = [
        (2, part, 3 * width),
        (4, share, width),
        (4, share, hidden_units),
        (4, deep, width),
        (4, 8, half),
        (4, 8, width),
    ]
    flat = [array for pair in shares for array in pair]
    outs = pl.pallas_call(
        finish_kernel,
        out_shape=[jax.ShapeDtypeStruct((layers,) + shape, jnp.float32) for shape in shapes],
        grid_spec=pltpu.PrefetchScalarGridSpec(
            num_scalar_prefetch=1,
            grid=(layers,),
            in_specs=[whole_block(array.shape) for array in flat],
            out_specs=[
                pl.BlockSpec((1,) + shape, lambda i, me: (i, 0, 0, 0)) for shape in shapes
            ],
        ),
        compiler_params=pltpu.CompilerParams(vmem_limit_bytes=32 * 2**20),
        name="finish_shares",
    )(me, *flat)
    return [out.reshape(layers, -1, out.shape[-1]) for out in outs[:4]] + list(outs[4:])


def row_mean(values):
    return jnp.mean(values, axis=1, keepdims=True)


def column_sum(values):
    return jnp.sum(values, axis=0, keepdims=True)


def standardized(values):
    centered = values - row_mean(values)
    scale = lax.rsqrt(row_mean(centered * centered) + EPSILON)
    return centered * scale, scale


def standard_back(grad, norm, scale, gain):
    weighted = grad * gain
    return (weighted - row_mean(weighted) - norm * row_mean(weighted * norm)) * scale


def join_rows(ref, whole_scr):
    quarters, shards, pieces, share, unused = ref.shape
    for shard in range(shards):
        for quarter in range(quarters):
            for piece in range(pieces):
                begin_at = ((shard * quarters + quarter) * pieces + piece) * share
                whole_scr[begin_at : begin_at + share, :] = ref[quarter, shard, piece]


def piece_specs(pieces, steps):
    quarters, shards, unused, share, width = pieces.shape
    deep = steps
    return [
        pl.BlockSpec((quarters, shards, 1, share, width), lambda j, me: (0, 0, deep + j, 0, 0)),
        pl.BlockSpec((quarters, shards // steps, deep, share, width), lambda j, me: (0, j, 0, 0, 0)),
        pl.BlockSpec((quarters, shards, 1, share, width), lambda j, me: (0, 0, deep + steps, 0, 0)),
    ]


def tail_forward_kernel(
    me,
    own_ref,
    far_ref,
    state_ref,
    expand_ref,
    reduce_ref,
    mixer_ref,
    bias_in_ref,
    vector_ref,
    mix_out,
    norm_one_out,
    scale_one_out,
    low_out,
    active_out,
    slope_out,
    norm_two_out,
    scale_two_out,
    state_out,
    state_low_out,
    wide_scr,
    total_scr,
    one_scr,
    two_scr,
):
    step = pl.program_id(0)
    half = own_ref.shape[1]

    @pl.when(step == 0)
    def begin():
        mix_out[:, pl.ds(pl.multiple_of(me[1] * half, 128), half)] = own_ref[...]
        mix_out[:, pl.ds(pl.multiple_of((1 - me[1]) * half, 128), half)] = far_ref[...]
        join_rows(mixer_ref, one_scr)
        branch = jnp.dot(mix_out[...], one_scr[...], preferred_element_type=jnp.float32)
        norm, scale = standardized(state_ref[...].astype(jnp.float32) + (branch + vector_ref[2:3]))
        norm_one_out[...] = norm
        scale_one_out[...] = jnp.broadcast_to(scale, scale_one_out.shape)
        wide = norm * vector_ref[10:11] + vector_ref[3:4]
        wide_scr[...] = wide
        low_out[...] = wide.astype(jnp.bfloat16)
        total_scr[...] = jnp.zeros_like(total_scr)

    join_rows(expand_ref, one_scr)
    join_rows(reduce_ref, two_scr)
    before = (
        jnp.dot(low_out[...], one_scr[...], preferred_element_type=jnp.float32)
        + bias_in_ref[...]
    )
    normal = 0.5 * (1.0 + lax.erf(before * 0.7071067811865476))
    density = jnp.exp(before * before * -0.5) * 0.3989422804014327
    active = (before * normal).astype(jnp.bfloat16)
    active_out[...] = active
    slope_out[...] = normal + before * density
    total_scr[...] += jnp.dot(active, two_scr[...], preferred_element_type=jnp.float32)

    @pl.when(step == pl.num_programs(0) - 1)
    def end():
        norm, scale = standardized(wide_scr[...] + (total_scr[...] + vector_ref[8:9]))
        norm_two_out[...] = norm
        scale_two_out[...] = jnp.broadcast_to(scale, scale_two_out.shape)
        state = norm * vector_ref[11:12] + vector_ref[9:10]
        state_out[...] = state
        state_low_out[...] = state.astype(jnp.bfloat16)


def tail_forward(me, own_mix, far_mix, state, pieces, bias_in, vectors):
    rows, width = state.shape
    hidden_units = bias_in.shape[1]
    steps = hidden_units // width
    whole = whole_block((rows, width))
    halves = whole_block((rows, width // 2))
    scale = whole_block((rows, 128))
    tile = pl.BlockSpec((rows, width), lambda j, me: (0, j))

    def shaped(columns, kind):
        return jax.ShapeDtypeStruct((rows, columns), kind)

    return pl.pallas_call(
        tail_forward_kernel,
        out_shape=[
            shaped(width, jnp.bfloat16),
            shaped(width, jnp.float32),
            shaped(128, jnp.float32),
            shaped(width, jnp.bfloat16),
            shaped(hidden_units, jnp.bfloat16),
            shaped(hidden_units, jnp.float32),
            shaped(width, jnp.float32),
            shaped(128, jnp.float32),
            shaped(width, jnp.float32),
            shaped(width, jnp.bfloat16),
        ],
        grid_spec=pltpu.PrefetchScalarGridSpec(
            num_scalar_prefetch=1,
            grid=(steps,),
            in_specs=[
                halves,
                halves,
                whole,
            ]
            + piece_specs(pieces, steps)
            + [pl.BlockSpec((1, width), lambda j, me: (0, j)), whole_block(vectors.shape)],
            out_specs=[whole, whole, scale, whole, tile, tile, whole, scale, whole, whole],
            scratch_shapes=[
                pltpu.VMEM((rows, width), jnp.float32),
                pltpu.VMEM((rows, width), jnp.float32),
                pltpu.VMEM((width, width), jnp.bfloat16),
                pltpu.VMEM((width, width), jnp.bfloat16),
            ],
        ),
        compiler_params=pltpu.CompilerParams(vmem_limit_bytes=44 * 2**20),
        cost_estimate=pl.CostEstimate(
            flops=2 * rows * width * (width + 2 * hidden_units),
            bytes_accessed=32 * 2**20,
            transcendentals=2 * rows * hidden_units,
        ),
        name="tail_forward",
    )(me, own_mix, far_mix, state, *[in_main(pieces)] * 3, bias_in, vectors)


def tail_backward_kernel(
    me,
    grad_ref,
    norm_two_ref,
    scale_two_ref,
    norm_one_ref,
    scale_one_ref,
    low_ref,
    mix_ref,
    slope_ref,
    active_ref,
    expand_ref,
    reduce_ref,
    mixer_ref,
    vector_ref,
    sum_out,
    own_out,
    far_out,
    mixer_out,
    expand_out,
    reduce_out,
    bias_in_out,
    vector_out,
    wide_scr,
    feed_scr,
    total_scr,
    one_scr,
    two_scr,
):
    step = pl.program_id(0)
    half = own_out.shape[1]

    @pl.when(step == 0)
    def begin():
        grad = grad_ref[...]
        norm = norm_two_ref[...]
        wide = standard_back(grad, norm, scale_two_ref[:, 0:1], vector_ref[11:12])
        wide_scr[...] = wide
        feed = wide.astype(jnp.bfloat16)
        feed_scr[...] = feed
        vector_out[...] = jnp.zeros_like(vector_out)
        vector_out[3:4] = column_sum(feed.astype(jnp.float32))
        vector_out[4:5] = column_sum(grad * norm)
        vector_out[5:6] = column_sum(grad)
        total_scr[...] = jnp.zeros_like(total_scr)

    join_rows(expand_ref, one_scr)
    join_rows(reduce_ref, two_scr)
    feed = feed_scr[...]
    active_grad = turned_dot(feed, two_scr[...])
    before = (active_grad * slope_ref[...]).astype(jnp.bfloat16)
    bias_in_out[...] = column_sum(before.astype(jnp.float32))
    reduce_out[...] = across_dot(active_ref[...], feed).astype(jnp.bfloat16)
    expand_out[...] = across_dot(low_ref[...], before).astype(jnp.bfloat16)
    total_scr[...] += turned_dot(before, one_scr[...])

    @pl.when(step == pl.num_programs(0) - 1)
    def end():
        grad = wide_scr[...] + total_scr[...]
        norm = norm_one_ref[...]
        wide = standard_back(grad, norm, scale_one_ref[:, 0:1], vector_ref[10:11])
        sum_out[...] = wide
        branch = wide.astype(jnp.bfloat16)
        vector_out[0:1] = column_sum(branch.astype(jnp.float32))
        vector_out[1:2] = column_sum(grad * norm)
        vector_out[2:3] = column_sum(grad)
        mixer_out[...] = across_dot(mix_ref[...], branch).astype(jnp.bfloat16)
        join_rows(mixer_ref, one_scr)
        mixed = turned_dot(branch, one_scr[...]).astype(jnp.bfloat16)
        total_scr[...] = mixed.astype(jnp.float32)
        own = total_scr[:, pl.ds(pl.multiple_of(me[1] * half, 128), half)]
        far = total_scr[:, pl.ds(pl.multiple_of((1 - me[1]) * half, 128), half)]
        own_out[...] = own.astype(jnp.bfloat16)
        far_out[...] = far.astype(jnp.bfloat16)


def tail_backward(me, grad, kept, pieces, vectors):
    norm_two, scale_two, norm_one, scale_one, low, mixed, slope, active = kept
    rows, width = grad.shape
    hidden_units = active.shape[1]
    steps = hidden_units // width
    whole = whole_block((rows, width))
    halves = whole_block((rows, width // 2))
    scale = whole_block((rows, 128))
    square = whole_block((width, width))
    tile = pl.BlockSpec((rows, width), lambda j, me: (0, j))
    across = pl.BlockSpec((width, width), lambda j, me: (0, j))
    down = pl.BlockSpec((width, width), lambda j, me: (j, 0))
    line = pl.BlockSpec((1, width), lambda j, me: (0, j))

    def shaped(rows, columns, kind):
        return jax.ShapeDtypeStruct((rows, columns), kind)

    return pl.pallas_call(
        tail_backward_kernel,
        out_shape=[
            shaped(rows, width, jnp.float32),
            shaped(rows, width // 2, jnp.bfloat16),
            shaped(rows, width // 2, jnp.bfloat16),
            shaped(width, width, jnp.bfloat16),
            shaped(width, hidden_units, jnp.bfloat16),
            shaped(hidden_units, width, jnp.bfloat16),
            shaped(1, hidden_units, jnp.float32),
            shaped(8, width, jnp.float32),
        ],
        grid_spec=pltpu.PrefetchScalarGridSpec(
            num_scalar_prefetch=1,
            grid=(steps,),
            in_specs=[whole, whole, scale, whole, scale, whole, whole, tile, tile]
            + piece_specs(pieces, steps)
            + [whole_block(vectors.shape)],
            out_specs=[whole, halves, halves, square, across, down, line, whole_block((8, width))],
            scratch_shapes=[
                pltpu.VMEM((rows, width), jnp.float32),
                pltpu.VMEM((rows, width), jnp.bfloat16),
                pltpu.VMEM((rows, width), jnp.float32),
                pltpu.VMEM((width, width), jnp.bfloat16),
                pltpu.VMEM((width, width), jnp.bfloat16),
            ],
        ),
        compiler_params=pltpu.CompilerParams(vmem_limit_bytes=48 * 2**20),
        cost_estimate=pl.CostEstimate(
            flops=2 * rows * width * (2 * width + 4 * hidden_units),
            bytes_accessed=40 * 2**20,
            transcendentals=0,
        ),
        name="tail_backward",
    )(
        me,
        grad,
        norm_two,
        scale_two,
        norm_one,
        scale_one,
        low,
        mixed,
        slope,
        active,
        *[in_main(pieces)] * 3,
        vectors,
    )


def gather_all(local):
    places, share, width = local.shape
    gathered = lax.all_gather(local.reshape(-1, width), BOTH, axis=0, tiled=False)
    return gathered.reshape(4, 8, places, share, width)


def join_kernel(me, a_ref, b_ref, project_ref, small_ref):
    half = a_ref.shape[-1]
    for y_bit in range(GRP_Y):
        y = y_bit ^ me[0]
        for x_bit in range(SHARD_X):
            for z_bits in range(SHARD_Z):
                shard = (z_bits ^ me[3]) * SHARD_X + (x_bit ^ me[2])
                project_ref[shard, y, :, :half] = a_ref[y_bit, x_bit, z_bits, 0]
                project_ref[shard, y, :, half : 2 * half] = a_ref[y_bit, x_bit, z_bits, 1]
                project_ref[shard, y, :, 2 * half :] = b_ref[x_bit, y_bit, z_bits, 0]
                if y_bit == 0:
                    small_ref[shard, :, :half] = b_ref[x_bit, y_bit, z_bits, 1, 0:8, :]
                    small_ref[shard, :, half:] = b_ref[x_bit, y_bit, z_bits, 1, 8:16, :]


def gather_first(me, local, rows):
    part, half = local.shape[1:]
    pair = jnp.stack([local, swap_z(local, 1)])
    pair, rows = lax.optimization_barrier((pair, rows))
    window = window_of(rows)
    four = jnp.concatenate([pair, swap_z(pair, 2)])
    a_part, b_part = four[:, :2], four[:, 2:]
    a_two = jnp.stack([a_part, swap_x(a_part)])
    b_two = jnp.stack([b_part, swap_y(b_part)])
    a_four = jnp.stack([a_two, swap_y(a_two)])
    b_four = jnp.stack([b_two, swap_x(b_two)])
    project, small = pl.pallas_call(
        join_kernel,
        out_shape=[
            jax.ShapeDtypeStruct((8, 2, part, 3 * half), local.dtype),
            jax.ShapeDtypeStruct((8, 8, 2 * half), local.dtype),
        ],
        grid_spec=pltpu.PrefetchScalarGridSpec(
            num_scalar_prefetch=1,
            grid=(1,),
            in_specs=[whole_block(a_four.shape)] * 2,
            out_specs=[whole_block((8, 2, part, 3 * half)), whole_block((8, 8, 2 * half))],
        ),
        compiler_params=pltpu.CompilerParams(vmem_limit_bytes=24 * 2**20),
        name="join_projection",
    )(me, a_four, b_four)
    return project.reshape(-1, 3 * half), small, four, rows, window


def on_device_turned(
    tokens,
    cotangent,
    seq_lengths,
    seq_order,
    w_project,
    w_mixer,
    w_expand,
    w_reduce,
    biases,
    norm_gains,
):
    row_count, width = tokens.shape
    shard_index = lax.axis_index("shard")
    quarter = lax.axis_index("grp")
    z, x = shard_index // SHARD_X, shard_index % SHARD_X
    y, core = quarter // GRP_CORE, quarter % GRP_CORE
    me = jnp.stack([y, core, x, z]).astype(jnp.int32)
    hidden_units = w_expand.shape[2]
    group_slots = row_count * 8
    seq_count = seq_lengths.shape[1]
    seq_ends = group_ends(seq_lengths, seq_order, y * GRP_CORE + x)
    block_index = z * GRP_CORE + jnp.stack([core, 1 - core])
    slot_index = block_index[:, None] * row_count + jnp.arange(row_count, dtype=jnp.int32)[None, :]
    slot_index = slot_index.reshape(-1)
    before_slot = seq_ends[None, :] <= slot_index[:, None]
    own_segment = jnp.sum(before_slot[:row_count].astype(jnp.int32), axis=1, dtype=jnp.int32)
    starts = jnp.max(jnp.where(before_slot, seq_ends[None, :], 0), axis=1)
    stops = jnp.min(jnp.where(before_slot, group_slots, seq_ends[None, :]), axis=1)
    window_begin = (z - 1) * GRP_CORE * row_count
    low = starts - window_begin
    high = stops - window_begin
    low_line = jnp.broadcast_to(low[None, :], (8, 2 * row_count))
    high_line = jnp.broadcast_to(high[None, :], (8, 2 * row_count))
    places = [(1, 0, 2)[t // 2] + ((t % 2) ^ core) * 3 for t in range(6)]
    bounds = jnp.stack(
        [
            low[0] // KEY_ROWS,
            (high[row_count - 1] + KEY_ROWS - 1) // KEY_ROWS,
            low[row_count] // KEY_ROWS,
            (high[2 * row_count - 1] + KEY_ROWS - 1) // KEY_ROWS,
        ]
        + places
    ).astype(jnp.int32)
    valid_rows = (own_segment < seq_count).astype(jnp.float32)[:, None]

    small = jnp.concatenate(
        [jnp.concatenate([biases[i], norm_gains[i]]) for i in range(LAYERS)]
    ).reshape(-1, width)
    share = w_project.shape[1] // 4
    deep = w_reduce.shape[1] // 4
    bias_count = biases.shape[1]
    small_rows = small.shape[0]
    small = jnp.concatenate([small, jnp.zeros((8 - small_rows, width), small.dtype)])
    near_first, far_first, far_last = pick_quarters(
        me, w_project, w_mixer, w_expand, w_reduce, small
    )
    state_low = turn_rows(tokens)
    state_grad = turn_rows(cotangent)
    project_first, small_all, arrived, state_low, first_window = gather_first(
        me, near_first, state_low
    )
    far_first, arrived = lax.optimization_barrier((far_first, arrived))
    far_kinds = ("columns", "columns", "rows")
    far_shapes = [(share, width), (share, hidden_units), (deep, width)]
    far_count = far_last.shape[0]
    pieces = gather_all(far_first)
    project_last = unpack_weights_of(pieces, far_count, 3, ("columns",), [(share, 3 * width)])[0]
    project_last = jnp.concatenate(
        [half_of(project_last[:, i * width : (i + 1) * width], 1, core) for i in range(3)], axis=1
    )
    tail_pieces = [pieces, gather_all(far_last)]
    small_all = small_all[:, :small_rows].reshape(8, LAYERS, -1)
    weights = []
    vector_rows = []
    for layer_index, project in enumerate([project_first, project_last]):
        bias_vec = small_all[:, layer_index, :bias_count].reshape(-1)
        gain_vec = small_all[:, layer_index, bias_count:].reshape(-1)
        weights.append(
            unpack_weights((project, None, None, None, bias_vec, gain_vec), width, hidden_units)
        )
        vector_rows.append(
            jnp.concatenate([bias_vec, gain_vec]).astype(jnp.float32).reshape(-1, width)
        )

    hidden_state = state_low.astype(jnp.float32)
    kept_list = []
    for layer_index in range(LAYERS):
        project, mixing, expand, shrink, bias_list, gain_one, gain_two = weights[layer_index]
        bias_q, bias_v, bias_mix, shift_one, bias_in, bias_out, shift_two = bias_list
        state_window = first_window if layer_index == 0 else window_of(state_low)
        half = width // 2
        far_begin = 3 * row_count
        queries = [
            (
                jnp.dot(
                    state_window[begin_at : begin_at + row_count],
                    project[:, :half],
                    preferred_element_type=jnp.float32,
                )
                + half_of(bias_q, 0, core)
            ).astype(jnp.bfloat16)
            for begin_at in (0, far_begin)
        ]
        key_value = (
            jnp.dot(state_window, project[:, half:], preferred_element_type=jnp.float32)
            + jnp.concatenate([jnp.zeros((half,), jnp.float32), half_of(bias_v, 0, core)])
        ).astype(jnp.bfloat16)
        own_mix, far_mix, own_wide, far_wide, lse = flash_forward(bounds, queries, key_value, low_line, high_line)
        far_mix = swap_core(far_mix)
        tail_vectors = vector_rows[layer_index]
        (
            mixed_low,
            norm_one,
            scale_one,
            normed_low,
            active_low,
            slope,
            norm_two,
            scale_two,
            hidden_state,
            next_low,
        ) = tail_forward(
            me, own_mix, far_mix, hidden_state, tail_pieces[layer_index], bias_in[None], tail_vectors
        )
        kept_list.append(
            (
                state_low,
                state_window,
                queries,
                key_value,
                (own_wide, far_wide),
                lse,
                (norm_two, scale_two, norm_one, scale_one, normed_low, mixed_low, slope, active_low),
                tail_vectors,
            )
        )
        state_low = next_low
    activations = turn_rows((hidden_state * valid_rows).astype(jnp.bfloat16))
    state_grad = state_grad.astype(jnp.float32) * valid_rows
    results = [None] * LAYERS
    spreads = [None] * LAYERS
    for layer_index in reversed(range(LAYERS)):
        layer_low, state_window, queries, key_value, wides, lse, kept, tail_vectors = kept_list[
            layer_index
        ]
        project, mixing, expand, shrink, *unused = weights[layer_index]
        (
            sum_one_grad,
            own_mix_grad,
            far_mix_grad,
            mixing_grad,
            expand_grad,
            shrink_grad,
            bias_in_grad,
            vector_grads,
        ) = tail_backward(me, state_grad, kept, tail_pieces[layer_index], tail_vectors)
        bias_mix_grad, gain_one_grad, shift_one_grad, bias_out_grad, gain_two_grad, shift_two_grad = [
            vector_grads[i] for i in range(6)
        ]
        mixed_grads = (own_mix_grad, swap_core(far_mix_grad))
        own_grad, far_grad, key_value_grad = flash_backward(
            bounds, queries, key_value, mixed_grads, wides, lse, low_line, high_line
        )
        if layer_index == 0:
            key_value_grad, started = lax.optimization_barrier((key_value_grad, started))
        query_term = jnp.einsum(
            "td,te->de", layer_low, own_grad, preferred_element_type=jnp.float32
        ) + jnp.einsum(
            "td,te->de",
            state_window[far_begin : far_begin + row_count],
            far_grad,
            preferred_element_type=jnp.float32,
        )
        key_value_term = jnp.einsum(
            "td,te->de", state_window, key_value_grad, preferred_element_type=jnp.float32
        )
        bias_q_grad = jnp.sum(own_grad, axis=0, dtype=jnp.float32) + jnp.sum(
            far_grad, axis=0, dtype=jnp.float32
        )
        bias_v_grad = jnp.sum(key_value_grad[:, half:], axis=0, dtype=jnp.float32)
        window_grad = jnp.einsum(
            "te,de->td", key_value_grad, project[:, half:], preferred_element_type=jnp.float32
        )
        own_part = jnp.einsum(
            "te,de->td", own_grad, project[:, :half], preferred_element_type=jnp.float32
        )
        far_part = jnp.einsum(
            "te,de->td", far_grad, project[:, :half], preferred_element_type=jnp.float32
        )
        near_terms = jnp.concatenate(
            [window_grad[:row_count] + own_part, window_grad[row_count:far_begin]]
        )
        far_terms = jnp.concatenate(
            [
                window_grad[far_begin : far_begin + row_count] + far_part,
                window_grad[far_begin + row_count :],
            ]
        )
        state_grad = sum_one_grad + window_back(near_terms, far_terms, row_count)
        zeros_two = jnp.zeros((2 * width,), jnp.float32)
        vectors = jnp.concatenate(
            [
                zeros_two,
                bias_mix_grad,
                shift_one_grad,
                bias_in_grad[0],
                bias_out_grad,
                shift_two_grad,
            ]
        ).reshape(8, -1)
        gains = jnp.concatenate([gain_one_grad, gain_two_grad]).reshape(8, -1)
        vectors = jnp.concatenate([vectors, gains], axis=1).astype(jnp.bfloat16)
        vectors = vectors.reshape(8, 4, 1, -1).transpose(1, 0, 2, 3)
        vectors = jnp.pad(vectors, ((0, 0), (0, 0), (0, 7), (0, width - vectors.shape[3])))
        terms = (mixing_grad, expand_grad, shrink_grad)
        pieces = pack_terms(terms, far_kinds, width, vectors)
        fed = lax.psum_scatter(
            pieces.reshape(32, -1, width), BOTH, scatter_dimension=0, tiled=True
        )[0]
        lines = jnp.zeros((8 * bias_count,), jnp.float32)
        lines = lax.dynamic_update_slice(lines, bias_q_grad, (core * half,))
        lines = lax.dynamic_update_slice(lines, bias_v_grad, (width + core * half,))
        lines = lines.reshape(8, 2, -1).transpose(1, 0, 2).astype(jnp.bfloat16)
        lines = jnp.pad(lines, ((0, 0), (0, 0), (0, width - lines.shape[2])))
        lines = jnp.pad(lines.reshape(2, 8, 2, half), ((0, 0), (0, 0), (0, 6), (0, 0)))
        query_term = query_term.astype(jnp.bfloat16)
        key_value_term = key_value_term.astype(jnp.bfloat16)
        if layer_index > 0:
            state_grad, query_term, key_value_term, activations = lax.optimization_barrier(
                (state_grad, query_term, key_value_term, activations)
            )
        spreads[layer_index] = spread_terms(me, query_term, key_value_term, lines)
        if layer_index > 0:
            started = swap_x(spreads[layer_index][:, 1])
        results[layer_index] = gather_quarters(fed)
    attended = gather_quarters(scatter_terms(*spreads, started))
    results = [
        (attended[:, :, 4 * layer_index : 4 * (layer_index + 1)], results[layer_index])
        for layer_index in range(LAYERS)
    ]
    outs = finish_shares(me, results, hidden_units, deep)
    quarter_len = (bias_count + norm_gains.shape[1]) // 4
    vectors = outs[5][:, :, 0, :quarter_len].reshape(LAYERS, -1)
    lines = outs[4][:, :, :2].reshape(LAYERS, GRP_Y, GRP_CORE, width)[..., : bias_count // 2]
    lines = jnp.sum(lines, axis=2).reshape(LAYERS, bias_count)
    input_grad = turn_rows(state_grad.astype(jnp.bfloat16)).astype(jnp.float32)
    return (
        activations,
        input_grad,
        outs[0],
        outs[1],
        outs[2],
        outs[3],
        vectors[:, :bias_count] + lines,
        vectors[:, bias_count:],
    )


def solution(mesh):
    in_specs = (
        P(("grp", "shard"), None),
        P(("grp", "shard"), None),
        P(),
        P(),
        P(None, "shard", None),
        P(None, "shard", None),
        P(None, "shard", None),
        P(None, "shard", None),
        P(None, "shard"),
        P(None, "shard"),
    )
    out_specs = (
        P(("grp", "shard"), None),
        P(("grp", "shard"), None),
        P(None, "shard", None),
        P(None, "shard", None),
        P(None, "shard", None),
        P(None, "shard", None),
        P(None, "shard"),
        P(None, "shard"),
    )
    body = on_device_turned if mesh.shape["shard"] == 8 and mesh.shape["grp"] == 4 else on_device
    return jax.shard_map(
        body, mesh=mesh, in_specs=in_specs, out_specs=out_specs, check_vma=False
    )
```
